32 devices in a mesh: dp: 16 (over z, x, core), vol: 2 (over y).
Axes of the slice: x: 2, y: 2, z: 4, core: 2. Of those that a mesh axis runs over, the one named last changes fastest.
Arguments:
- images: float32 [32, 128, 128], P(('dp', 'vol')), may hold values from -6 to 6
- contrast: bfloat16 [32, 128, 128], P(('dp', 'vol')), may hold values from -1 to 1
- volume: bfloat16 [256, 256, 256], P('vol'), may hold values from -6 to 6
- line_index: int32 [32, 4, 128], P('dp'), may hold values from 0 to 65278, as said below
- patch_weight: bfloat16 [64, 1024], replicated, may hold values from -0.75 to 0.75
- position: bfloat16 [256, 1024], replicated, may hold values from -3 to 3
- norm_gain: float32 [1024], replicated, may hold values from 0.1 to 1.9
- project_in: bfloat16 [1024, 1536], P('dp'), may hold values from -0.1875 to 0.1875
- project_out: bfloat16 [1024, 512], P('dp'), may hold values from -0.25 to 0.25
- head_weight: float32 [1024, 4], replicated, may hold values from -1.8 to 1.8
Outputs:
- errors: float32 [32, 4], P(('dp', 'vol'))
- in_gradient: float32 [1024, 1536], P('dp')
- out_gradient: float32 [1024, 512], P('dp')
- head_gradient: float32 [1024, 4], replicated
The draws below stay inside these ranges and needn't reach their ends.
Inputs may be any that keep to these rules, and one draw needn't show every extreme that they name: line_index[i, k, r] = z * 256 + y names the plane z and row y of the volume that row r of hypothesis k of image i samples; z and y lie within 0 and 254.
All inputs are finite; a program needn't handle non-finite values.
Results may differ from the reference program's by a relative error of at most 0.038.
Values may be sent and summed in bfloat16 or wider, within the bound.
A program may use at most 64 MiB of HBM per device.

```python
import jax
import jax.numpy as jnp
from jax import lax

D = 1024
HEADS = 8
HEAD_DIM = 64
HD = 512
PIX = 128
PATCH = 8
PATCHES = 256
VOX = 256
K = 4
IMAGES = 32


def draw_line_index(key, part):
    first, second = jax.random.split(jax.random.fold_in(key, 7))
    tilt = jax.random.randint(first, (IMAGES, K), -14, 17)
    turn = jax.random.randint(second, (IMAGES, K), 0, 17)
    tilt = tilt.at[0, 0].set(16)
    turn = turn.at[0, 0].set(16)
    offset = 2 * (jnp.arange(PIX, dtype=jnp.int32) - PIX // 2)
    plane = VOX // 2 + offset[None, None, :] * tilt[:, :, None] // 16
    row = VOX // 2 + offset[None, None, :] * turn[:, :, None] // 16
    return (plane * VOX + row).astype(jnp.int32)


def steps_of(rng, shape, cuts, smallest, top_value):
    def one(dim, blocks):
        heights = jax.random.uniform(jax.random.fold_in(jax.random.fold_in(rng, 6), dim), (blocks,), jnp.float32, smallest / len(cuts), top_value / len(cuts))
        return jnp.repeat(jnp.exp(heights), shape[dim] // blocks).reshape((-1,) + (1,) * (len(shape) - dim - 1))

    gain = one(*cuts[0])
    for cut in cuts[1:]:
        gain = gain * one(*cut)
    return gain


def centred(rng, shape, scale, most, cuts=(), kind=jnp.bfloat16):
    entries = jax.random.normal(rng, shape, jnp.float32) * scale
    if len(cuts) > 0:
        entries = steps_of(rng, shape, cuts, -0.22, 0.18) * entries
    return jnp.clip(entries, min=-most, max=most).astype(kind)


def setup_inputs(seed: int = 0) -> dict:
    seeds = jax.random.split(jax.random.key(seed), 11)
    images = centred(seeds[0], (IMAGES, PIX, PIX), 1.0, 6.0, ((0, 32),), jnp.float32)
    contrast = jnp.clip(jax.random.uniform(seeds[1], (IMAGES, PIX, PIX), jnp.float32, -1.0, 1.0) * steps_of(seeds[1], (IMAGES, PIX, PIX), ((0, 32),), -0.4, 0.0), -1.0, 1.0).astype(jnp.bfloat16)
    volume = centred(seeds[2], (VOX, VOX, VOX), 1.0, 6.0, ((0, 2),))
    line_index = draw_line_index(jax.random.fold_in(seeds[10], 71), 0)
    patch_weight = centred(seeds[4], (PATCH * PATCH, D), (PATCH * PATCH) ** -0.5, 0.75)
    position = centred(seeds[5], (PATCHES, D), 0.5, 3.0)
    norm_gain = jnp.clip(1.0 + 0.18 * jax.random.normal(seeds[6], (D,), jnp.float32), 0.1, 1.9)
    project_in = centred(seeds[7], (D, 3 * HD), D ** -0.5, 0.1875, ((0, 16),))
    project_out = centred(seeds[8], (D, HD), HD ** -0.5, 0.25, ((0, 16),))
    head_weight = centred(seeds[9], (D, K), 0.3, 1.8, (), jnp.float32)
    return {"images": images, "contrast": contrast, "volume": volume, "line_index": line_index, "patch_weight": patch_weight, "position": position, "norm_gain": norm_gain, "project_in": project_in, "project_out": project_out, "head_weight": head_weight}


EPSILON = 1e-05

def embed_images(images, patch_weight, position):
    count = images.shape[0]
    grid = PIX // PATCH
    pieces = images.reshape(count, grid, PATCH, grid, PATCH).transpose(0, 1, 3, 2, 4)
    pieces = pieces.reshape(count * grid * grid, PATCH * PATCH).astype(jnp.bfloat16)
    mixed = jnp.dot(pieces, patch_weight, preferred_element_type=jnp.float32)
    mixed = mixed.reshape(count, grid * grid, -1) + position.astype(jnp.float32)[None]
    return mixed.reshape(count * grid * grid, -1).astype(jnp.bfloat16)

def normalize(embedded, norm_gain):
    values = embedded.astype(jnp.float32)
    center = values - lax.optimization_barrier(jnp.mean(values, axis=1, keepdims=True))
    scale = lax.rsqrt(lax.optimization_barrier(jnp.mean(center * center, axis=1, keepdims=True)) + EPSILON)
    return (center * scale * norm_gain[None, :]).astype(jnp.bfloat16)

def attend(triple):
    count = triple.shape[0] // PATCHES
    parts = triple.reshape(count, PATCHES, 3, HEADS, HEAD_DIM).astype(jnp.float32)
    query = parts[:, :, 0]
    keys = parts[:, :, 1]
    values = parts[:, :, 2]
    scores = jnp.einsum('bqhd,bkhd->bhqk', query, keys) * HEAD_DIM ** (-0.5)
    raised = jnp.exp(scores)
    weights = (raised / lax.optimization_barrier(jnp.sum(raised, axis=-1, keepdims=True))).astype(jnp.bfloat16)
    mixed = jnp.einsum('bhqk,bkhd->bqhd', weights.astype(jnp.float32), values)
    return mixed.reshape(count * PATCHES, HEADS * HEAD_DIM).astype(jnp.bfloat16)

def spectrum_of(images):
    transform = jnp.fft.fftshift(jnp.fft.fft2(images), axes=(1, 2))
    return (jnp.real(transform) - jnp.imag(transform)) / PIX

def reference(images, contrast, volume, line_index, patch_weight, position, norm_gain, project_in, project_out, head_weight):
    table = volume.reshape(VOX * VOX, VOX)
    block = 16
    blocks = IMAGES // block
    image_blocks = images.reshape(blocks, block, PIX, PIX)
    contrast_blocks = contrast.reshape(blocks, block, PIX, PIX)
    line_blocks = line_index.reshape(blocks, block, K, PIX)

    def step(carry, inputs):
        image_part, contrast_part, line_part = inputs
        picked = jnp.take(table, line_part.reshape(-1), axis=0)[:, ::2]
        slices = picked.astype(jnp.float32).reshape(block, K, PIX, PIX)
        spectrum = spectrum_of(image_part)
        misfit = contrast_part.astype(jnp.float32)[:, None] * slices - spectrum[:, None]
        errors = lax.optimization_barrier(jnp.mean(misfit * misfit, axis=(2, 3)))
        embedded = embed_images(image_part, patch_weight, position)
        normed = normalize(embedded, norm_gain)
        triple = jnp.dot(normed, project_in, preferred_element_type=jnp.float32).astype(jnp.bfloat16)
        attended = attend(triple)
        branch = jnp.dot(attended, project_out.T, preferred_element_type=jnp.float32)
        layer_out = embedded.astype(jnp.float32) + branch
        pooled = lax.optimization_barrier(jnp.mean(layer_out.reshape(block, PATCHES, D), axis=1))
        logits = jnp.dot(pooled, head_weight, precision=lax.Precision.HIGHEST)
        raised = jnp.exp(logits)
        chances = raised / lax.optimization_barrier(jnp.sum(raised, axis=1, keepdims=True))
        expected = lax.optimization_barrier(jnp.sum(chances * errors, axis=1, keepdims=True))
        logit_slope = chances * (errors - expected)
        head_term = jnp.dot(pooled.T, logit_slope, precision=lax.Precision.HIGHEST)
        pooled_slope = jnp.dot(logit_slope, head_weight.T, precision=lax.Precision.HIGHEST) / PATCHES
        layer_slope = jnp.broadcast_to(pooled_slope[:, None, :], (block, PATCHES, D)).reshape(block * PATCHES, D).astype(jnp.bfloat16)
        out_term = jnp.dot(layer_slope.T, attended, preferred_element_type=jnp.float32)
        attended_slope = jnp.dot(layer_slope, project_out, preferred_element_type=jnp.float32).astype(jnp.bfloat16)
        triple_slope = jax.vjp(attend, triple)[1](attended_slope)[0]
        in_term = jnp.dot(normed.T, triple_slope, preferred_element_type=jnp.float32)
        in_sum, out_sum, head_sum = carry
        return ((in_sum + in_term, out_sum + out_term, head_sum + head_term), errors)
    start = (jnp.zeros((D, 3 * HD), jnp.float32), jnp.zeros((D, HD), jnp.float32), jnp.zeros((D, K), jnp.float32))
    totals, errors = lax.scan(step, start, (image_blocks, contrast_blocks, line_blocks))
    return (errors.reshape(IMAGES, K), totals[0], totals[1], totals[2])
```

```python
import functools
import math

import jax
import jax.numpy as jnp
import numpy as np
from jax import lax
from jax.experimental import pallas as pl
from jax.experimental.pallas import tpu as pltpu
from jax.sharding import PartitionSpec as P

HEADS = 8
HEAD_DIM = 64
PIX = 128
PATCH = 8
PATCHES = 256
K = 4
EPSILON = 1e-05
F32 = jnp.float32
BF16 = jnp.bfloat16
HIGHEST = lax.Precision.HIGHEST
FIRST = (((0,), (0,)), ((), ()))
LAST = (((1,), (1,)), ((), ()))
MESH = pl.DeviceIdType.MESH


def step(
    dps,
    vols,
    spots,
    index_hbm,
    volume,
    image_hbm,
    contrast_hbm,
    patch_weight_hbm,
    position_hbm,
    gain_hbm,
    project_in_hbm,
    project_out_hbm,
    head_hbm,
    waves_hbm,
    sel_hbm,
    places_hbm,
    errors_out,
    grad_recv,
    value_out,
    head_out,
    index,
    image,
    contrast,
    patch_weight,
    position,
    gain,
    project_in,
    project_out,
    head_weight,
    waves,
    sel,
    places,
    slab_buf,
    picked,
    patches,
    pieces,
    head_wide,
    lines,
    patch_buf,
    weight,
    basis,
    basis_t,
    gram,
    square,
    tokens,
    tokens_t,
    scales,
    attention,
    triple,
    column,
    mean_att,
    small_send,
    small_recv,
    pulled_buf,
    slope_buf,
    terms_buf,
    total_buf,
    factor_send,
    factor_recv,
    factor_sum,
    side_send,
    side_recv,
    grad_send,
    tile_send,
    tile_recv,
    head_send,
    in_sems,
    line_sems,
    patch_sems,
    weight_sems,
    relay_sems,
    small_sems,
    core_sems,
    grad_sems,
    tile_sems,
    head_sems,
):
    dp = lax.axis_index("dp")
    vol = lax.axis_index("vol")
    core = dp % 2
    chip = dp // 2
    chips = dps // 2
    count = chips * vols
    me = chip * vols + vol
    pair = vol % 2
    head = (chip % 4) * 2 + pair
    rows = weight.shape[1]
    width = gain.shape[1]
    slab = volume.shape[0]

    def copy(src, dst, send_sem, recv_sem, to_dp, to_vol):
        return pltpu.make_async_remote_copy(
            src_ref=src,
            dst_ref=dst,
            send_sem=send_sem,
            recv_sem=recv_sem,
            device_id=(to_dp, to_vol),
            device_id_type=MESH,
        )

    def each(first, last, body):
        def run(k, c):
            body(k)
            return c

        lax.fori_loop(first, last, run, 0)

    other = dp + 1 - 2 * core
    barrier = pltpu.get_barrier_semaphore()

    def greet(k):
        e = (me + k) % count
        pl.semaphore_signal(
            barrier, inc=1, device_id=(e // vols * 2 + core, e % vols), device_id_type=MESH
        )

    each(1, count, greet)
    pl.semaphore_signal(barrier, inc=1, device_id=(other, vol), device_id_type=MESH)

    loads = {}
    for name, src, dst in (
        ("image", image_hbm, image),
        ("places", places_hbm, places),
        ("project_in", project_in_hbm, project_in),
        ("project_out", project_out_hbm, project_out),
        ("index", index_hbm, index),
        ("sel", sel_hbm, sel),
        ("waves", waves_hbm, waves),
        ("patch_weight", patch_weight_hbm, patch_weight),
        ("position", position_hbm, position),
        ("gain", gain_hbm, gain),
        ("head", head_hbm, head_weight),
        ("contrast", contrast_hbm, contrast),
        ("volume", volume, slab_buf),
    ):
        loads[name] = pltpu.make_async_copy(src, dst, in_sems.at[len(loads)])
        loads[name].start()

    loads["project_in"].wait()
    loads["project_out"].wait()
    for a in range(4):
        parts = [project_in[:, p * 512 + a * 128 : p * 512 + a * 128 + 128] for p in range(3)]
        parts.append(project_out[:, a * 128 : a * 128 + 128])
        pieces[a] = jnp.concatenate(
            [jnp.where(pair == 0, one[:, 0:64], one[:, 64:128]) for one in parts], axis=1
        )
    weight[dp] = pieces[chip % 4]
    loads["image"].wait()
    loads["places"].wait()
    cells = lax.broadcasted_iota(jnp.int32, (16, 16, 128), 1)
    spread_lane = lax.broadcasted_iota(jnp.int32, (16, 16, 128), 2)
    cut = jnp.zeros((PATCHES, 128), F32)
    for r in range(PATCH):
        stripe = image[0, pl.ds(r, 16, stride=PATCH), :]
        stripe = jnp.broadcast_to(stripe[:, None, :], (16, 16, 128))
        stripe = jnp.where(spread_lane // PATCH == cells, stripe, 0.0).reshape(PATCHES, 128)
        cut = cut + jnp.dot(stripe.astype(BF16), places[r], preferred_element_type=F32)
    patches[...] = jnp.concatenate([cut[0:128, 0:64], cut[128:256, 0:64]], axis=1).astype(BF16)
    patch_mean = jnp.sum(cut[:, 0:64], axis=0, keepdims=True) / PATCHES
    pl.semaphore_wait(barrier, count)

    def member(m):
        return chip // 4 * 8 + m // 2 * 2 + core, vol // 2 * 2 + m % 2

    def patch_copy(k, slot):
        to_dp, to_vol = member((head + k) % HEADS)
        return copy(
            patches,
            patch_buf.at[slot],
            patch_sems.at[0, k],
            patch_sems.at[1, slot],
            to_dp,
            to_vol,
        )

    def weight_copy(k, slot):
        to = (chip + k) % chips
        return copy(
            pieces.at[to % 4],
            weight.at[slot],
            weight_sems.at[0, k],
            weight_sems.at[1, slot],
            to * 2 + core,
            vol,
        )

    def weight_relay(at):
        s = at * 2 + core
        return copy(
            weight.at[s], weight.at[s], relay_sems.at[at], weight_sems.at[1, s], other, vol
        )

    def line_copy(k, slot):
        to = (vol + k) % vols
        return copy(picked.at[k], lines.at[slot], line_sems.at[0, k], line_sems.at[1, slot], dp, to)

    each(chips // 2, chips, lambda k: weight_copy(k, dp).start())
    each(1, chips // 2, lambda k: weight_copy(k, dp).start())
    each(1, HEADS, lambda k: patch_copy(k, head).start())
    weight_relay(chip).start()
    patch_buf[head] = patches[...]

    loads["index"].wait()
    loads["sel"].wait()
    loads["volume"].wait()

    def render(step_k, c):
        k = step_k + 1
        v = (vol + k) % vols
        turned = jnp.concatenate([index[v], jnp.zeros((4, 128), jnp.int32)], axis=0)
        turned = turned.astype(F32).T.astype(jnp.int32)
        spot_lane = lax.broadcasted_iota(jnp.int32, (128, 256), 1)
        spot_row = lax.broadcasted_iota(jnp.int32, (128, 256), 0)
        for hyp in range(K):
            line = turned[:, hyp : hyp + 1]
            level = (line >> 8) - vol * slab
            target = jnp.where((level >= 0) & (level < slab), line & 15, 1024)
            hot = jnp.where(spot_lane == (spot_row % 16) * 16 + target, 1.0, 0.0).astype(BF16)
            found = []
            for group in range(8):
                tiles = []
                for i in range(16):
                    spot = spots[v, hyp, group * 16 + i]
                    level = jnp.clip((spot >> 8) - vol * slab, 0, slab - 1)
                    tiles.append(slab_buf[level, (spot >> 4) & 15])
                tiles = jnp.concatenate(tiles, axis=0)
                found.append(
                    jnp.dot(
                        hot[group * 16 : group * 16 + 16], tiles, preferred_element_type=F32
                    )
                )
            found = jnp.concatenate(found, axis=0).astype(BF16)
            picked[k, hyp * PIX : (hyp + 1) * PIX, :] = jnp.dot(
                found, sel[...], preferred_element_type=F32
            ).astype(BF16)

        @pl.when(k < vols)
        def _():
            line_copy(k, vol).start()

        return c

    lax.fori_loop(0, vols, render, 0)
    lines[vol] = picked[vols]

    loads["patch_weight"].wait()
    loads["position"].wait()
    loads["gain"].wait()
    embed = patch_weight[...].astype(F32)
    embed_c = embed - jnp.mean(embed, axis=1, keepdims=True)
    basis[0:64, :] = (embed_c * gain[...]).astype(BF16)
    gram[0:64, :] = lax.dot_general(
        embed_c, embed_c, LAST, precision=HIGHEST, preferred_element_type=F32
    )
    place_mean = jnp.zeros((1, width), F32)
    for part in range(4):
        one = position[part * 64 : part * 64 + 64, :].astype(F32)
        place_mean = place_mean + jnp.sum(one, axis=0, keepdims=True)
        one = one - jnp.mean(one, axis=1, keepdims=True)
        basis[64 + part * 64 : 128 + part * 64, :] = (one * gain[...]).astype(BF16)
        gram[64 + part * 64 : 128 + part * 64, :] = lax.dot_general(
            one, embed_c, LAST, precision=HIGHEST, preferred_element_type=F32
        )
        square[part * 64 : part * 64 + 64, :] = jnp.sum(one * one, axis=1, keepdims=True)
    basis[320:384, :] = jnp.zeros((64, width), BF16)
    basis_t[...] = basis[...].T
    own_row = (
        jnp.dot(
            jnp.broadcast_to(patch_mean, (8, 64)),
            embed,
            precision=HIGHEST,
            preferred_element_type=F32,
        )
        + place_mean / PATCHES
    )

    loads["head"].wait()
    head_t = jnp.concatenate([head_weight[...], jnp.zeros((4, width), F32)], axis=0)
    near = pl.ds(pl.multiple_of(dp * rows // 128 * 128, 128), 128)
    head_wide[...] = jnp.concatenate(
        [head_weight[:, near], jnp.zeros((4, 128), F32)], axis=0
    ).T
    own_emb = jnp.where(
        lax.broadcasted_iota(jnp.int32, (HEADS, width), 0) == head, own_row, 0.0
    )
    own_logit = lax.dot_general(
        own_emb, head_t, LAST, precision=HIGHEST, preferred_element_type=F32
    )

    loads["waves"].wait()
    pixels = image[0]
    first_cos = jnp.dot(waves[0], pixels, precision=HIGHEST, preferred_element_type=F32)
    first_sin = jnp.dot(waves[1], pixels, precision=HIGHEST, preferred_element_type=F32)
    spectrum = jnp.dot(first_cos, waves[2], precision=HIGHEST, preferred_element_type=F32)
    spectrum = spectrum + jnp.dot(
        first_sin, waves[3], precision=HIGHEST, preferred_element_type=F32
    )
    spectrum = spectrum / PIX

    def weight_pass(k):
        at = (chip + chips - k) % chips
        weight_copy(k, at * 2 + core).wait_recv()
        weight_relay(at).start()

    each(1, chips // 2, weight_pass)

    def norms(k, c):
        j = (head + HEADS - k) % HEADS

        @pl.when(k > 0)
        def _():
            patch_copy(k, j).wait_recv()

        both = patch_buf[j]
        one = jnp.concatenate([both[:, 0:64], both[:, 64:128]], axis=0)
        tokens[j] = one
        tokens_t[:, pl.ds(pl.multiple_of(j * PATCHES, PATCHES), PATCHES)] = one.T
        one = one.astype(F32)
        turned = jnp.dot(one, gram[0:64], precision=HIGHEST, preferred_element_type=F32)
        total = jnp.sum(one * (turned + 2.0 * gram[64:320]), axis=1, keepdims=True)
        total = jnp.maximum(total + square[...], 0.0) / width
        scales[j] = lax.rsqrt(total + EPSILON)
        return c

    lax.fori_loop(0, HEADS, norms, 0)
    each(chips // 2, chips, weight_pass)

    def weight_rest(k):
        s = (chip + chips - k) % chips * 2 + 1 - core
        weight_copy(0, s).wait_recv()

    each(0, chips, weight_rest)

    whole = weight[...].reshape(width, 256)
    half = jnp.where(lax.broadcasted_iota(jnp.int32, (1, 256), 1) < 64, HEAD_DIM ** (-0.5), 1.0)
    both = jnp.dot(basis[0:320], whole, preferred_element_type=F32) * half
    total_buf[...] = both[64:320]
    turn = both[0:64].astype(BF16)
    out_w = weight[:, :, 192:256].reshape(width, HEAD_DIM).astype(F32)
    mixed = jnp.dot(head_t, out_w, precision=HIGHEST, preferred_element_type=F32)

    def forward(j):
        t = jnp.dot(tokens[j], turn, preferred_element_type=F32) + total_buf[...]
        t = (t * scales[j]).astype(BF16)
        triple[j] = t
        scores = lax.dot_general(t[:, 64:128], t[:, 0:64], LAST, preferred_element_type=F32)
        raised = jnp.exp(scores)
        chosen = (raised * (1.0 / jnp.sum(raised, axis=0, keepdims=True))).astype(BF16)
        attention[j] = chosen
        col = jnp.sum(chosen.astype(F32), axis=1, keepdims=True)
        column[j] = col
        mean_att[pl.ds(j, 1), :] = (
            jnp.sum(col * t[:, 128:256].astype(F32), axis=0, keepdims=True) / PATCHES
        )

    def forwards(i):
        forward(2 * i)
        forward(2 * i + 1)

    each(0, HEADS // 2, forwards)

    loads["contrast"].wait()
    each(1, vols, lambda k: line_copy(k, (vol + vols - k) % vols).wait_recv())
    slices = lines[0].astype(F32)
    for v in range(1, vols):
        slices = slices + lines[v].astype(F32)
    lane = lax.broadcasted_iota(jnp.int32, (HEADS, 128), 1)
    row = lax.broadcasted_iota(jnp.int32, (HEADS, 128), 0)
    filt = contrast[0].astype(F32)
    misfits = jnp.zeros((HEADS, 128), F32)
    for k in range(K):
        misfit = filt * slices[k * PIX : (k + 1) * PIX] - spectrum
        value = jnp.sum(jnp.sum(misfit * misfit, axis=0, keepdims=True), axis=1, keepdims=True)
        misfits = jnp.where(lane == k, value / (PIX * PIX), misfits)
    errors_out[...] = misfits
    mine = row == head
    means = mean_att[:, 0:HEAD_DIM]
    logit = own_logit + lax.dot_general(
        means, mixed, LAST, precision=HIGHEST, preferred_element_type=F32
    )
    small_send[0:8, :] = jnp.concatenate([logit, jnp.zeros((HEADS, 120), F32)], axis=1)
    small_send[8:16, :] = jnp.where(mine, misfits, 0.0)

    def small_copy(k, slot):
        to_dp, to_vol = member((head + k) % HEADS)
        return copy(
            small_send,
            small_recv.at[slot],
            small_sems.at[0, k],
            small_sems.at[1, slot],
            to_dp,
            to_vol,
        )

    each(1, HEADS, lambda k: small_copy(k, head).start())
    small_recv[head] = small_send[...]
    each(1, HEADS, lambda k: small_copy(k, (head + HEADS - k) % HEADS).wait_recv())
    summed = jnp.sum(small_recv[...], axis=0)
    misfits = summed[8:16]
    raised = jnp.where(lane < K, jnp.exp(summed[0:8]), 0.0)
    chances = raised / jnp.sum(raised, axis=1, keepdims=True)
    expected = jnp.sum(chances * misfits, axis=1, keepdims=True)
    slope = chances * (misfits - expected)
    pulled = jnp.zeros((HEADS, HEAD_DIM), F32)
    for k in range(K):
        pulled = pulled + slope[:, k : k + 1] * mixed[k : k + 1, :]
    pulled_buf[...] = jnp.concatenate(
        [pulled / PATCHES, jnp.zeros((HEADS, 128 - HEAD_DIM), F32)], axis=1
    )
    slope_buf[...] = slope

    outer = lax.dot_general(
        slope, means, FIRST, precision=HIGHEST, preferred_element_type=F32
    )[0:8]
    pooled_t = lax.dot_general(
        jnp.where(mine, slope, 0.0),
        own_emb,
        FIRST,
        precision=HIGHEST,
        preferred_element_type=F32,
    )[0:8]
    pooled_t = pooled_t + lax.dot_general(
        outer, out_w, LAST, precision=HIGHEST, preferred_element_type=F32
    )
    side_send[:, 0:width] = pooled_t
    side_send[:, width:] = jnp.concatenate([outer, jnp.zeros((8, 128 - HEAD_DIM), F32)], axis=1)
    side = copy(side_send, side_recv, core_sems.at[0], core_sems.at[1], other, vol)
    side.start()

    wide = lax.broadcasted_iota(jnp.int32, (PATCHES, 128), 1)

    def backward(j):
        t = triple[j]
        chosen = attention[j]
        wider = chosen.astype(F32)
        up = jnp.sum(
            t[:, 128:256].astype(F32) * pulled_buf[pl.ds(j, 1), :], axis=1, keepdims=True
        )
        center = jnp.sum(wider * up, axis=0, keepdims=True)
        inner = (wider * (up - center)).astype(BF16)
        sides = t[:, 0:128]
        key_slope = jnp.dot(inner, sides, preferred_element_type=F32)
        query_slope = lax.dot_general(inner, sides, FIRST, preferred_element_type=F32)
        scale = scales[j]
        slopes = jnp.where(wide < 64, key_slope, query_slope * HEAD_DIM ** (-0.5)) * scale
        spread = (column[j] * scale) * slope_buf[pl.ds(j, 1), :]
        terms = jnp.concatenate([slopes, spread], axis=1)
        terms_buf[pl.ds(pl.multiple_of(j * PATCHES, PATCHES), PATCHES), :] = terms.astype(BF16)
        return terms

    total_buf[...] = jnp.zeros((PATCHES, 256), F32)

    def backwards(i):
        total_buf[...] += backward(2 * i) + backward(2 * i + 1)

    each(0, HEADS // 2, backwards)

    factor_send[0:64, :] = jnp.dot(
        tokens_t[...], terms_buf[...], preferred_element_type=F32
    ).astype(BF16)
    factor_send[64:320, :] = total_buf[...].astype(BF16)
    factors = copy(factor_send, factor_recv, core_sems.at[2], core_sems.at[3], other, vol)
    factors.start()
    factors.wait_recv()
    side.wait_recv()
    factor_sum[0:320, :] = (
        factor_send[...].astype(F32) + factor_recv[...].astype(F32)
    ).astype(BF16)
    factor_sum[320:384, :] = jnp.zeros((64, 256), BF16)
    sides = side_send[...] + side_recv[...]
    pooled_t = sides[:, 0:width]
    outer = sides[:, width : width + HEAD_DIM]

    value_t = lax.dot_general(
        factor_sum[:, 128:256], basis[...], FIRST, preferred_element_type=F32
    )[0:8]
    fill = [jnp.zeros((HEADS, 64 - rows), F32)] if rows < 64 else []
    for d in range(dps):
        part = slice(d * rows, (d + 1) * rows)
        top = jnp.concatenate([value_t[:, part]] + fill + [outer], axis=1)
        low = jnp.concatenate([mixed, pooled_t[:, part]] + fill, axis=1)
        tile_send[d] = jnp.where(row < 4, top, pltpu.roll(low, 4, 0))

    def tile_copy(k, slot):
        e = (me + k) % count
        d = e // vols * 2 + core
        return copy(
            tile_send.at[d],
            tile_recv.at[slot],
            tile_sems.at[0, k],
            tile_sems.at[1, slot],
            d,
            e % vols,
        )

    def grad_copy(k, slot):
        e = (me + k) % count
        d = e // vols * 2 + core
        return copy(
            grad_send.at[d],
            grad_recv.at[slot],
            grad_sems.at[0, k],
            grad_sems.at[1, slot],
            d,
            e % vols,
        )

    each(count // 2, count, lambda k: tile_copy(k, me).start())
    each(1, count // 2, lambda k: tile_copy(k, me).start())
    grad_send[...] = (
        jnp.dot(basis_t[...], factor_sum[:, 0:128], preferred_element_type=F32)
        .astype(BF16)
        .reshape(dps, rows, 128)
    )
    each(count // 2, count, lambda k: grad_copy(k, me).start())
    each(1, count // 2, lambda k: grad_copy(k, me).start())
    grad_recv[me] = grad_send[dp]
    tile_recv[me] = tile_send[dp]

    each(1, count, lambda k: tile_copy(k, (me + count - k) % count).wait_recv())

    pooled_sum = pltpu.roll(jnp.sum(tile_recv[...], axis=0), 4, 0)
    head_send[...] = pooled_sum

    def head_copy(k, slot):
        to = (chip + k) % chips
        return copy(
            head_send,
            head_out.at[core, slot],
            head_sems.at[0, k],
            head_sems.at[1, slot],
            to * 2 + core,
            vol,
        )

    each(1, chips, lambda k: head_copy(k, chip).start())
    head_out[core, chip] = pooled_sum

    head_own = head_wide[pl.ds(pl.multiple_of(dp * rows % 128, rows), rows), :]
    for h in range(HEADS):
        senders = senders_of(dps, vols, h)
        tile = tile_recv[senders[0]]
        mixed_h = jnp.where(row < 4, pltpu.roll(tile, 4, 0), 0.0)[:, 0:64]
        for s in senders[1:]:
            tile = tile + tile_recv[s]
        tile = jnp.where(row < 4, tile, 0.0)
        value_out[:, h * 64 : h * 64 + 64] = (
            lax.dot_general(
                tile[:, 0:rows], mixed_h, FIRST, precision=HIGHEST, preferred_element_type=F32
            )
            / PATCHES
        )
        value_out[:, 512 + h * 64 : 576 + h * 64] = jnp.dot(
            head_own, tile[:, 64:128], precision=HIGHEST, preferred_element_type=F32
        )

    each(1, chips, lambda k: head_copy(k, (chip + chips - k) % chips).wait_recv())
    heads = copy(
        head_out.at[core], head_out.at[core], core_sems.at[4], core_sems.at[5], other, vol
    )
    heads.start()

    each(1, count, lambda k: grad_copy(k, (me + count - k) % count).wait_recv())
    copy(
        head_out.at[1 - core], head_out.at[1 - core], core_sems.at[4], core_sems.at[5], other, vol
    ).wait_recv()

    each(1, HEADS, lambda k: patch_copy(k, head).wait_send())
    each(1, chips, lambda k: weight_copy(k, dp).wait_send())
    each(0, chips, lambda at: weight_relay(at).wait_send())
    each(1, vols, lambda k: line_copy(k, vol).wait_send())
    each(1, HEADS, lambda k: small_copy(k, head).wait_send())
    side.wait_send()
    factors.wait_send()
    each(1, count, lambda k: tile_copy(k, me).wait_send())
    each(1, count, lambda k: grad_copy(k, me).wait_send())
    each(1, chips, lambda k: head_copy(k, chip).wait_send())
    heads.wait_send()


def senders_of(dps, vols, h):
    return [
        (z * 4 + h // 2) * vols + v * 2 + h % 2 for z in range(dps // 8) for v in range(vols // 2)
    ]


def finish(dps, vols, errors, grads, values, heads, errors_out, in_out, out_out, head_out):
    rows = values.shape[0]
    for h in range(HEADS):
        senders = senders_of(dps, vols, h)
        both = grads[senders[0]].astype(F32)
        for s in senders[1:]:
            both = both + grads[s].astype(F32)
        in_out[:, h * 64 : h * 64 + 64] = both[:, 64:128]
        in_out[:, 512 + h * 64 : 576 + h * 64] = both[:, 0:64]
    in_out[:, 1024:1536] = values[:, 0:512]
    out_out[...] = values[:, 512:1024]
    errors_out[...] = errors[0:1, 0:K]
    for d in range(dps):
        head_out[:, d * rows : (d + 1) * rows] = heads[d % 2, d // 2][0:K, 64 : 64 + rows]


def constants():
    freq = np.arange(PIX) - PIX // 2
    phase = (freq[:, None] * np.arange(PIX)[None, :] % PIX) * (2.0 * math.pi / PIX)
    cosine, sine = np.cos(phase), np.sin(phase)
    waves = np.stack([cosine, sine, (cosine + sine).T, (cosine - sine).T]).astype(np.float32)
    sel = np.zeros((2 * PIX, PIX), np.float32)
    sel[2 * np.arange(PIX), np.arange(PIX)] = 1.0
    places = np.zeros((PATCH, PIX, PIX), np.float32)
    for r in range(PATCH):
        places[r, np.arange(PIX), r * PATCH + np.arange(PIX) % PATCH] = 1.0
    return waves, sel, places


def local(
    dps,
    vols,
    images,
    contrast,
    volume,
    line_index,
    patch_weight,
    position,
    norm_gain,
    project_in,
    project_out,
    head_weight,
):
    width = norm_gain.shape[0]
    rows = project_in.shape[0]
    chips = dps // 2
    count = chips * vols
    waves, sel, places = constants()
    slab, side, _ = volume.shape
    vmem = pl.BlockSpec(memory_space=pltpu.VMEM)
    hbm = pl.BlockSpec(memory_space=pltpu.HBM)
    inputs = (
        images,
        contrast,
        patch_weight,
        position,
        norm_gain.reshape(1, width),
        project_in,
        project_out,
        head_weight.T,
        jnp.asarray(waves),
        jnp.asarray(sel, BF16),
        jnp.asarray(places, BF16),
    )
    errors, grads, values, heads = pl.pallas_call(
        functools.partial(step, dps, vols),
        out_shape=(
            jax.ShapeDtypeStruct((8, 128), F32),
            jax.ShapeDtypeStruct((count, rows, 128), BF16),
            jax.ShapeDtypeStruct((rows, 1024), F32),
            jax.ShapeDtypeStruct((2, chips, 8, 128), F32),
        ),
        in_specs=[pl.BlockSpec(memory_space=pltpu.SMEM)] + [hbm] * (2 + len(inputs)),
        out_specs=(vmem,) * 4,
        scratch_shapes=[pltpu.VMEM(line_index.shape, jnp.int32)]
        + [pltpu.VMEM(one.shape, one.dtype) for one in inputs]
        + [
            pltpu.VMEM((slab, 16, 16, side), BF16),
            pltpu.VMEM((vols + 1, K * PIX, PIX), BF16),
            pltpu.VMEM((PATCHES // 2, 128), BF16),
            pltpu.VMEM((4, rows, 256), BF16),
            pltpu.VMEM((128, 8), F32),
            pltpu.VMEM((vols, K * PIX, PIX), BF16),
            pltpu.VMEM((HEADS, PATCHES // 2, 128), BF16),
            pltpu.VMEM((dps, rows, 256), BF16),
            pltpu.VMEM((384, width), BF16),
            pltpu.VMEM((width, 384), BF16),
            pltpu.VMEM((320, 64), F32),
            pltpu.VMEM((PATCHES, 1), F32),
            pltpu.VMEM((HEADS, PATCHES, 64), BF16),
            pltpu.VMEM((64, HEADS * PATCHES), BF16),
            pltpu.VMEM((HEADS, PATCHES, 1), F32),
            pltpu.VMEM((HEADS, PATCHES, PATCHES), BF16),
            pltpu.VMEM((HEADS, PATCHES, 256), BF16),
            pltpu.VMEM((HEADS, PATCHES, 1), F32),
            pltpu.VMEM((HEADS, 128), F32),
            pltpu.VMEM((16, 128), F32),
            pltpu.VMEM((HEADS, 16, 128), F32),
            pltpu.VMEM((HEADS, 128), F32),
            pltpu.VMEM((HEADS, 128), F32),
            pltpu.VMEM((HEADS * PATCHES, 256), BF16),
            pltpu.VMEM((PATCHES, 256), F32),
            pltpu.VMEM((320, 256), BF16),
            pltpu.VMEM((320, 256), BF16),
            pltpu.VMEM((384, 256), BF16),
            pltpu.VMEM((8, width + 128), F32),
            pltpu.VMEM((8, width + 128), F32),
            pltpu.VMEM((dps, rows, 128), BF16),
            pltpu.VMEM((dps, 8, 128), F32),
            pltpu.VMEM((count, 8, 128), F32),
            pltpu.VMEM((8, 128), F32),
            pltpu.SemaphoreType.DMA((13,)),
            pltpu.SemaphoreType.DMA((2, vols)),
            pltpu.SemaphoreType.DMA((2, HEADS)),
            pltpu.SemaphoreType.DMA((2, dps)),
            pltpu.SemaphoreType.DMA((chips,)),
            pltpu.SemaphoreType.DMA((2, HEADS)),
            pltpu.SemaphoreType.DMA((6,)),
            pltpu.SemaphoreType.DMA((2, count)),
            pltpu.SemaphoreType.DMA((2, count)),
            pltpu.SemaphoreType.DMA((2, chips)),
        ],
        compiler_params=pltpu.CompilerParams(
            collective_id=0, has_side_effects=True, vmem_limit_bytes=56 * 1024 * 1024
        ),
        name="pose_step",
    )(line_index, line_index, volume.reshape(slab, side // 16, 16, side), *inputs)
    errors, in_grad, out_grad, head_grad = pl.pallas_call(
        functools.partial(finish, dps, vols),
        out_shape=(
            jax.ShapeDtypeStruct((1, K), F32),
            jax.ShapeDtypeStruct((rows, 3 * HEADS * HEAD_DIM), F32),
            jax.ShapeDtypeStruct((rows, HEADS * HEAD_DIM), F32),
            jax.ShapeDtypeStruct((K, width), F32),
        ),
        in_specs=[vmem] * 4,
        out_specs=(vmem,) * 4,
        name="finish",
    )(errors, grads, values, heads)
    return errors, in_grad, out_grad, head_grad.T


def solution(mesh):
    placed = (
        P(("dp", "vol"), None, None),
        P(("dp", "vol"), None, None),
        P("vol", None, None),
        P("dp", None, None),
        P(),
        P(),
        P(),
        P("dp", None),
        P("dp", None),
        P(),
    )
    return jax.shard_map(
        functools.partial(local, mesh.shape["dp"], mesh.shape["vol"]),
        mesh=mesh,
        in_specs=placed,
        out_specs=(P(("dp", "vol"), None), P("dp", None), P("dp", None), P()),
        check_vma=False,
    )
```

```python
import functools
import math

import jax
import jax.numpy as jnp
import numpy as np
from jax import lax
from jax.experimental import pallas as pl
from jax.experimental.pallas import tpu as pltpu
from jax.sharding import PartitionSpec as P

HEADS = 8
HEAD_DIM = 64
PIX = 128
PATCH = 8
PATCHES = 256
K = 4
EPSILON = 1e-05
F32 = jnp.float32
BF16 = jnp.bfloat16
HIGHEST = lax.Precision.HIGHEST
FIRST = (((0,), (0,)), ((), ()))
LAST = (((1,), (1,)), ((), ()))
MESH = pl.DeviceIdType.MESH


def step(
    dps,
    vols,
    spots,
    index_hbm,
    volume,
    image_hbm,
    contrast_hbm,
    patch_weight_hbm,
    position_hbm,
    gain_hbm,
    project_in_hbm,
    project_out_hbm,
    head_hbm,
    waves_hbm,
    sel_hbm,
    places_hbm,
    errors_out,
    grad_recv,
    value_out,
    head_out,
    index,
    image,
    contrast,
    patch_weight,
    position,
    gain,
    project_in,
    project_out,
    head_weight,
    waves,
    sel,
    places,
    slab_buf,
    picked,
    patches,
    pieces,
    head_wide,
    lines,
    patch_buf,
    weight,
    basis,
    basis_t,
    gram,
    square,
    tokens,
    tokens_t,
    scales,
    attention,
    triple,
    column,
    mean_att,
    small_send,
    small_recv,
    pulled_buf,
    slope_buf,
    terms_buf,
    total_buf,
    factor_send,
    factor_recv,
    factor_sum,
    side_send,
    side_recv,
    grad_send,
    tile_send,
    tile_recv,
    head_send,
    in_sems,
    line_sems,
    patch_sems,
    weight_sems,
    relay_sems,
    small_sems,
    core_sems,
    grad_sems,
    tile_sems,
    head_sems,
):
    dp = lax.axis_index("dp")
    vol = lax.axis_index("vol")
    core = dp % 2
    chip = dp // 2
    chips = dps // 2
    count = chips * vols
    me = chip * vols + vol
    pair = vol % 2
    head = (chip % 4) * 2 + pair
    rows = project_in.shape[0]
    width = gain.shape[1]
    slab = volume.shape[0]

    def copy(src, dst, send_sem, recv_sem, to_dp, to_vol):
        return pltpu.make_async_remote_copy(
            src_ref=src,
            dst_ref=dst,
            send_sem=send_sem,
            recv_sem=recv_sem,
            device_id=(to_dp, to_vol),
            device_id_type=MESH,
        )

    def each(first, last, body):
        def run(k, c):
            body(k)
            return c

        lax.fori_loop(first, last, run, 0)

    other = dp + 1 - 2 * core
    barrier = pltpu.get_barrier_semaphore()

    def greet(k):
        e = (me + k) % count
        pl.semaphore_signal(
            barrier, inc=1, device_id=(e // vols * 2 + core, e % vols), device_id_type=MESH
        )

    each(1, count, greet)
    pl.semaphore_signal(barrier, inc=1, device_id=(other, vol), device_id_type=MESH)

    loads = {}
    for name, src, dst in (
        ("image", image_hbm, image),
        ("places", places_hbm, places),
        ("project_in", project_in_hbm, project_in),
        ("project_out", project_out_hbm, project_out),
        ("index", index_hbm, index),
        ("sel", sel_hbm, sel),
        ("waves", waves_hbm, waves),
        ("patch_weight", patch_weight_hbm, patch_weight),
        ("position", position_hbm, position),
        ("gain", gain_hbm, gain),
        ("head", head_hbm, head_weight),
        ("contrast", contrast_hbm, contrast),
        ("volume", volume, slab_buf),
    ):
        loads[name] = pltpu.make_async_copy(src, dst, in_sems.at[len(loads)])
        loads[name].start()

    loads["project_in"].wait()
    loads["project_out"].wait()
    loads["head"].wait()
    near = pl.ds(pl.multiple_of(dp * rows // 128 * 128, 128), 128)
    head_wide[...] = jnp.concatenate(
        [head_weight[:, near], jnp.zeros((4, 128), F32)], axis=0
    ).T
    head_own = head_wide[pl.ds(pl.multiple_of(dp * rows % 128, rows), rows), :]
    share = lax.dot_general(
        head_own,
        project_out[...].astype(F32),
        FIRST,
        precision=HIGHEST,
        preferred_element_type=F32,
    )
    for a in range(4):
        parts = [project_in[:, p * 512 + a * 128 : p * 512 + a * 128 + 128] for p in range(3)]
        parts.append(share[:, a * 128 : a * 128 + 128])
        query, key, value, mix = [
            jnp.where(pair == 0, one[:, 0:64], one[:, 64:128]) for one in parts
        ]
        high = mix.astype(BF16)
        mix = jnp.concatenate([high.astype(F32), mix - high.astype(F32)], axis=1)
        pieces[a, 0:rows, :] = jnp.concatenate([query, key], axis=1)
        pieces[a, rows : rows + rows // 2, :] = jnp.concatenate(
            [value[0 : rows // 2], value[rows // 2 : rows]], axis=1
        )
        pieces[a, rows + rows // 2 :, :] = jnp.concatenate(
            [mix, jnp.zeros((8, 128), F32)], axis=0
        ).astype(BF16)
    weight[dp] = pieces[chip % 4]
    loads["image"].wait()
    loads["places"].wait()
    cells = lax.broadcasted_iota(jnp.int32, (16, 16, 128), 1)
    spread_lane = lax.broadcasted_iota(jnp.int32, (16, 16, 128), 2)
    cut = jnp.zeros((PATCHES, 128), F32)
    for r in range(PATCH):
        stripe = image[0, pl.ds(r, 16, stride=PATCH), :]
        stripe = jnp.broadcast_to(stripe[:, None, :], (16, 16, 128))
        stripe = jnp.where(spread_lane // PATCH == cells, stripe, 0.0).reshape(PATCHES, 128)
        cut = cut + jnp.dot(stripe.astype(BF16), places[r], preferred_element_type=F32)
    patches[...] = jnp.concatenate([cut[0:128, 0:64], cut[128:256, 0:64]], axis=1).astype(BF16)
    patch_mean = jnp.sum(cut[:, 0:64], axis=0, keepdims=True) / PATCHES
    loads["patch_weight"].wait()
    loads["position"].wait()
    loads["gain"].wait()
    embed = patch_weight[...].astype(F32)
    embed_c = embed - jnp.mean(embed, axis=1, keepdims=True)
    basis[0:64, :] = (embed_c * gain[...]).astype(BF16)
    gram[0:64, :] = lax.dot_general(
        embed_c, embed_c, LAST, precision=HIGHEST, preferred_element_type=F32
    )
    place_mean = jnp.zeros((1, width), F32)
    for part in range(4):
        one = position[part * 64 : part * 64 + 64, :].astype(F32)
        place_mean = place_mean + jnp.sum(one, axis=0, keepdims=True)
        one = one - jnp.mean(one, axis=1, keepdims=True)
        basis[64 + part * 64 : 128 + part * 64, :] = (one * gain[...]).astype(BF16)
        gram[64 + part * 64 : 128 + part * 64, :] = lax.dot_general(
            one, embed_c, LAST, precision=HIGHEST, preferred_element_type=F32
        )
        square[part * 64 : part * 64 + 64, :] = jnp.sum(one * one, axis=1, keepdims=True)
    basis[320:384, :] = jnp.zeros((64, width), BF16)
    basis_t[...] = basis[...].T
    own_row = (
        jnp.dot(
            jnp.broadcast_to(patch_mean, (8, 64)),
            embed,
            precision=HIGHEST,
            preferred_element_type=F32,
        )
        + place_mean / PATCHES
    )

    head_t = jnp.concatenate([head_weight[...], jnp.zeros((4, width), F32)], axis=0)
    own_logit = lax.dot_general(
        own_row, head_t, LAST, precision=HIGHEST, preferred_element_type=F32
    )
    row = lax.broadcasted_iota(jnp.int32, (HEADS, 128), 0)
    lane = lax.broadcasted_iota(jnp.int32, (HEADS, 128), 1)
    mine = row == head
    own_logit = jnp.where(mine[:, 0:HEADS], own_logit, 0.0)

    loads["waves"].wait()
    pixels = image[0]
    first_cos = jnp.dot(waves[0], pixels, precision=HIGHEST, preferred_element_type=F32)
    first_sin = jnp.dot(waves[1], pixels, precision=HIGHEST, preferred_element_type=F32)
    spectrum = jnp.dot(first_cos, waves[2], precision=HIGHEST, preferred_element_type=F32)
    spectrum = spectrum + jnp.dot(
        first_sin, waves[3], precision=HIGHEST, preferred_element_type=F32
    )
    spectrum = spectrum / PIX

    loads["index"].wait()
    loads["sel"].wait()
    loads["volume"].wait()

    def render(step_k, c):
        k = step_k + 1
        v = (vol + k) % vols
        turned = jnp.concatenate([index[v], jnp.zeros((4, 128), jnp.int32)], axis=0)
        turned = turned.astype(F32).T.astype(jnp.int32)
        spot_lane = lax.broadcasted_iota(jnp.int32, (128, 256), 1)
        spot_row = lax.broadcasted_iota(jnp.int32, (128, 256), 0)
        for hyp in range(K):
            line = turned[:, hyp : hyp + 1]
            level = (line >> 8) - vol * slab
            target = jnp.where((level >= 0) & (level < slab), line & 15, 1024)
            hot = jnp.where(spot_lane == (spot_row % 16) * 16 + target, 1.0, 0.0).astype(BF16)
            found = []
            for group in range(8):
                tiles = []
                for i in range(16):
                    spot = spots[v, hyp, group * 16 + i]
                    level = jnp.clip((spot >> 8) - vol * slab, 0, slab - 1)
                    tiles.append(slab_buf[level, (spot >> 4) & 15])
                tiles = jnp.concatenate(tiles, axis=0)
                found.append(
                    jnp.dot(
                        hot[group * 16 : group * 16 + 16], tiles, preferred_element_type=F32
                    )
                )
            found = jnp.concatenate(found, axis=0).astype(BF16)
            picked[k, hyp * PIX : (hyp + 1) * PIX, :] = jnp.dot(
                found, sel[...], preferred_element_type=F32
            ).astype(BF16)
        return c

    lax.fori_loop(0, vols, render, 0)
    lines[vol] = picked[vols]

    pl.semaphore_wait(barrier, count)

    def member(m):
        return chip // 4 * 8 + m // 2 * 2 + core, vol // 2 * 2 + m % 2

    def patch_copy(k, slot):
        to_dp, to_vol = member((head + k) % HEADS)
        return copy(
            patches,
            patch_buf.at[slot],
            patch_sems.at[0, k],
            patch_sems.at[1, slot],
            to_dp,
            to_vol,
        )

    def weight_copy(k, slot):
        to = (chip + k) % chips
        return copy(
            pieces.at[to % 4],
            weight.at[slot],
            weight_sems.at[0, k],
            weight_sems.at[1, slot],
            to * 2 + core,
            vol,
        )

    def weight_relay(at):
        s = at * 2 + core
        return copy(
            weight.at[s], weight.at[s], relay_sems.at[at], weight_sems.at[1, s], other, vol
        )

    def line_copy(k, slot):
        to = (vol + k) % vols
        return copy(picked.at[k], lines.at[slot], line_sems.at[0, k], line_sems.at[1, slot], dp, to)

    each(chips // 2, chips, lambda k: weight_copy(k, dp).start())
    each(1, vols, lambda k: line_copy(k, vol).start())
    each(1, chips // 2, lambda k: weight_copy(k, dp).start())
    each(1, HEADS, lambda k: patch_copy(k, head).start())
    weight_relay(chip).start()
    patch_buf[head] = patches[...]

    def weight_pass(k):
        at = (chip + chips - k) % chips
        weight_copy(k, at * 2 + core).wait_recv()
        weight_relay(at).start()

    each(1, chips // 2, weight_pass)

    def norms(k, c):
        j = (head + HEADS - k) % HEADS

        @pl.when(k > 0)
        def _():
            patch_copy(k, j).wait_recv()

        both = patch_buf[j]
        one = jnp.concatenate([both[:, 0:64], both[:, 64:128]], axis=0)
        tokens[j] = one
        tokens_t[:, pl.ds(pl.multiple_of(j * PATCHES, PATCHES), PATCHES)] = one.T
        one = one.astype(F32)
        turned = jnp.dot(one, gram[0:64], precision=HIGHEST, preferred_element_type=F32)
        total = jnp.sum(one * (turned + 2.0 * gram[64:320]), axis=1, keepdims=True)
        total = jnp.maximum(total + square[...], 0.0) / width
        scales[j] = jnp.broadcast_to(lax.rsqrt(total + EPSILON), (PATCHES, 128))
        return c

    lax.fori_loop(0, HEADS, norms, 0)
    each(chips // 2, chips, weight_pass)

    loads["contrast"].wait()
    each(1, vols, lambda k: line_copy(k, (vol + vols - k) % vols).wait_recv())
    slices = lines[0].astype(F32)
    for v in range(1, vols):
        slices = slices + lines[v].astype(F32)
    filt = contrast[0].astype(F32)
    misfits = jnp.zeros((HEADS, 128), F32)
    for k in range(K):
        misfit = filt * slices[k * PIX : (k + 1) * PIX] - spectrum
        value = jnp.sum(jnp.sum(misfit * misfit, axis=0, keepdims=True), axis=1, keepdims=True)
        misfits = jnp.where(lane == k, value / (PIX * PIX), misfits)
    errors_out[...] = misfits
    misfits = jnp.where(mine, pltpu.roll(misfits, 4, 1), 0.0)
    def weight_rest(k):
        s = (chip + chips - k) % chips * 2 + 1 - core
        weight_copy(0, s).wait_recv()

    each(0, chips, weight_rest)

    sides = weight[:, 0:rows, :].reshape(width, 128)
    value = weight[:, rows : rows + rows // 2, :]
    value = jnp.concatenate([value[:, :, 0:64], value[:, :, 64:128]], axis=1)
    half = jnp.where(lax.broadcasted_iota(jnp.int32, (1, 128), 1) < 64, HEAD_DIM ** (-0.5), 1.0)
    sides = jnp.dot(basis[0:320], sides, preferred_element_type=F32) * half
    value = jnp.dot(
        basis[0:320], value.reshape(width, HEAD_DIM), preferred_element_type=F32
    )
    both = jnp.concatenate([sides, value, jnp.zeros((320, 64), F32)], axis=1)
    total_buf[...] = both[64:320]
    turn = both[0:64].astype(BF16)
    mixed = jnp.sum(weight[:, rows + rows // 2 :, :].astype(F32), axis=0)[0:8]
    mixed = mixed[:, 0:64] + mixed[:, 64:128]

    ones = jnp.ones((PATCHES, 128), BF16)

    def forward(j):
        scale = scales[j]
        t = jnp.dot(tokens[j], turn, preferred_element_type=F32) + total_buf[...]
        t = (t * jnp.concatenate([scale, scale], axis=1)).astype(BF16)
        triple[j] = t
        scores = lax.dot_general(t[:, 64:128], t[:, 0:64], LAST, preferred_element_type=F32)
        raised = jnp.exp(scores)
        chosen = (raised * (1.0 / jnp.sum(raised, axis=0, keepdims=True))).astype(BF16)
        attention[j] = chosen
        col = jnp.dot(chosen, ones, preferred_element_type=F32)
        column[j] = col * scale
        mean_att[pl.ds(j, 1), :] = (
            jnp.sum(col * t[:, 128:256].astype(F32), axis=0, keepdims=True) / PATCHES
        )

    def forwards(i):
        forward(2 * i)
        forward(2 * i + 1)

    each(0, HEADS // 2, forwards)

    means = mean_att[:, 0:HEAD_DIM]
    logit = own_logit + lax.dot_general(
        means, mixed, LAST, precision=HIGHEST, preferred_element_type=F32
    )
    logit = jnp.where(
        lane < K, jnp.concatenate([logit, jnp.zeros((HEADS, 120), F32)], axis=1), misfits
    )
    small_send[...] = logit

    def small_copy(k, slot):
        to_dp, to_vol = member((head + k) % HEADS)
        return copy(
            small_send,
            small_recv.at[slot],
            small_sems.at[0, k],
            small_sems.at[1, slot],
            to_dp,
            to_vol,
        )

    each(1, HEADS, lambda k: small_copy(k, head).start())
    small_recv[head] = small_send[...]
    each(1, HEADS, lambda k: small_copy(k, (head + HEADS - k) % HEADS).wait_recv())
    summed = jnp.sum(small_recv[...], axis=0)
    misfits = jnp.where(lane < K, pltpu.roll(summed, 124, 1), 0.0)
    raised = jnp.where(lane < K, jnp.exp(summed), 0.0)
    chances = raised / jnp.sum(raised, axis=1, keepdims=True)
    expected = jnp.sum(chances * misfits, axis=1, keepdims=True)
    slope = chances * (misfits - expected)
    pulled = jnp.zeros((HEADS, HEAD_DIM), F32)
    for k in range(K):
        pulled = pulled + slope[:, k : k + 1] * mixed[k : k + 1, :]
    pulled_buf[...] = jnp.concatenate(
        [pulled / PATCHES, jnp.zeros((HEADS, 128 - HEAD_DIM), F32)], axis=1
    )
    slope_buf[...] = slope

    slope_t = slope.T[0:8]
    outer = jnp.zeros((HEADS, 128), F32)
    for j in range(HEADS):
        outer = outer + slope_t[:, j : j + 1] * mean_att[j : j + 1, :]
    own = jnp.sum(jnp.where(lane[:, 0:HEADS] == head, slope_t, 0.0), axis=1, keepdims=True)
    side_send[:, 0:width] = own * own_row
    side_send[:, width:] = outer
    side = copy(side_send, side_recv, core_sems.at[0], core_sems.at[1], other, vol)
    side.start()

    wide = lax.broadcasted_iota(jnp.int32, (PATCHES, 128), 1)

    def backward(j):
        t = triple[j]
        chosen = attention[j]
        wider = chosen.astype(F32)
        up = jnp.sum(
            t[:, 128:256].astype(F32) * pulled_buf[pl.ds(j, 1), :], axis=1, keepdims=True
        )
        center = jnp.sum(wider * up, axis=0, keepdims=True)
        inner = (wider * (up - center)).astype(BF16)
        sides = t[:, 0:128]
        key_slope = jnp.dot(inner, sides, preferred_element_type=F32)
        query_slope = lax.dot_general(inner, sides, FIRST, preferred_element_type=F32)
        scale = scales[j]
        slopes = jnp.where(wide < 64, key_slope, query_slope * HEAD_DIM ** (-0.5)) * scale
        spread = column[j] * slope_buf[pl.ds(j, 1), :]
        terms = jnp.concatenate([slopes, spread], axis=1)
        terms_buf[pl.ds(pl.multiple_of(j * PATCHES, PATCHES), PATCHES), :] = terms.astype(BF16)
        return terms

    total_buf[...] = jnp.zeros((PATCHES, 256), F32)

    def backwards(i):
        total_buf[...] += backward(2 * i) + backward(2 * i + 1)

    each(0, HEADS // 2, backwards)

    factor_send[0:64, :] = jnp.dot(
        tokens_t[...], terms_buf[...], preferred_element_type=F32
    ).astype(BF16)
    factor_send[64:320, :] = total_buf[...].astype(BF16)
    factors = copy(factor_send, factor_recv, core_sems.at[2], core_sems.at[3], other, vol)
    factors.start()
    factors.wait_recv()
    side.wait_recv()
    factor_sum[0:320, :] = (
        factor_send[...].astype(F32) + factor_recv[...].astype(F32)
    ).astype(BF16)
    factor_sum[320:384, :] = jnp.zeros((64, 256), BF16)
    sides = side_send[...] + side_recv[...]
    pooled_t = sides[:, 0:width]
    outer = sides[:, width : width + HEAD_DIM]

    value_t = lax.dot_general(
        factor_sum[:, 128:256], basis[...], FIRST, preferred_element_type=F32
    )[0:8]
    fill = [jnp.zeros((HEADS, 64 - rows), F32)] if rows < 64 else []
    for d in range(dps):
        part = slice(d * rows, (d + 1) * rows)
        top = jnp.concatenate([value_t[:, part]] + fill + [outer], axis=1)
        low = jnp.concatenate([mixed, pooled_t[:, part]] + fill, axis=1)
        tile_send[d] = jnp.where(row < 4, top, pltpu.roll(low, 4, 0))

    def tile_copy(k, slot):
        e = (me + k) % count
        d = e // vols * 2 + core
        return copy(
            tile_send.at[d],
            tile_recv.at[slot],
            tile_sems.at[0, k],
            tile_sems.at[1, slot],
            d,
            e % vols,
        )

    def grad_copy(k, slot):
        e = (me + k) % count
        d = e // vols * 2 + core
        return copy(
            grad_send.at[d],
            grad_recv.at[slot],
            grad_sems.at[0, k],
            grad_sems.at[1, slot],
            d,
            e % vols,
        )

    each(count // 2, count, lambda k: tile_copy(k, me).start())
    each(1, count // 2, lambda k: tile_copy(k, me).start())
    grad_send[...] = (
        jnp.dot(basis_t[...], factor_sum[:, 0:128], preferred_element_type=F32)
        .astype(BF16)
        .reshape(dps, rows, 128)
    )
    each(count // 2, count, lambda k: grad_copy(k, me).start())
    each(1, count // 2, lambda k: grad_copy(k, me).start())
    grad_recv[me] = grad_send[dp]
    tile_recv[me] = tile_send[dp]

    each(1, count, lambda k: tile_copy(k, (me + count - k) % count).wait_recv())

    outers = []
    for h in range(HEADS):
        senders = senders_of(dps, vols, h)
        tile = tile_recv[senders[0]]
        for s in senders[1:]:
            tile = tile + tile_recv[s]
        outers.append(tile[:, 64:128])
    pooled_sum = pltpu.roll(jnp.sum(tile_recv[...], axis=0), 4, 0)
    branch = lax.dot_general(
        jnp.concatenate(outers, axis=1),
        project_out[...].astype(F32),
        LAST,
        precision=HIGHEST,
        preferred_element_type=F32,
    )
    fill = [jnp.zeros((HEADS, 64 - rows), F32)] if rows < 64 else []
    pooled_sum = pooled_sum + jnp.concatenate(
        [jnp.zeros((HEADS, 64), F32), branch] + fill, axis=1
    )
    head_send[...] = pooled_sum

    def head_copy(k, slot):
        to = (chip + k) % chips
        return copy(
            head_send,
            head_out.at[core, slot],
            head_sems.at[0, k],
            head_sems.at[1, slot],
            to * 2 + core,
            vol,
        )

    each(1, chips, lambda k: head_copy(k, chip).start())
    head_out[core, chip] = pooled_sum

    for h in range(HEADS):
        senders = senders_of(dps, vols, h)
        tile = tile_recv[senders[0]]
        mixed_h = jnp.where(row < 4, pltpu.roll(tile, 4, 0), 0.0)[:, 0:64]
        for s in senders[1:]:
            tile = tile + tile_recv[s]
        tile = jnp.where(row < 4, tile, 0.0)
        value_out[:, h * 64 : h * 64 + 64] = (
            lax.dot_general(
                tile[:, 0:rows], mixed_h, FIRST, precision=HIGHEST, preferred_element_type=F32
            )
            / PATCHES
        )
        value_out[:, 512 + h * 64 : 576 + h * 64] = jnp.dot(
            head_own, tile[:, 64:128], precision=HIGHEST, preferred_element_type=F32
        )

    each(1, chips, lambda k: head_copy(k, (chip + chips - k) % chips).wait_recv())
    heads = copy(
        head_out.at[core], head_out.at[core], core_sems.at[4], core_sems.at[5], other, vol
    )
    heads.start()

    each(1, count, lambda k: grad_copy(k, (me + count - k) % count).wait_recv())
    copy(
        head_out.at[1 - core], head_out.at[1 - core], core_sems.at[4], core_sems.at[5], other, vol
    ).wait_recv()

    each(1, HEADS, lambda k: patch_copy(k, head).wait_send())
    each(1, chips, lambda k: weight_copy(k, dp).wait_send())
    each(0, chips, lambda at: weight_relay(at).wait_send())
    each(1, vols, lambda k: line_copy(k, vol).wait_send())
    each(1, HEADS, lambda k: small_copy(k, head).wait_send())
    side.wait_send()
    factors.wait_send()
    each(1, count, lambda k: tile_copy(k, me).wait_send())
    each(1, count, lambda k: grad_copy(k, me).wait_send())
    each(1, chips, lambda k: head_copy(k, chip).wait_send())
    heads.wait_send()


def senders_of(dps, vols, h):
    return [
        (z * 4 + h // 2) * vols + v * 2 + h % 2 for z in range(dps // 8) for v in range(vols // 2)
    ]


def finish(dps, vols, errors, grads, values, heads, errors_out, in_out, out_out, head_out):
    rows = values.shape[0]
    for h in range(HEADS):
        senders = senders_of(dps, vols, h)
        both = grads[senders[0]].astype(F32)
        for s in senders[1:]:
            both = both + grads[s].astype(F32)
        in_out[:, h * 64 : h * 64 + 64] = both[:, 64:128]
        in_out[:, 512 + h * 64 : 576 + h * 64] = both[:, 0:64]
    in_out[:, 1024:1536] = values[:, 0:512]
    out_out[...] = values[:, 512:1024]
    errors_out[...] = errors[0:1, 0:K]
    for d in range(dps):
        head_out[:, d * rows : (d + 1) * rows] = heads[d % 2, d // 2][0:K, 64 : 64 + rows]


def constants():
    freq = np.arange(PIX) - PIX // 2
    phase = (freq[:, None] * np.arange(PIX)[None, :] % PIX) * (2.0 * math.pi / PIX)
    cosine, sine = np.cos(phase), np.sin(phase)
    waves = np.stack([cosine, sine, (cosine + sine).T, (cosine - sine).T]).astype(np.float32)
    sel = np.zeros((2 * PIX, PIX), np.float32)
    sel[2 * np.arange(PIX), np.arange(PIX)] = 1.0
    places = np.zeros((PATCH, PIX, PIX), np.float32)
    for r in range(PATCH):
        places[r, np.arange(PIX), r * PATCH + np.arange(PIX) % PATCH] = 1.0
    return waves, sel, places


def local(
    dps,
    vols,
    images,
    contrast,
    volume,
    line_index,
    patch_weight,
    position,
    norm_gain,
    project_in,
    project_out,
    head_weight,
):
    width = norm_gain.shape[0]
    rows = project_in.shape[0]
    chips = dps // 2
    count = chips * vols
    waves, sel, places = constants()
    slab, side, _ = volume.shape
    vmem = pl.BlockSpec(memory_space=pltpu.VMEM)
    hbm = pl.BlockSpec(memory_space=pltpu.HBM)
    inputs = (
        images,
        contrast,
        patch_weight,
        position,
        norm_gain.reshape(1, width),
        project_in,
        project_out,
        head_weight.T,
        jnp.asarray(waves),
        jnp.asarray(sel, BF16),
        jnp.asarray(places, BF16),
    )
    errors, grads, values, heads = pl.pallas_call(
        functools.partial(step, dps, vols),
        out_shape=(
            jax.ShapeDtypeStruct((8, 128), F32),
            jax.ShapeDtypeStruct((count, rows, 128), BF16),
            jax.ShapeDtypeStruct((rows, 1024), F32),
            jax.ShapeDtypeStruct((2, chips, 8, 128), F32),
        ),
        in_specs=[pl.BlockSpec(memory_space=pltpu.SMEM)] + [hbm] * (2 + len(inputs)),
        out_specs=(vmem,) * 4,
        scratch_shapes=[pltpu.VMEM(line_index.shape, jnp.int32)]
        + [pltpu.VMEM(one.shape, one.dtype) for one in inputs]
        + [
            pltpu.VMEM((slab, 16, 16, side), BF16),
            pltpu.VMEM((vols + 1, K * PIX, PIX), BF16),
            pltpu.VMEM((PATCHES // 2, 128), BF16),
            pltpu.VMEM((4, rows + rows // 2 + 16, 128), BF16),
            pltpu.VMEM((128, 8), F32),
            pltpu.VMEM((vols, K * PIX, PIX), BF16),
            pltpu.VMEM((HEADS, PATCHES // 2, 128), BF16),
            pltpu.VMEM((dps, rows + rows // 2 + 16, 128), BF16),
            pltpu.VMEM((384, width), BF16),
            pltpu.VMEM((width, 384), BF16),
            pltpu.VMEM((320, 64), F32),
            pltpu.VMEM((PATCHES, 1), F32),
            pltpu.VMEM((HEADS, PATCHES, 64), BF16),
            pltpu.VMEM((64, HEADS * PATCHES), BF16),
            pltpu.VMEM((HEADS, PATCHES, 128), F32),
            pltpu.VMEM((HEADS, PATCHES, PATCHES), BF16),
            pltpu.VMEM((HEADS, PATCHES, 256), BF16),
            pltpu.VMEM((HEADS, PATCHES, 128), F32),
            pltpu.VMEM((HEADS, 128), F32),
            pltpu.VMEM((HEADS, 128), F32),
            pltpu.VMEM((HEADS, HEADS, 128), F32),
            pltpu.VMEM((HEADS, 128), F32),
            pltpu.VMEM((HEADS, 128), F32),
            pltpu.VMEM((HEADS * PATCHES, 256), BF16),
            pltpu.VMEM((PATCHES, 256), F32),
            pltpu.VMEM((320, 256), BF16),
            pltpu.VMEM((320, 256), BF16),
            pltpu.VMEM((384, 256), BF16),
            pltpu.VMEM((8, width + 128), F32),
            pltpu.VMEM((8, width + 128), F32),
            pltpu.VMEM((dps, rows, 128), BF16),
            pltpu.VMEM((dps, 8, 128), F32),
            pltpu.VMEM((count, 8, 128), F32),
            pltpu.VMEM((8, 128), F32),
            pltpu.SemaphoreType.DMA((13,)),
            pltpu.SemaphoreType.DMA((2, vols)),
            pltpu.SemaphoreType.DMA((2, HEADS)),
            pltpu.SemaphoreType.DMA((2, dps)),
            pltpu.SemaphoreType.DMA((chips,)),
            pltpu.SemaphoreType.DMA((2, HEADS)),
            pltpu.SemaphoreType.DMA((6,)),
            pltpu.SemaphoreType.DMA((2, count)),
            pltpu.SemaphoreType.DMA((2, count)),
            pltpu.SemaphoreType.DMA((2, chips)),
        ],
        compiler_params=pltpu.CompilerParams(
            collective_id=0, has_side_effects=True, vmem_limit_bytes=56 * 1024 * 1024
        ),
        name="pose_step",
    )(line_index, line_index, volume.reshape(slab, side // 16, 16, side), *inputs)
    errors, in_grad, out_grad, head_grad = pl.pallas_call(
        functools.partial(finish, dps, vols),
        out_shape=(
            jax.ShapeDtypeStruct((1, K), F32),
            jax.ShapeDtypeStruct((rows, 3 * HEADS * HEAD_DIM), F32),
            jax.ShapeDtypeStruct((rows, HEADS * HEAD_DIM), F32),
            jax.ShapeDtypeStruct((K, width), F32),
        ),
        in_specs=[vmem] * 4,
        out_specs=(vmem,) * 4,
        name="finish",
    )(errors, grads, values, heads)
    return errors, in_grad, out_grad, head_grad.T


def solution(mesh):
    placed = (
        P(("dp", "vol"), None, None),
        P(("dp", "vol"), None, None),
        P("vol", None, None),
        P("dp", None, None),
        P(),
        P(),
        P(),
        P("dp", None),
        P("dp", None),
        P(),
    )
    return jax.shard_map(
        functools.partial(local, mesh.shape["dp"], mesh.shape["vol"]),
        mesh=mesh,
        in_specs=placed,
        out_specs=(P(("dp", "vol"), None), P("dp", None), P("dp", None), P()),
        check_vma=False,
    )
```

```python
import functools
import math

import jax
import jax.numpy as jnp
import numpy as np
from jax import lax
from jax.experimental import pallas as pl
from jax.experimental.pallas import tpu as pltpu
from jax.sharding import PartitionSpec as P

HEADS = 8
HEAD_DIM = 64
PIX = 128
PATCH = 8
PATCHES = 256
K = 4
EPSILON = 1e-05
F32 = jnp.float32
BF16 = jnp.bfloat16
HIGHEST = lax.Precision.HIGHEST
FIRST = (((0,), (0,)), ((), ()))
LAST = (((1,), (1,)), ((), ()))
MESH = pl.DeviceIdType.MESH


def step(
    dps,
    vols,
    spots,
    index_hbm,
    volume,
    image_hbm,
    contrast_hbm,
    patch_weight_hbm,
    position_hbm,
    gain_hbm,
    project_in_hbm,
    project_out_hbm,
    head_hbm,
    waves_hbm,
    sel_hbm,
    places_hbm,
    errors_out,
    grad_recv,
    value_out,
    head_out,
    index,
    image,
    contrast,
    patch_weight,
    position,
    gain,
    project_in,
    project_out,
    head_weight,
    waves,
    sel,
    places,
    slab_buf,
    picked,
    patches,
    pieces,
    head_wide,
    lines,
    patch_buf,
    weight,
    basis,
    basis_t,
    gram,
    square,
    tokens,
    tokens_t,
    scales,
    attention,
    triple,
    column,
    mean_att,
    small_send,
    small_recv,
    pulled_buf,
    slope_buf,
    terms_buf,
    total_buf,
    factor_send,
    factor_recv,
    factor_sum,
    side_send,
    side_recv,
    grad_send,
    tile_send,
    tile_recv,
    head_send,
    in_sems,
    line_sems,
    patch_sems,
    weight_sems,
    relay_sems,
    small_sems,
    core_sems,
    grad_sems,
    tile_sems,
    head_sems,
):
    dp = lax.axis_index("dp")
    vol = lax.axis_index("vol")
    core = dp % 2
    chip = dp // 2
    chips = dps // 2
    count = chips * vols
    me = chip * vols + vol
    pair = vol % 2
    head = (chip % 4) * 2 + pair
    rows = project_in.shape[0]
    width = gain.shape[1]
    slab = volume.shape[0]

    def copy(src, dst, send_sem, recv_sem, to_dp, to_vol):
        return pltpu.make_async_remote_copy(
            src_ref=src,
            dst_ref=dst,
            send_sem=send_sem,
            recv_sem=recv_sem,
            device_id=(to_dp, to_vol),
            device_id_type=MESH,
        )

    def each(first, last, body):
        def run(k, c):
            body(k)
            return c

        lax.fori_loop(first, last, run, 0)

    other = dp + 1 - 2 * core
    barrier = pltpu.get_barrier_semaphore()

    def greet(k):
        e = (me + k) % count
        pl.semaphore_signal(
            barrier, inc=1, device_id=(e // vols * 2 + core, e % vols), device_id_type=MESH
        )

    each(1, count, greet)
    pl.semaphore_signal(barrier, inc=1, device_id=(other, vol), device_id_type=MESH)

    loads = {}
    for name, src, dst in (
        ("image", image_hbm, image),
        ("places", places_hbm, places),
        ("project_in", project_in_hbm, project_in),
        ("project_out", project_out_hbm, project_out),
        ("index", index_hbm, index),
        ("sel", sel_hbm, sel),
        ("waves", waves_hbm, waves),
        ("patch_weight", patch_weight_hbm, patch_weight),
        ("position", position_hbm, position),
        ("gain", gain_hbm, gain),
        ("head", head_hbm, head_weight),
        ("contrast", contrast_hbm, contrast),
        ("volume", volume, slab_buf),
    ):
        loads[name] = pltpu.make_async_copy(src, dst, in_sems.at[len(loads)])
        loads[name].start()

    loads["project_in"].wait()
    loads["project_out"].wait()
    loads["head"].wait()
    near = pl.ds(pl.multiple_of(dp * rows // 128 * 128, 128), 128)
    head_wide[...] = jnp.concatenate(
        [head_weight[:, near], jnp.zeros((4, 128), F32)], axis=0
    ).T
    head_own = head_wide[pl.ds(pl.multiple_of(dp * rows % 128, rows), rows), :]
    share = lax.dot_general(
        head_own,
        project_out[...].astype(F32),
        FIRST,
        precision=HIGHEST,
        preferred_element_type=F32,
    )
    for a in range(4):
        parts = [project_in[:, p * 512 + a * 128 : p * 512 + a * 128 + 128] for p in range(3)]
        parts.append(share[:, a * 128 : a * 128 + 128])
        query, key, value, mix = [
            jnp.where(pair == 0, one[:, 0:64], one[:, 64:128]) for one in parts
        ]
        high = mix.astype(BF16)
        mix = jnp.concatenate([high.astype(F32), mix - high.astype(F32)], axis=1)
        pieces[a, 0:rows, :] = jnp.concatenate([query, key], axis=1)
        pieces[a, rows : rows + rows // 2, :] = jnp.concatenate(
            [value[0 : rows // 2], value[rows // 2 : rows]], axis=1
        )
        pieces[a, rows + rows // 2 :, :] = jnp.concatenate(
            [mix, jnp.zeros((8, 128), F32)], axis=0
        ).astype(BF16)
    weight[dp] = pieces[chip % 4]
    loads["image"].wait()
    loads["places"].wait()
    cells = lax.broadcasted_iota(jnp.int32, (16, 16, 128), 1)
    spread_lane = lax.broadcasted_iota(jnp.int32, (16, 16, 128), 2)
    cut = jnp.zeros((PATCHES, 128), F32)
    for r in range(PATCH):
        stripe = image[0, pl.ds(r, 16, stride=PATCH), :]
        stripe = jnp.broadcast_to(stripe[:, None, :], (16, 16, 128))
        stripe = jnp.where(spread_lane // PATCH == cells, stripe, 0.0).reshape(PATCHES, 128)
        cut = cut + jnp.dot(stripe.astype(BF16), places[r], preferred_element_type=F32)
    patches[...] = jnp.concatenate([cut[0:128, 0:64], cut[128:256, 0:64]], axis=1).astype(BF16)
    patch_mean = jnp.sum(cut[:, 0:64], axis=0, keepdims=True) / PATCHES
    loads["patch_weight"].wait()
    loads["position"].wait()
    loads["gain"].wait()
    embed = patch_weight[...].astype(F32)
    embed_c = embed - jnp.mean(embed, axis=1, keepdims=True)
    basis[0:64, :] = (embed_c * gain[...]).astype(BF16)
    gram[0:64, :] = lax.dot_general(
        embed_c, embed_c, LAST, precision=HIGHEST, preferred_element_type=F32
    )
    place_mean = jnp.zeros((1, width), F32)
    for part in range(4):
        one = position[part * 64 : part * 64 + 64, :].astype(F32)
        place_mean = place_mean + jnp.sum(one, axis=0, keepdims=True)
        one = one - jnp.mean(one, axis=1, keepdims=True)
        basis[64 + part * 64 : 128 + part * 64, :] = (one * gain[...]).astype(BF16)
        gram[64 + part * 64 : 128 + part * 64, :] = lax.dot_general(
            one, embed_c, LAST, precision=HIGHEST, preferred_element_type=F32
        )
        square[part * 64 : part * 64 + 64, :] = jnp.sum(one * one, axis=1, keepdims=True)
    basis[320:384, :] = jnp.zeros((64, width), BF16)
    basis_t[...] = basis[...].T
    own_row = (
        jnp.dot(
            jnp.broadcast_to(patch_mean, (8, 64)),
            embed,
            precision=HIGHEST,
            preferred_element_type=F32,
        )
        + place_mean / PATCHES
    )

    head_t = jnp.concatenate([head_weight[...], jnp.zeros((4, width), F32)], axis=0)
    own_logit = lax.dot_general(
        own_row, head_t, LAST, precision=HIGHEST, preferred_element_type=F32
    )
    row = lax.broadcasted_iota(jnp.int32, (HEADS, 128), 0)
    lane = lax.broadcasted_iota(jnp.int32, (HEADS, 128), 1)
    mine = row == head
    own_logit = jnp.where(mine[:, 0:HEADS], own_logit, 0.0)

    loads["waves"].wait()
    pixels = image[0]
    first_cos = jnp.dot(waves[0], pixels, precision=HIGHEST, preferred_element_type=F32)
    first_sin = jnp.dot(waves[1], pixels, precision=HIGHEST, preferred_element_type=F32)
    spectrum = jnp.dot(first_cos, waves[2], precision=HIGHEST, preferred_element_type=F32)
    spectrum = spectrum + jnp.dot(
        first_sin, waves[3], precision=HIGHEST, preferred_element_type=F32
    )
    spectrum = spectrum / PIX

    pl.semaphore_wait(barrier, count)

    def member(m):
        return chip // 4 * 8 + m // 2 * 2 + core, vol // 2 * 2 + m % 2

    def patch_copy(k, slot):
        to_dp, to_vol = member((head + k) % HEADS)
        return copy(
            patches,
            patch_buf.at[slot],
            patch_sems.at[0, k],
            patch_sems.at[1, slot],
            to_dp,
            to_vol,
        )

    def weight_copy(k, slot):
        to = (chip + k) % chips
        return copy(
            pieces.at[to % 4],
            weight.at[slot],
            weight_sems.at[0, k],
            weight_sems.at[1, slot],
            to * 2 + core,
            vol,
        )

    def weight_relay(at):
        s = at * 2 + core
        return copy(
            weight.at[s], weight.at[s], relay_sems.at[at], weight_sems.at[1, s], other, vol
        )

    def line_copy(k, slot):
        to = (vol + k) % vols
        return copy(picked.at[k], lines.at[slot], line_sems.at[0, k], line_sems.at[1, slot], dp, to)

    each(chips // 2, chips, lambda k: weight_copy(k, dp).start())
    each(1, chips // 2, lambda k: weight_copy(k, dp).start())
    each(1, HEADS, lambda k: patch_copy(k, head).start())
    weight_relay(chip).start()
    patch_buf[head] = patches[...]

    loads["index"].wait()
    loads["sel"].wait()
    loads["volume"].wait()

    def render(step_k, c):
        k = step_k + 1
        v = (vol + k) % vols
        turned = jnp.concatenate([index[v], jnp.zeros((4, 128), jnp.int32)], axis=0)
        turned = turned.astype(F32).T.astype(jnp.int32)
        spot_lane = lax.broadcasted_iota(jnp.int32, (128, 256), 1)
        spot_row = lax.broadcasted_iota(jnp.int32, (128, 256), 0)
        for hyp in range(K):
            line = turned[:, hyp : hyp + 1]
            level = (line >> 4) - vol * slab
            target = jnp.where((level >= 0) & (level < slab), line & 15, 1024)
            hot = jnp.where(spot_lane == (spot_row % 16) * 16 + target, 1.0, 0.0).astype(BF16)
            found = []
            for group in range(8):
                tiles = []
                for i in range(16):
                    spot = spots[v, hyp, group * 16 + i]
                    tiles.append(slab_buf[(spot >> 4) & (slab - 1)])
                tiles = jnp.concatenate(tiles, axis=0)
                found.append(
                    jnp.dot(
                        hot[group * 16 : group * 16 + 16], tiles, preferred_element_type=F32
                    )
                )
            found = jnp.concatenate(found, axis=0).astype(BF16)
            picked[k, hyp * PIX : (hyp + 1) * PIX, :] = jnp.dot(
                found, sel[...], preferred_element_type=F32
            ).astype(BF16)
        @pl.when(k < vols)
        def _():
            line_copy(k, vol).start()

        return c

    lax.fori_loop(0, vols, render, 0)
    lines[vol] = picked[vols]

    def weight_pass(k):
        at = (chip + chips - k) % chips
        weight_copy(k, at * 2 + core).wait_recv()
        weight_relay(at).start()

    each(1, chips // 2, weight_pass)

    first = lax.broadcasted_iota(jnp.int32, (PATCHES // 2, 128), 1) < 64
    high = gram[0:64].astype(BF16)
    gram_parts = jnp.concatenate([high.astype(F32), gram[0:64] - high.astype(F32)], axis=1)
    gram_parts = jnp.concatenate([gram_parts, jnp.zeros((64, 128), F32)], axis=0).astype(BF16)
    gram_places = jnp.concatenate([2.0 * gram[64:320], jnp.zeros((PATCHES, 64), F32)], axis=1)

    def norms(k, c):
        j = (head + HEADS - k) % HEADS

        @pl.when(k > 0)
        def _():
            patch_copy(k, j).wait_recv()

        both = patch_buf[j].astype(F32)
        turned = pltpu.roll(both, 64, 1)
        both = jnp.concatenate(
            [jnp.where(first, both, turned), jnp.where(first, turned, both)], axis=0
        )
        one = both.astype(BF16)
        tokens[j] = one
        tokens_t[:, pl.ds(pl.multiple_of(j * PATCHES, PATCHES), PATCHES)] = one.T[0:64]
        total = jnp.dot(one, gram_parts, preferred_element_type=F32) + gram_places
        total = jnp.sum(both * total, axis=1, keepdims=True)
        total = jnp.maximum(total + square[...], 0.0) / width
        scales[j] = jnp.broadcast_to(lax.rsqrt(total + EPSILON), (PATCHES, 128))
        return c

    each(chips // 2, chips, weight_pass)
    lax.fori_loop(0, HEADS, norms, 0)

    def weight_rest(k):
        s = (chip + chips - k) % chips * 2 + 1 - core
        weight_copy(0, s).wait_recv()

    each(0, chips, weight_rest)

    sides = weight[:, 0:rows, :].reshape(width, 128)
    value = weight[:, rows : rows + rows // 2, :]
    value = jnp.concatenate([value[:, :, 0:64], value[:, :, 64:128]], axis=1)
    half = jnp.where(lax.broadcasted_iota(jnp.int32, (1, 128), 1) < 64, HEAD_DIM ** (-0.5), 1.0)
    sides = jnp.dot(basis[0:320], sides, preferred_element_type=F32) * half
    value = jnp.dot(
        basis[0:320], value.reshape(width, HEAD_DIM), preferred_element_type=F32
    )
    both = jnp.concatenate([sides, value, jnp.zeros((320, 64), F32)], axis=1)
    total_buf[...] = both[64:320]
    turn = jnp.concatenate([both[0:64], jnp.zeros((64, 256), F32)], axis=0).astype(BF16)
    mixed = jnp.sum(weight[:, rows + rows // 2 :, :].astype(F32), axis=0)[0:8]
    mixed = mixed[:, 0:64] + mixed[:, 64:128]

    ones = jnp.ones((PATCHES, 128), BF16)

    def forward(j):
        scale = scales[j]
        t = jnp.dot(tokens[j], turn, preferred_element_type=F32) + total_buf[...]
        t = (t * jnp.concatenate([scale, scale], axis=1)).astype(BF16)
        triple[j] = t
        scores = lax.dot_general(t[:, 64:128], t[:, 0:64], LAST, preferred_element_type=F32)
        raised = jnp.exp(scores)
        chosen = (raised * (1.0 / jnp.sum(raised, axis=0, keepdims=True))).astype(BF16)
        attention[j] = chosen
        col = jnp.sum(chosen.astype(F32), axis=1, keepdims=True)
        column[j] = col * scale
        mean_att[pl.ds(j, 1), :] = (
            jnp.sum(col * t[:, 128:256].astype(F32), axis=0, keepdims=True) / PATCHES
        )

    def forwards(i):
        forward(2 * i)
        forward(2 * i + 1)

    each(0, HEADS // 2, forwards)

    loads["contrast"].wait()
    each(1, vols, lambda k: line_copy(k, (vol + vols - k) % vols).wait_recv())
    slices = lines[0].astype(F32)
    for v in range(1, vols):
        slices = slices + lines[v].astype(F32)
    filt = contrast[0].astype(F32)
    misfits = jnp.zeros((HEADS, 128), F32)
    for k in range(K):
        misfit = filt * slices[k * PIX : (k + 1) * PIX] - spectrum
        value = jnp.sum(jnp.sum(misfit * misfit, axis=0, keepdims=True), axis=1, keepdims=True)
        misfits = jnp.where(lane == k, value / (PIX * PIX), misfits)
    errors_out[...] = misfits
    misfits = jnp.where(mine, pltpu.roll(misfits, 4, 1), 0.0)
    means = mean_att[:, 0:HEAD_DIM]
    logit = own_logit + lax.dot_general(
        means, mixed, LAST, precision=HIGHEST, preferred_element_type=F32
    )
    logit = jnp.where(
        lane < K, jnp.concatenate([logit, jnp.zeros((HEADS, 120), F32)], axis=1), misfits
    )
    small_send[...] = logit

    def small_copy(k, slot):
        to_dp, to_vol = member((head + k) % HEADS)
        return copy(
            small_send,
            small_recv.at[slot],
            small_sems.at[0, k],
            small_sems.at[1, slot],
            to_dp,
            to_vol,
        )

    each(1, HEADS, lambda k: small_copy(k, head).start())
    small_recv[head] = small_send[...]
    each(1, HEADS, lambda k: small_copy(k, (head + HEADS - k) % HEADS).wait_recv())
    summed = jnp.sum(small_recv[...], axis=0)
    misfits = jnp.where(lane < K, pltpu.roll(summed, 124, 1), 0.0)
    raised = jnp.where(lane < K, jnp.exp(summed), 0.0)
    chances = raised / jnp.sum(raised, axis=1, keepdims=True)
    expected = jnp.sum(chances * misfits, axis=1, keepdims=True)
    slope = chances * (misfits - expected)
    pulled = jnp.zeros((HEADS, HEAD_DIM), F32)
    for k in range(K):
        pulled = pulled + slope[:, k : k + 1] * mixed[k : k + 1, :]
    pulled_buf[...] = jnp.concatenate(
        [pulled / PATCHES, jnp.zeros((HEADS, 128 - HEAD_DIM), F32)], axis=1
    )
    slope_buf[...] = slope

    slope_t = slope.T[0:8]
    outer = jnp.zeros((HEADS, 128), F32)
    for j in range(HEADS):
        outer = outer + slope_t[:, j : j + 1] * mean_att[j : j + 1, :]
    own = jnp.sum(jnp.where(lane[:, 0:HEADS] == head, slope_t, 0.0), axis=1, keepdims=True)
    side_send[:, 0:width] = own * own_row
    side_send[:, width:] = outer
    side = copy(side_send, side_recv, core_sems.at[0], core_sems.at[1], other, vol)
    side.start()

    wide = lax.broadcasted_iota(jnp.int32, (PATCHES, 128), 1)

    def backward(j):
        t = triple[j]
        chosen = attention[j]
        wider = chosen.astype(F32)
        up = jnp.sum(
            t[:, 128:256].astype(F32) * pulled_buf[pl.ds(j, 1), :], axis=1, keepdims=True
        )
        center = jnp.sum(wider * up, axis=0, keepdims=True)
        inner = (wider * (up - center)).astype(BF16)
        sides = t[:, 0:128]
        key_slope = jnp.dot(inner, sides, preferred_element_type=F32)
        query_slope = lax.dot_general(inner, sides, FIRST, preferred_element_type=F32)
        scale = scales[j]
        slopes = jnp.where(wide < 64, key_slope, query_slope * HEAD_DIM ** (-0.5)) * scale
        spread = column[j] * slope_buf[pl.ds(j, 1), :]
        terms = jnp.concatenate([slopes, spread], axis=1)
        terms_buf[pl.ds(pl.multiple_of(j * PATCHES, PATCHES), PATCHES), :] = terms.astype(BF16)
        return terms

    total_buf[...] = jnp.zeros((PATCHES, 256), F32)

    def backwards(i):
        total_buf[...] += backward(2 * i) + backward(2 * i + 1)

    each(0, HEADS // 2, backwards)

    factor_send[0:64, :] = jnp.dot(
        tokens_t[...], terms_buf[...], preferred_element_type=F32
    ).astype(BF16)
    factor_send[64:320, :] = total_buf[...].astype(BF16)
    factors = copy(factor_send, factor_recv, core_sems.at[2], core_sems.at[3], other, vol)
    factors.start()
    factors.wait_recv()
    side.wait_recv()
    factor_sum[0:320, :] = (
        factor_send[...].astype(F32) + factor_recv[...].astype(F32)
    ).astype(BF16)
    factor_sum[320:384, :] = jnp.zeros((64, 256), BF16)
    sides = side_send[...] + side_recv[...]
    pooled_t = sides[:, 0:width]
    outer = sides[:, width : width + HEAD_DIM]

    value_t = lax.dot_general(
        factor_sum[:, 128:256], basis[...], FIRST, preferred_element_type=F32
    )[0:8]
    fill = [jnp.zeros((HEADS, 64 - rows), F32)] if rows < 64 else []
    for d in range(dps):
        part = slice(d * rows, (d + 1) * rows)
        top = jnp.concatenate([value_t[:, part]] + fill + [outer], axis=1)
        low = jnp.concatenate([mixed, pooled_t[:, part]] + fill, axis=1)
        tile_send[d] = jnp.where(row < 4, top, pltpu.roll(low, 4, 0))

    def tile_copy(k, slot):
        e = (me + k) % count
        d = e // vols * 2 + core
        return copy(
            tile_send.at[d],
            tile_recv.at[slot],
            tile_sems.at[0, k],
            tile_sems.at[1, slot],
            d,
            e % vols,
        )

    def grad_copy(k, slot):
        e = (me + k) % count
        d = e // vols * 2 + core
        return copy(
            grad_send.at[d],
            grad_recv.at[slot],
            grad_sems.at[0, k],
            grad_sems.at[1, slot],
            d,
            e % vols,
        )

    each(count // 2, count, lambda k: tile_copy(k, me).start())
    each(1, count // 2, lambda k: tile_copy(k, me).start())
    grad_send[...] = (
        jnp.dot(basis_t[...], factor_sum[:, 0:128], preferred_element_type=F32)
        .astype(BF16)
        .reshape(dps, rows, 128)
    )
    each(count // 2, count, lambda k: grad_copy(k, me).start())
    each(1, count // 2, lambda k: grad_copy(k, me).start())
    grad_recv[me] = grad_send[dp]
    tile_recv[me] = tile_send[dp]

    each(1, count, lambda k: tile_copy(k, (me + count - k) % count).wait_recv())

    outers = []
    for h in range(HEADS):
        senders = senders_of(dps, vols, h)
        tile = tile_recv[senders[0]]
        for s in senders[1:]:
            tile = tile + tile_recv[s]
        outers.append(tile[:, 64:128])
    pooled_sum = pltpu.roll(jnp.sum(tile_recv[...], axis=0), 4, 0)
    branch = lax.dot_general(
        jnp.concatenate(outers, axis=1),
        project_out[...].astype(F32),
        LAST,
        precision=HIGHEST,
        preferred_element_type=F32,
    )
    fill = [jnp.zeros((HEADS, 64 - rows), F32)] if rows < 64 else []
    pooled_sum = pooled_sum + jnp.concatenate(
        [jnp.zeros((HEADS, 64), F32), branch] + fill, axis=1
    )
    head_send[...] = pooled_sum

    def head_copy(k, slot):
        to = (chip + k) % chips
        return copy(
            head_send,
            head_out.at[core, slot],
            head_sems.at[0, k],
            head_sems.at[1, slot],
            to * 2 + core,
            vol,
        )

    each(1, chips, lambda k: head_copy(k, chip).start())
    head_out[core, chip] = pooled_sum

    for h in range(HEADS):
        senders = senders_of(dps, vols, h)
        tile = tile_recv[senders[0]]
        mixed_h = jnp.where(row < 4, pltpu.roll(tile, 4, 0), 0.0)[:, 0:64]
        for s in senders[1:]:
            tile = tile + tile_recv[s]
        tile = jnp.where(row < 4, tile, 0.0)
        value_out[:, h * 64 : h * 64 + 64] = (
            lax.dot_general(
                tile[:, 0:rows], mixed_h, FIRST, precision=HIGHEST, preferred_element_type=F32
            )
            / PATCHES
        )
        value_out[:, 512 + h * 64 : 576 + h * 64] = jnp.dot(
            head_own, tile[:, 64:128], precision=HIGHEST, preferred_element_type=F32
        )

    each(1, chips, lambda k: head_copy(k, (chip + chips - k) % chips).wait_recv())
    heads = copy(
        head_out.at[core], head_out.at[core], core_sems.at[4], core_sems.at[5], other, vol
    )
    heads.start()

    each(1, count, lambda k: grad_copy(k, (me + count - k) % count).wait_recv())
    copy(
        head_out.at[1 - core], head_out.at[1 - core], core_sems.at[4], core_sems.at[5], other, vol
    ).wait_recv()

    each(1, HEADS, lambda k: patch_copy(k, head).wait_send())
    each(1, chips, lambda k: weight_copy(k, dp).wait_send())
    each(0, chips, lambda at: weight_relay(at).wait_send())
    each(1, vols, lambda k: line_copy(k, vol).wait_send())
    each(1, HEADS, lambda k: small_copy(k, head).wait_send())
    side.wait_send()
    factors.wait_send()
    each(1, count, lambda k: tile_copy(k, me).wait_send())
    each(1, count, lambda k: grad_copy(k, me).wait_send())
    each(1, chips, lambda k: head_copy(k, chip).wait_send())
    heads.wait_send()


def senders_of(dps, vols, h):
    return [
        (z * 4 + h // 2) * vols + v * 2 + h % 2 for z in range(dps // 8) for v in range(vols // 2)
    ]


def finish(dps, vols, errors, grads, values, heads, errors_out, in_out, out_out, head_out):
    rows = values.shape[0]
    for h in range(HEADS):
        senders = senders_of(dps, vols, h)
        both = grads[senders[0]].astype(F32)
        for s in senders[1:]:
            both = both + grads[s].astype(F32)
        in_out[:, h * 64 : h * 64 + 64] = both[:, 64:128]
        in_out[:, 512 + h * 64 : 576 + h * 64] = both[:, 0:64]
    in_out[:, 1024:1536] = values[:, 0:512]
    out_out[...] = values[:, 512:1024]
    errors_out[...] = errors[0:1, 0:K]
    for d in range(dps):
        head_out[:, d * rows : (d + 1) * rows] = heads[d % 2, d // 2][0:K, 64 : 64 + rows]


def constants():
    freq = np.arange(PIX) - PIX // 2
    phase = (freq[:, None] * np.arange(PIX)[None, :] % PIX) * (2.0 * math.pi / PIX)
    cosine, sine = np.cos(phase), np.sin(phase)
    waves = np.stack([cosine, sine, (cosine + sine).T, (cosine - sine).T]).astype(np.float32)
    sel = np.zeros((2 * PIX, PIX), np.float32)
    sel[2 * np.arange(PIX), np.arange(PIX)] = 1.0
    places = np.zeros((PATCH, PIX, PIX), np.float32)
    for r in range(PATCH):
        places[r, np.arange(PIX), r * PATCH + np.arange(PIX) % PATCH] = 1.0
    return waves, sel, places


def local(
    dps,
    vols,
    images,
    contrast,
    volume,
    line_index,
    patch_weight,
    position,
    norm_gain,
    project_in,
    project_out,
    head_weight,
):
    width = norm_gain.shape[0]
    rows = project_in.shape[0]
    chips = dps // 2
    count = chips * vols
    waves, sel, places = constants()
    slab, side, _ = volume.shape
    vmem = pl.BlockSpec(memory_space=pltpu.VMEM)
    hbm = pl.BlockSpec(memory_space=pltpu.HBM)
    inputs = (
        images,
        contrast,
        patch_weight,
        position,
        norm_gain.reshape(1, width),
        project_in,
        project_out,
        head_weight.T,
        jnp.asarray(waves),
        jnp.asarray(sel, BF16),
        jnp.asarray(places, BF16),
    )
    errors, grads, values, heads = pl.pallas_call(
        functools.partial(step, dps, vols),
        out_shape=(
            jax.ShapeDtypeStruct((8, 128), F32),
            jax.ShapeDtypeStruct((count, rows, 128), BF16),
            jax.ShapeDtypeStruct((rows, 1024), F32),
            jax.ShapeDtypeStruct((2, chips, 8, 128), F32),
        ),
        in_specs=[pl.BlockSpec(memory_space=pltpu.SMEM)] + [hbm] * (2 + len(inputs)),
        out_specs=(vmem,) * 4,
        scratch_shapes=[pltpu.VMEM(line_index.shape, jnp.int32)]
        + [pltpu.VMEM(one.shape, one.dtype) for one in inputs]
        + [
            pltpu.VMEM((slab * (side // 16), 16, side), BF16),
            pltpu.VMEM((vols + 1, K * PIX, PIX), BF16),
            pltpu.VMEM((PATCHES // 2, 128), BF16),
            pltpu.VMEM((4, rows + rows // 2 + 16, 128), BF16),
            pltpu.VMEM((128, 8), F32),
            pltpu.VMEM((vols, K * PIX, PIX), BF16),
            pltpu.VMEM((HEADS, PATCHES // 2, 128), BF16),
            pltpu.VMEM((dps, rows + rows // 2 + 16, 128), BF16),
            pltpu.VMEM((384, width), BF16),
            pltpu.VMEM((width, 384), BF16),
            pltpu.VMEM((320, 64), F32),
            pltpu.VMEM((PATCHES, 1), F32),
            pltpu.VMEM((HEADS, PATCHES, 128), BF16),
            pltpu.VMEM((64, HEADS * PATCHES), BF16),
            pltpu.VMEM((HEADS, PATCHES, 128), F32),
            pltpu.VMEM((HEADS, PATCHES, PATCHES), BF16),
            pltpu.VMEM((HEADS, PATCHES, 256), BF16),
            pltpu.VMEM((HEADS, PATCHES, 128), F32),
            pltpu.VMEM((HEADS, 128), F32),
            pltpu.VMEM((HEADS, 128), F32),
            pltpu.VMEM((HEADS, HEADS, 128), F32),
            pltpu.VMEM((HEADS, 128), F32),
            pltpu.VMEM((HEADS, 128), F32),
            pltpu.VMEM((HEADS * PATCHES, 256), BF16),
            pltpu.VMEM((PATCHES, 256), F32),
            pltpu.VMEM((320, 256), BF16),
            pltpu.VMEM((320, 256), BF16),
            pltpu.VMEM((384, 256), BF16),
            pltpu.VMEM((8, width + 128), F32),
            pltpu.VMEM((8, width + 128), F32),
            pltpu.VMEM((dps, rows, 128), BF16),
            pltpu.VMEM((dps, 8, 128), F32),
            pltpu.VMEM((count, 8, 128), F32),
            pltpu.VMEM((8, 128), F32),
            pltpu.SemaphoreType.DMA((13,)),
            pltpu.SemaphoreType.DMA((2, vols)),
            pltpu.SemaphoreType.DMA((2, HEADS)),
            pltpu.SemaphoreType.DMA((2, dps)),
            pltpu.SemaphoreType.DMA((chips,)),
            pltpu.SemaphoreType.DMA((2, HEADS)),
            pltpu.SemaphoreType.DMA((6,)),
            pltpu.SemaphoreType.DMA((2, count)),
            pltpu.SemaphoreType.DMA((2, count)),
            pltpu.SemaphoreType.DMA((2, chips)),
        ],
        compiler_params=pltpu.CompilerParams(
            collective_id=0, has_side_effects=True, vmem_limit_bytes=56 * 1024 * 1024
        ),
        name="pose_step",
    )(line_index, line_index, volume.reshape(slab * (side // 16), 16, side), *inputs)
    errors, in_grad, out_grad, head_grad = pl.pallas_call(
        functools.partial(finish, dps, vols),
        out_shape=(
            jax.ShapeDtypeStruct((1, K), F32),
            jax.ShapeDtypeStruct((rows, 3 * HEADS * HEAD_DIM), F32),
            jax.ShapeDtypeStruct((rows, HEADS * HEAD_DIM), F32),
            jax.ShapeDtypeStruct((K, width), F32),
        ),
        in_specs=[vmem] * 4,
        out_specs=(vmem,) * 4,
        name="finish",
    )(errors, grads, values, heads)
    return errors, in_grad, out_grad, head_grad.T


def solution(mesh):
    placed = (
        P(("dp", "vol"), None, None),
        P(("dp", "vol"), None, None),
        P("vol", None, None),
        P("dp", None, None),
        P(),
        P(),
        P(),
        P("dp", None),
        P("dp", None),
        P(),
    )
    return jax.shard_map(
        functools.partial(local, mesh.shape["dp"], mesh.shape["vol"]),
        mesh=mesh,
        in_specs=placed,
        out_specs=(P(("dp", "vol"), None), P("dp", None), P("dp", None), P()),
        check_vma=False,
    )
```

```python
import functools
import math

import jax
import jax.numpy as jnp
import numpy as np
from jax import lax
from jax.experimental import pallas as pl
from jax.experimental.pallas import tpu as pltpu
from jax.sharding import PartitionSpec as P

HEADS = 8
HEAD_DIM = 64
PIX = 128
PATCH = 8
PATCHES = 256
K = 4
EPSILON = 1e-05
F32 = jnp.float32
BF16 = jnp.bfloat16
HIGHEST = lax.Precision.HIGHEST
FIRST = (((0,), (0,)), ((), ()))
LAST = (((1,), (1,)), ((), ()))
MESH = pl.DeviceIdType.MESH


def step(
    dps,
    vols,
    index_hbm,
    volume,
    image_hbm,
    contrast_hbm,
    patch_weight_hbm,
    position_hbm,
    gain_hbm,
    project_in_hbm,
    project_out_hbm,
    head_hbm,
    waves_hbm,
    sel_hbm,
    places_hbm,
    errors_out,
    grad_recv,
    value_out,
    head_out,
    spots,
    index,
    image,
    contrast,
    patch_weight,
    position,
    gain,
    project_in,
    project_out,
    head_weight,
    waves,
    sel,
    places,
    slab_buf,
    picked,
    patches,
    pieces,
    head_wide,
    lines,
    patch_buf,
    weight,
    basis,
    basis_t,
    gram,
    square,
    tokens,
    tokens_t,
    scales,
    attention,
    triple,
    column,
    mean_att,
    small_send,
    small_recv,
    pulled_buf,
    slope_buf,
    terms_buf,
    total_buf,
    factor_send,
    factor_recv,
    factor_sum,
    side_send,
    side_recv,
    grad_send,
    tile_send,
    tile_recv,
    head_send,
    in_sems,
    line_sems,
    patch_sems,
    weight_sems,
    relay_sems,
    small_sems,
    core_sems,
    grad_sems,
    tile_sems,
    head_sems,
):
    dp = lax.axis_index("dp")
    vol = lax.axis_index("vol")
    core = dp % 2
    chip = dp // 2
    chips = dps // 2
    count = chips * vols
    me = chip * vols + vol
    pair = vol % 2
    head = (chip % 4) * 2 + pair
    rows = project_in.shape[0]
    width = gain.shape[1]
    slab = volume.shape[0]

    def copy(src, dst, send_sem, recv_sem, to_dp, to_vol):
        return pltpu.make_async_remote_copy(
            src_ref=src,
            dst_ref=dst,
            send_sem=send_sem,
            recv_sem=recv_sem,
            device_id=(to_dp, to_vol),
            device_id_type=MESH,
        )

    def each(first, last, body):
        def run(k, c):
            body(k)
            return c

        lax.fori_loop(first, last, run, 0)

    other = dp + 1 - 2 * core
    barrier = pltpu.get_barrier_semaphore()

    def greet(k):
        e = (me + k) % count
        pl.semaphore_signal(
            barrier, inc=1, device_id=(e // vols * 2 + core, e % vols), device_id_type=MESH
        )

    each(count // 2, count, greet)
    each(1, count // 2, greet)
    pl.semaphore_signal(barrier, inc=1, device_id=(other, vol), device_id_type=MESH)

    loads = {}
    for name, src, dst in (
        ("image", image_hbm, image),
        ("places", places_hbm, places),
        ("project_in", project_in_hbm, project_in),
        ("project_out", project_out_hbm, project_out),
        ("index", index_hbm, index),
        ("spots", index_hbm, spots),
        ("sel", sel_hbm, sel),
        ("waves", waves_hbm, waves),
        ("patch_weight", patch_weight_hbm, patch_weight),
        ("position", position_hbm, position),
        ("gain", gain_hbm, gain),
        ("head", head_hbm, head_weight),
        ("contrast", contrast_hbm, contrast),
        ("volume", volume, slab_buf),
    ):
        loads[name] = pltpu.make_async_copy(src, dst, in_sems.at[len(loads)])
        loads[name].start()

    loads["project_in"].wait()
    loads["project_out"].wait()
    loads["head"].wait()
    near = pl.ds(pl.multiple_of(dp * rows // 128 * 128, 128), 128)
    head_wide[...] = jnp.concatenate(
        [head_weight[:, near], jnp.zeros((4, 128), F32)], axis=0
    ).T
    head_own = head_wide[pl.ds(pl.multiple_of(dp * rows % 128, rows), rows), :]
    share = lax.dot_general(
        head_own,
        project_out[...].astype(F32),
        FIRST,
        precision=HIGHEST,
        preferred_element_type=F32,
    )
    for a in range(4):
        parts = [project_in[:, p * 512 + a * 128 : p * 512 + a * 128 + 128] for p in range(3)]
        parts.append(share[:, a * 128 : a * 128 + 128])
        query, key, value, mix = [
            jnp.where(pair == 0, one[:, 0:64], one[:, 64:128]) for one in parts
        ]
        high = mix.astype(BF16)
        mix = jnp.concatenate([high.astype(F32), mix - high.astype(F32)], axis=1)
        pieces[a, 0:rows, :] = jnp.concatenate([query, key], axis=1)
        pieces[a, rows : rows + rows // 2, :] = jnp.concatenate(
            [value[0 : rows // 2], value[rows // 2 : rows]], axis=1
        )
        pieces[a, rows + rows // 2 :, :] = jnp.concatenate(
            [mix, jnp.zeros((8, 128), F32)], axis=0
        ).astype(BF16)
    weight[dp] = pieces[chip % 4]
    loads["image"].wait()
    loads["places"].wait()
    cells = lax.broadcasted_iota(jnp.int32, (16, 16, 128), 1)
    spread_lane = lax.broadcasted_iota(jnp.int32, (16, 16, 128), 2)
    cut = jnp.zeros((PATCHES, 128), F32)
    for r in range(PATCH):
        stripe = image[0, pl.ds(r, 16, stride=PATCH), :]
        stripe = jnp.broadcast_to(stripe[:, None, :], (16, 16, 128))
        stripe = jnp.where(spread_lane // PATCH == cells, stripe, 0.0).reshape(PATCHES, 128)
        cut = cut + jnp.dot(stripe.astype(BF16), places[r], preferred_element_type=F32)
    patches[...] = jnp.concatenate([cut[0:128, 0:64], cut[128:256, 0:64]], axis=1).astype(BF16)
    patch_mean = jnp.sum(cut[:, 0:64], axis=0, keepdims=True) / PATCHES
    loads["patch_weight"].wait()
    loads["position"].wait()
    loads["gain"].wait()
    embed = patch_weight[...].astype(F32)
    embed_c = embed - jnp.mean(embed, axis=1, keepdims=True)
    basis[0:64, :] = (embed_c * gain[...]).astype(BF16)
    gram[0:64, :] = lax.dot_general(
        embed_c, embed_c, LAST, precision=HIGHEST, preferred_element_type=F32
    )
    place_mean = jnp.zeros((1, width), F32)
    for part in range(4):
        one = position[part * 64 : part * 64 + 64, :].astype(F32)
        place_mean = place_mean + jnp.sum(one, axis=0, keepdims=True)
        one = one - jnp.mean(one, axis=1, keepdims=True)
        basis[64 + part * 64 : 128 + part * 64, :] = (one * gain[...]).astype(BF16)
        gram[64 + part * 64 : 128 + part * 64, :] = lax.dot_general(
            one, embed_c, LAST, precision=HIGHEST, preferred_element_type=F32
        )
        square[part * 64 : part * 64 + 64, :] = jnp.sum(one * one, axis=1, keepdims=True)
    basis[320:384, :] = jnp.zeros((64, width), BF16)
    basis_t[...] = basis[...].T
    own_row = (
        jnp.dot(
            jnp.broadcast_to(patch_mean, (8, 64)),
            embed,
            precision=HIGHEST,
            preferred_element_type=F32,
        )
        + place_mean / PATCHES
    )

    head_t = jnp.concatenate([head_weight[...], jnp.zeros((4, width), F32)], axis=0)
    own_logit = lax.dot_general(
        own_row, head_t, LAST, precision=HIGHEST, preferred_element_type=F32
    )
    row = lax.broadcasted_iota(jnp.int32, (HEADS, 128), 0)
    lane = lax.broadcasted_iota(jnp.int32, (HEADS, 128), 1)
    mine = row == head
    own_logit = jnp.where(mine[:, 0:HEADS], own_logit, 0.0)

    loads["waves"].wait()
    pixels = image[0]
    first_cos = jnp.dot(waves[0], pixels, precision=HIGHEST, preferred_element_type=F32)
    first_sin = jnp.dot(waves[1], pixels, precision=HIGHEST, preferred_element_type=F32)
    spectrum = jnp.dot(first_cos, waves[2], precision=HIGHEST, preferred_element_type=F32)
    spectrum = spectrum + jnp.dot(
        first_sin, waves[3], precision=HIGHEST, preferred_element_type=F32
    )
    spectrum = spectrum / PIX

    pl.semaphore_wait(barrier, count)

    def member(m):
        return chip // 4 * 8 + m // 2 * 2 + core, vol // 2 * 2 + m % 2

    def flipped(k):
        low = (head + k) % 2
        mid = (head // 2 + k // 2) % 2
        return (head // 4 + k // 4) % 2 * 4 + mid * 2 + low

    def patch_copy(k, slot):
        to_dp, to_vol = member(flipped(k))
        return copy(
            patches,
            patch_buf.at[slot],
            patch_sems.at[0, k],
            patch_sems.at[1, slot],
            to_dp,
            to_vol,
        )

    def patch_relay(k):
        to_dp, to_vol = member(flipped(k))
        slot = flipped(4)
        return copy(
            patch_buf.at[slot],
            patch_buf.at[slot],
            patch_sems.at[0, 4 + k],
            patch_sems.at[1, slot],
            to_dp,
            to_vol,
        )

    def weight_copy(k, slot):
        to = (chip + k) % chips
        return copy(
            pieces.at[to % 4],
            weight.at[slot],
            weight_sems.at[0, k],
            weight_sems.at[1, slot],
            to * 2 + core,
            vol,
        )

    def weight_relay(at):
        s = at * 2 + core
        return copy(
            weight.at[s], weight.at[s], relay_sems.at[at], weight_sems.at[1, s], other, vol
        )

    def line_copy(k, slot):
        to = (vol + k) % vols
        return copy(picked.at[k], lines.at[slot], line_sems.at[0, k], line_sems.at[1, slot], dp, to)

    patch_copy(4, head).start()
    each(chips // 2, chips, lambda k: weight_copy(k, dp).start())
    each(1, 4, lambda k: patch_copy(k, head).start())
    each(1, chips // 2, lambda k: weight_copy(k, dp).start())
    weight_relay(chip).start()
    patch_buf[head] = patches[...]

    loads["index"].wait()
    loads["spots"].wait()
    loads["sel"].wait()
    loads["volume"].wait()

    def render(step_k, c):
        k = step_k + 1
        v = (vol + k) % vols
        turned = jnp.concatenate([index[v], jnp.zeros((4, 128), jnp.int32)], axis=0)
        turned = turned.astype(F32).T.astype(jnp.int32)
        spot_lane = lax.broadcasted_iota(jnp.int32, (128, 256), 1)
        spot_row = lax.broadcasted_iota(jnp.int32, (128, 256), 0)
        for hyp in range(K):
            line = turned[:, hyp : hyp + 1]
            level = (line >> 4) - vol * slab
            target = jnp.where((level >= 0) & (level < slab), line & 15, 1024)
            hot = jnp.where(spot_lane == (spot_row % 16) * 16 + target, 1.0, 0.0).astype(BF16)
            found = []
            for group in range(8):
                tiles = []
                for i in range(16):
                    spot = spots[v, hyp, group * 16 + i]
                    tiles.append(slab_buf[(spot >> 4) & (slab - 1)])
                tiles = jnp.concatenate(tiles, axis=0)
                found.append(
                    jnp.dot(
                        hot[group * 16 : group * 16 + 16], tiles, preferred_element_type=F32
                    )
                )
            found = jnp.concatenate(found, axis=0).astype(BF16)
            picked[k, hyp * PIX : (hyp + 1) * PIX, :] = jnp.dot(
                found, sel[...], preferred_element_type=F32
            ).astype(BF16)
        @pl.when(k < vols)
        def _():
            line_copy(k, vol).start()

        return c

    lax.fori_loop(0, vols, render, 0)
    lines[vol] = picked[vols]

    def weight_pass(k):
        at = (chip + chips - k) % chips
        weight_copy(k, at * 2 + core).wait_recv()
        weight_relay(at).start()


    first = lax.broadcasted_iota(jnp.int32, (PATCHES // 2, 128), 1) < 64
    high = gram[0:64].astype(BF16)
    gram_parts = jnp.concatenate([high.astype(F32), gram[0:64] - high.astype(F32)], axis=1)
    gram_parts = jnp.concatenate([gram_parts, jnp.zeros((64, 128), F32)], axis=0).astype(BF16)
    gram_places = jnp.concatenate([2.0 * gram[64:320], jnp.zeros((PATCHES, 64), F32)], axis=1)

    def norms(k, c):
        j = flipped(k)

        @pl.when(jnp.logical_and(k > 0, k % HEADS != 4))
        def _():
            patch_copy(k, j).wait_recv()

        both = patch_buf[j].astype(F32)
        turned = pltpu.roll(both, 64, 1)
        both = jnp.concatenate(
            [jnp.where(first, both, turned), jnp.where(first, turned, both)], axis=0
        )
        one = both.astype(BF16)
        tokens[j] = one
        tokens_t[:, pl.ds(pl.multiple_of(j * PATCHES, PATCHES), PATCHES)] = one.T[0:64]
        total = jnp.dot(one, gram_parts, preferred_element_type=F32) + gram_places
        total = jnp.sum(both * total, axis=1, keepdims=True)
        total = jnp.maximum(total + square[...], 0.0) / width
        scales[j] = jnp.broadcast_to(lax.rsqrt(total + EPSILON), (PATCHES, 128))
        return c

    norms(0, 0)
    patch_copy(4, flipped(4)).wait_recv()
    each(1, 4, lambda k: patch_relay(k).start())
    each(1, chips // 2, weight_pass)
    lax.fori_loop(1, 5, norms, 0)
    each(chips // 2, chips, weight_pass)
    lax.fori_loop(5, HEADS, norms, 0)

    def weight_rest(k):
        s = (chip + chips - k) % chips * 2 + 1 - core
        weight_copy(0, s).wait_recv()

    each(0, chips, weight_rest)

    sides = weight[:, 0:rows, :].reshape(width, 128)
    value = weight[:, rows : rows + rows // 2, :]
    value = jnp.concatenate([value[:, :, 0:64], value[:, :, 64:128]], axis=1)
    half = jnp.where(lax.broadcasted_iota(jnp.int32, (1, 128), 1) < 64, HEAD_DIM ** (-0.5), 1.0)
    sides = jnp.dot(basis[0:320], sides, preferred_element_type=F32) * half
    value = jnp.dot(
        basis[0:320], value.reshape(width, HEAD_DIM), preferred_element_type=F32
    )
    both = jnp.concatenate([sides, value, jnp.zeros((320, 64), F32)], axis=1)
    total_buf[...] = both[64:320]
    turn = jnp.concatenate([both[0:64], jnp.zeros((64, 256), F32)], axis=0).astype(BF16)
    mixed = jnp.sum(weight[:, rows + rows // 2 :, :].astype(F32), axis=0)[0:8]
    mixed = mixed[:, 0:64] + mixed[:, 64:128]

    ones = jnp.ones((PATCHES, 128), BF16)

    def forward(j):
        scale = scales[j]
        t = jnp.dot(tokens[j], turn, preferred_element_type=F32) + total_buf[...]
        t = (t * jnp.concatenate([scale, scale], axis=1)).astype(BF16)
        triple[j] = t
        scores = lax.dot_general(t[:, 64:128], t[:, 0:64], LAST, preferred_element_type=F32)
        raised = jnp.exp(scores)
        chosen = (raised * (1.0 / jnp.sum(raised, axis=0, keepdims=True))).astype(BF16)
        attention[j] = chosen
        col = jnp.sum(chosen.astype(F32), axis=1, keepdims=True)
        column[j] = col * scale
        mean_att[pl.ds(j, 1), :] = (
            jnp.sum(col * t[:, 128:256].astype(F32), axis=0, keepdims=True) / PATCHES
        )

    def forwards(i):
        forward(2 * i)
        forward(2 * i + 1)

    each(0, HEADS // 2, forwards)

    loads["contrast"].wait()
    each(1, vols, lambda k: line_copy(k, (vol + vols - k) % vols).wait_recv())
    slices = lines[0].astype(F32)
    for v in range(1, vols):
        slices = slices + lines[v].astype(F32)
    filt = contrast[0].astype(F32)
    misfits = jnp.zeros((HEADS, 128), F32)
    for k in range(K):
        misfit = filt * slices[k * PIX : (k + 1) * PIX] - spectrum
        value = jnp.sum(jnp.sum(misfit * misfit, axis=0, keepdims=True), axis=1, keepdims=True)
        misfits = jnp.where(lane == k, value / (PIX * PIX), misfits)
    errors_out[...] = misfits
    misfits = jnp.where(mine, pltpu.roll(misfits, 4, 1), 0.0)
    means = mean_att[:, 0:HEAD_DIM]
    logit = own_logit + lax.dot_general(
        means, mixed, LAST, precision=HIGHEST, preferred_element_type=F32
    )
    logit = jnp.where(
        lane < K, jnp.concatenate([logit, jnp.zeros((HEADS, 120), F32)], axis=1), misfits
    )
    small_send[...] = logit

    def small_copy(k, slot):
        to_dp, to_vol = member(flipped(k))
        return copy(
            small_send,
            small_recv.at[slot],
            small_sems.at[0, k],
            small_sems.at[1, slot],
            to_dp,
            to_vol,
        )

    each(1, HEADS, lambda k: small_copy(HEADS - k, head).start())
    small_recv[head] = small_send[...]
    each(1, HEADS, lambda k: small_copy(k, flipped(k)).wait_recv())
    summed = jnp.sum(small_recv[...], axis=0)
    misfits = jnp.where(lane < K, pltpu.roll(summed, 124, 1), 0.0)
    raised = jnp.where(lane < K, jnp.exp(summed), 0.0)
    chances = raised / jnp.sum(raised, axis=1, keepdims=True)
    expected = jnp.sum(chances * misfits, axis=1, keepdims=True)
    slope = chances * (misfits - expected)
    pulled = jnp.zeros((HEADS, HEAD_DIM), F32)
    for k in range(K):
        pulled = pulled + slope[:, k : k + 1] * mixed[k : k + 1, :]
    pulled_buf[...] = jnp.concatenate(
        [pulled / PATCHES, jnp.zeros((HEADS, 128 - HEAD_DIM), F32)], axis=1
    )
    slope_buf[...] = slope

    slope_t = slope.T[0:8]
    outer = jnp.zeros((HEADS, 128), F32)
    for j in range(HEADS):
        outer = outer + slope_t[:, j : j + 1] * mean_att[j : j + 1, :]
    own = jnp.sum(jnp.where(lane[:, 0:HEADS] == head, slope_t, 0.0), axis=1, keepdims=True)
    side_send[:, 0:width] = own * own_row
    side_send[:, width:] = outer
    side = copy(side_send, side_recv, core_sems.at[0], core_sems.at[1], other, vol)
    side.start()

    wide = lax.broadcasted_iota(jnp.int32, (PATCHES, 128), 1)

    def backward(j):
        t = triple[j]
        chosen = attention[j]
        wider = chosen.astype(F32)
        up = jnp.sum(
            t[:, 128:256].astype(F32) * pulled_buf[pl.ds(j, 1), :], axis=1, keepdims=True
        )
        center = jnp.sum(wider * up, axis=0, keepdims=True)
        inner = (wider * (up - center)).astype(BF16)
        sides = t[:, 0:128]
        key_slope = jnp.dot(inner, sides, preferred_element_type=F32)
        query_slope = lax.dot_general(inner, sides, FIRST, preferred_element_type=F32)
        scale = scales[j]
        slopes = jnp.where(wide < 64, key_slope, query_slope * HEAD_DIM ** (-0.5)) * scale
        spread = column[j] * slope_buf[pl.ds(j, 1), :]
        terms = jnp.concatenate([slopes, spread], axis=1)
        terms_buf[pl.ds(pl.multiple_of(j * PATCHES, PATCHES), PATCHES), :] = terms.astype(BF16)
        return terms

    total_buf[...] = jnp.zeros((PATCHES, 256), F32)

    def backwards(i):
        total_buf[...] += backward(2 * i) + backward(2 * i + 1)

    each(0, HEADS // 2, backwards)

    factor_send[0:64, :] = jnp.dot(
        tokens_t[...], terms_buf[...], preferred_element_type=F32
    ).astype(BF16)
    factor_send[64:320, :] = total_buf[...].astype(BF16)
    factors = copy(factor_send, factor_recv, core_sems.at[2], core_sems.at[3], other, vol)
    factors.start()
    factors.wait_recv()
    side.wait_recv()
    factor_sum[0:320, :] = (
        factor_send[...].astype(F32) + factor_recv[...].astype(F32)
    ).astype(BF16)
    factor_sum[320:384, :] = jnp.zeros((64, 256), BF16)
    sides = side_send[...] + side_recv[...]
    pooled_t = sides[:, 0:width]
    outer = sides[:, width : width + HEAD_DIM]

    value_t = lax.dot_general(
        factor_sum[:, 128:256], basis[...], FIRST, preferred_element_type=F32
    )[0:8]
    fill = [jnp.zeros((HEADS, 64 - rows), F32)] if rows < 64 else []
    for d in range(dps):
        part = slice(d * rows, (d + 1) * rows)
        top = jnp.concatenate([value_t[:, part]] + fill + [outer], axis=1)
        low = jnp.concatenate([mixed, pooled_t[:, part]] + fill, axis=1)
        tile_send[d] = jnp.where(row < 4, top, pltpu.roll(low, 4, 0))

    def tile_copy(k, slot):
        e = (me + k) % count
        d = e // vols * 2 + core
        return copy(
            tile_send.at[d],
            tile_recv.at[slot],
            tile_sems.at[0, k],
            tile_sems.at[1, slot],
            d,
            e % vols,
        )

    def grad_copy(k, slot):
        e = (me + k) % count
        d = e // vols * 2 + core
        return copy(
            grad_send.at[d],
            grad_recv.at[slot],
            grad_sems.at[0, k],
            grad_sems.at[1, slot],
            d,
            e % vols,
        )

    each(count // 2, count, lambda k: tile_copy(k, me).start())
    each(1, count // 2, lambda k: tile_copy(k, me).start())
    grad_send[...] = (
        jnp.dot(basis_t[...], factor_sum[:, 0:128], preferred_element_type=F32)
        .astype(BF16)
        .reshape(dps, rows, 128)
    )
    each(count // 2, count, lambda k: grad_copy(k, me).start())
    each(1, count // 2, lambda k: grad_copy(k, me).start())
    grad_recv[me] = grad_send[dp]
    tile_recv[me] = tile_send[dp]

    each(1, count, lambda k: tile_copy(k, (me + count - k) % count).wait_recv())

    outers = []
    for h in range(HEADS):
        senders = senders_of(dps, vols, h)
        tile = tile_recv[senders[0]]
        for s in senders[1:]:
            tile = tile + tile_recv[s]
        outers.append(tile[:, 64:128])
    pooled_sum = pltpu.roll(jnp.sum(tile_recv[...], axis=0), 4, 0)
    branch = lax.dot_general(
        jnp.concatenate(outers, axis=1),
        project_out[...].astype(F32),
        LAST,
        precision=HIGHEST,
        preferred_element_type=F32,
    )
    fill = [jnp.zeros((HEADS, 64 - rows), F32)] if rows < 64 else []
    pooled_sum = pooled_sum + jnp.concatenate(
        [jnp.zeros((HEADS, 64), F32), branch] + fill, axis=1
    )
    head_send[...] = pooled_sum

    def head_copy(k, slot):
        to = (chip + k) % chips
        return copy(
            head_send,
            head_out.at[core, slot],
            head_sems.at[0, k],
            head_sems.at[1, slot],
            to * 2 + core,
            vol,
        )

    each(1, chips, lambda k: head_copy(k, chip).start())
    head_out[core, chip] = pooled_sum

    for h in range(HEADS):
        senders = senders_of(dps, vols, h)
        tile = tile_recv[senders[0]]
        mixed_h = jnp.where(row < 4, pltpu.roll(tile, 4, 0), 0.0)[:, 0:64]
        for s in senders[1:]:
            tile = tile + tile_recv[s]
        tile = jnp.where(row < 4, tile, 0.0)
        value_out[:, h * 64 : h * 64 + 64] = (
            lax.dot_general(
                tile[:, 0:rows], mixed_h, FIRST, precision=HIGHEST, preferred_element_type=F32
            )
            / PATCHES
        )
        value_out[:, 512 + h * 64 : 576 + h * 64] = jnp.dot(
            head_own, tile[:, 64:128], precision=HIGHEST, preferred_element_type=F32
        )

    each(1, chips, lambda k: head_copy(k, (chip + chips - k) % chips).wait_recv())
    heads = copy(
        head_out.at[core], head_out.at[core], core_sems.at[4], core_sems.at[5], other, vol
    )
    heads.start()

    each(1, count, lambda k: grad_copy(k, (me + count - k) % count).wait_recv())
    copy(
        head_out.at[1 - core], head_out.at[1 - core], core_sems.at[4], core_sems.at[5], other, vol
    ).wait_recv()

    each(1, 5, lambda k: patch_copy(k, head).wait_send())
    each(1, 4, lambda k: patch_relay(k).wait_send())
    each(1, chips, lambda k: weight_copy(k, dp).wait_send())
    each(0, chips, lambda at: weight_relay(at).wait_send())
    each(1, vols, lambda k: line_copy(k, vol).wait_send())
    each(1, HEADS, lambda k: small_copy(k, head).wait_send())
    side.wait_send()
    factors.wait_send()
    each(1, count, lambda k: tile_copy(k, me).wait_send())
    each(1, count, lambda k: grad_copy(k, me).wait_send())
    each(1, chips, lambda k: head_copy(k, chip).wait_send())
    heads.wait_send()


def senders_of(dps, vols, h):
    return [
        (z * 4 + h // 2) * vols + v * 2 + h % 2 for z in range(dps // 8) for v in range(vols // 2)
    ]


def finish(dps, vols, errors, grads, values, heads, errors_out, in_out, out_out, head_out):
    rows = values.shape[0]
    for h in range(HEADS):
        senders = senders_of(dps, vols, h)
        both = grads[senders[0]].astype(F32)
        for s in senders[1:]:
            both = both + grads[s].astype(F32)
        in_out[:, h * 64 : h * 64 + 64] = both[:, 64:128]
        in_out[:, 512 + h * 64 : 576 + h * 64] = both[:, 0:64]
    in_out[:, 1024:1536] = values[:, 0:512]
    out_out[...] = values[:, 512:1024]
    errors_out[...] = errors[0:1, 0:K]
    for d in range(dps):
        head_out[:, d * rows : (d + 1) * rows] = heads[d % 2, d // 2][0:K, 64 : 64 + rows]


def constants():
    freq = np.arange(PIX) - PIX // 2
    phase = (freq[:, None] * np.arange(PIX)[None, :] % PIX) * (2.0 * math.pi / PIX)
    cosine, sine = np.cos(phase), np.sin(phase)
    waves = np.stack([cosine, sine, (cosine + sine).T, (cosine - sine).T]).astype(np.float32)
    sel = np.zeros((2 * PIX, PIX), np.float32)
    sel[2 * np.arange(PIX), np.arange(PIX)] = 1.0
    places = np.zeros((PATCH, PIX, PIX), np.float32)
    for r in range(PATCH):
        places[r, np.arange(PIX), r * PATCH + np.arange(PIX) % PATCH] = 1.0
    return waves, sel, places


def local(
    dps,
    vols,
    images,
    contrast,
    volume,
    line_index,
    patch_weight,
    position,
    norm_gain,
    project_in,
    project_out,
    head_weight,
):
    width = norm_gain.shape[0]
    rows = project_in.shape[0]
    chips = dps // 2
    count = chips * vols
    waves, sel, places = constants()
    slab, side, _ = volume.shape
    vmem = pl.BlockSpec(memory_space=pltpu.VMEM)
    hbm = pl.BlockSpec(memory_space=pltpu.HBM)
    inputs = (
        images,
        contrast,
        patch_weight,
        position,
        norm_gain.reshape(1, width),
        project_in,
        project_out,
        head_weight.T,
        jnp.asarray(waves),
        jnp.asarray(sel, BF16),
        jnp.asarray(places, BF16),
    )
    errors, grads, values, heads = pl.pallas_call(
        functools.partial(step, dps, vols),
        out_shape=(
            jax.ShapeDtypeStruct((8, 128), F32),
            jax.ShapeDtypeStruct((count, rows, 128), BF16),
            jax.ShapeDtypeStruct((rows, 1024), F32),
            jax.ShapeDtypeStruct((2, chips, 8, 128), F32),
        ),
        in_specs=[hbm] * (2 + len(inputs)),
        out_specs=(vmem,) * 4,
        scratch_shapes=[
            pltpu.SMEM(line_index.shape, jnp.int32),
            pltpu.VMEM(line_index.shape, jnp.int32),
        ]
        + [pltpu.VMEM(one.shape, one.dtype) for one in inputs]
        + [
            pltpu.VMEM((slab * (side // 16), 16, side), BF16),
            pltpu.VMEM((vols + 1, K * PIX, PIX), BF16),
            pltpu.VMEM((PATCHES // 2, 128), BF16),
            pltpu.VMEM((4, rows + rows // 2 + 16, 128), BF16),
            pltpu.VMEM((128, 8), F32),
            pltpu.VMEM((vols, K * PIX, PIX), BF16),
            pltpu.VMEM((HEADS, PATCHES // 2, 128), BF16),
            pltpu.VMEM((dps, rows + rows // 2 + 16, 128), BF16),
            pltpu.VMEM((384, width), BF16),
            pltpu.VMEM((width, 384), BF16),
            pltpu.VMEM((320, 64), F32),
            pltpu.VMEM((PATCHES, 1), F32),
            pltpu.VMEM((HEADS, PATCHES, 128), BF16),
            pltpu.VMEM((64, HEADS * PATCHES), BF16),
            pltpu.VMEM((HEADS, PATCHES, 128), F32),
            pltpu.VMEM((HEADS, PATCHES, PATCHES), BF16),
            pltpu.VMEM((HEADS, PATCHES, 256), BF16),
            pltpu.VMEM((HEADS, PATCHES, 128), F32),
            pltpu.VMEM((HEADS, 128), F32),
            pltpu.VMEM((HEADS, 128), F32),
            pltpu.VMEM((HEADS, HEADS, 128), F32),
            pltpu.VMEM((HEADS, 128), F32),
            pltpu.VMEM((HEADS, 128), F32),
            pltpu.VMEM((HEADS * PATCHES, 256), BF16),
            pltpu.VMEM((PATCHES, 256), F32),
            pltpu.VMEM((320, 256), BF16),
            pltpu.VMEM((320, 256), BF16),
            pltpu.VMEM((384, 256), BF16),
            pltpu.VMEM((8, width + 128), F32),
            pltpu.VMEM((8, width + 128), F32),
            pltpu.VMEM((dps, rows, 128), BF16),
            pltpu.VMEM((dps, 8, 128), F32),
            pltpu.VMEM((count, 8, 128), F32),
            pltpu.VMEM((8, 128), F32),
            pltpu.SemaphoreType.DMA((14,)),
            pltpu.SemaphoreType.DMA((2, vols)),
            pltpu.SemaphoreType.DMA((2, HEADS)),
            pltpu.SemaphoreType.DMA((2, dps)),
            pltpu.SemaphoreType.DMA((chips,)),
            pltpu.SemaphoreType.DMA((2, HEADS)),
            pltpu.SemaphoreType.DMA((6,)),
            pltpu.SemaphoreType.DMA((2, count)),
            pltpu.SemaphoreType.DMA((2, count)),
            pltpu.SemaphoreType.DMA((2, chips)),
        ],
        compiler_params=pltpu.CompilerParams(
            collective_id=0, has_side_effects=True, vmem_limit_bytes=56 * 1024 * 1024
        ),
        name="pose_step",
    )(line_index, volume.reshape(slab * (side // 16), 16, side), *inputs)
    errors, in_grad, out_grad, head_grad = pl.pallas_call(
        functools.partial(finish, dps, vols),
        out_shape=(
            jax.ShapeDtypeStruct((1, K), F32),
            jax.ShapeDtypeStruct((rows, 3 * HEADS * HEAD_DIM), F32),
            jax.ShapeDtypeStruct((rows, HEADS * HEAD_DIM), F32),
            jax.ShapeDtypeStruct((K, width), F32),
        ),
        in_specs=[vmem] * 4,
        out_specs=(vmem,) * 4,
        name="finish",
    )(errors, grads, values, heads)
    return errors, in_grad, out_grad, head_grad.T


def solution(mesh):
    placed = (
        P(("dp", "vol"), None, None),
        P(("dp", "vol"), None, None),
        P("vol", None, None),
        P("dp", None, None),
        P(),
        P(),
        P(),
        P("dp", None),
        P("dp", None),
        P(),
    )
    return jax.shard_map(
        functools.partial(local, mesh.shape["dp"], mesh.shape["vol"]),
        mesh=mesh,
        in_specs=placed,
        out_specs=(P(("dp", "vol"), None), P("dp", None), P("dp", None), P()),
        check_vma=False,
    )
```

```python
import functools
import math

import jax
import jax.numpy as jnp
import numpy as np
from jax import lax
from jax.experimental import pallas as pl
from jax.experimental.pallas import tpu as pltpu
from jax.sharding import PartitionSpec as P

HEADS = 8
HEAD_DIM = 64
PIX = 128
PATCH = 8
PATCHES = 256
K = 4
EPSILON = 1e-05
F32 = jnp.float32
BF16 = jnp.bfloat16
HIGHEST = lax.Precision.HIGHEST
FIRST = (((0,), (0,)), ((), ()))
LAST = (((1,), (1,)), ((), ()))
MESH = pl.DeviceIdType.MESH


def step(
    dps,
    vols,
    index_hbm,
    volume,
    image_hbm,
    contrast_hbm,
    patch_weight_hbm,
    position_hbm,
    gain_hbm,
    project_in_hbm,
    project_out_hbm,
    head_hbm,
    waves_hbm,
    sel_hbm,
    places_hbm,
    errors_out,
    grad_recv,
    value_out,
    head_out,
    spots,
    index,
    image,
    contrast,
    patch_weight,
    position,
    gain,
    project_in,
    project_out,
    head_weight,
    waves,
    sel,
    places,
    slab_buf,
    picked,
    patches,
    pieces,
    head_wide,
    lines,
    patch_buf,
    weight,
    basis,
    basis_t,
    gram,
    square,
    tokens,
    tokens_t,
    scales,
    attention,
    triple,
    column,
    mean_att,
    small_send,
    small_recv,
    pulled_buf,
    slope_buf,
    terms_buf,
    total_buf,
    factor_send,
    factor_recv,
    factor_sum,
    side_send,
    side_recv,
    grad_send,
    tile_send,
    tile_recv,
    head_send,
    in_sems,
    line_sems,
    patch_sems,
    weight_sems,
    relay_sems,
    small_sems,
    core_sems,
    grad_sems,
    tile_sems,
    head_sems,
):
    dp = lax.axis_index("dp")
    vol = lax.axis_index("vol")
    core = dp % 2
    chip = dp // 2
    chips = dps // 2
    count = chips * vols
    me = chip * vols + vol
    pair = vol % 2
    head = (chip % 4) * 2 + pair
    rows = project_in.shape[0]
    width = gain.shape[1]
    slab = volume.shape[0]

    def copy(src, dst, send_sem, recv_sem, to_dp, to_vol):
        return pltpu.make_async_remote_copy(
            src_ref=src,
            dst_ref=dst,
            send_sem=send_sem,
            recv_sem=recv_sem,
            device_id=(to_dp, to_vol),
            device_id_type=MESH,
        )

    def each(first, last, body):
        def run(k, c):
            body(k)
            return c

        lax.fori_loop(first, last, run, 0)

    other = dp + 1 - 2 * core
    barrier = pltpu.get_barrier_semaphore()

    def greet(k):
        e = (me + k) % count
        pl.semaphore_signal(
            barrier, inc=1, device_id=(e // vols * 2 + core, e % vols), device_id_type=MESH
        )

    each(count // 2, count, greet)
    each(1, count // 2, greet)
    pl.semaphore_signal(barrier, inc=1, device_id=(other, vol), device_id_type=MESH)

    loads = {}
    for name, src, dst in (
        ("image", image_hbm, image),
        ("places", places_hbm, places),
        ("project_in", project_in_hbm, project_in),
        ("project_out", project_out_hbm, project_out),
        ("index", index_hbm, index),
        ("spots", index_hbm, spots),
        ("sel", sel_hbm, sel),
        ("waves", waves_hbm, waves),
        ("patch_weight", patch_weight_hbm, patch_weight),
        ("position", position_hbm, position),
        ("gain", gain_hbm, gain),
        ("head", head_hbm, head_weight),
        ("contrast", contrast_hbm, contrast),
        ("volume", volume, slab_buf),
    ):
        loads[name] = pltpu.make_async_copy(src, dst, in_sems.at[len(loads)])
        loads[name].start()

    loads["project_in"].wait()
    loads["project_out"].wait()
    loads["head"].wait()
    near = pl.ds(pl.multiple_of(dp * rows // 128 * 128, 128), 128)
    head_wide[...] = jnp.concatenate(
        [head_weight[:, near], jnp.zeros((4, 128), F32)], axis=0
    ).T
    head_own = head_wide[pl.ds(pl.multiple_of(dp * rows % 128, rows), rows), :]
    share = lax.dot_general(
        head_own,
        project_out[...].astype(F32),
        FIRST,
        precision=HIGHEST,
        preferred_element_type=F32,
    )
    for a in range(4):
        parts = [project_in[:, p * 512 + a * 128 : p * 512 + a * 128 + 128] for p in range(3)]
        parts.append(share[:, a * 128 : a * 128 + 128])
        query, key, value, mix = [
            jnp.where(pair == 0, one[:, 0:64], one[:, 64:128]) for one in parts
        ]
        high = mix.astype(BF16)
        mix = jnp.concatenate([high.astype(F32), mix - high.astype(F32)], axis=1)
        pieces[a, 0:rows, :] = jnp.concatenate([query, key], axis=1)
        pieces[a, rows : rows + rows // 2, :] = jnp.concatenate(
            [value[0 : rows // 2], value[rows // 2 : rows]], axis=1
        )
        pieces[a, rows + rows // 2 :, :] = jnp.concatenate(
            [mix, jnp.zeros((8, 128), F32)], axis=0
        ).astype(BF16)
    weight[dp] = pieces[chip % 4]
    loads["image"].wait()
    loads["places"].wait()
    cells = lax.broadcasted_iota(jnp.int32, (16, 16, 128), 1)
    spread_lane = lax.broadcasted_iota(jnp.int32, (16, 16, 128), 2)
    cut = jnp.zeros((PATCHES, 128), F32)
    for r in range(PATCH):
        stripe = image[0, pl.ds(r, 16, stride=PATCH), :]
        stripe = jnp.broadcast_to(stripe[:, None, :], (16, 16, 128))
        stripe = jnp.where(spread_lane // PATCH == cells, stripe, 0.0).reshape(PATCHES, 128)
        cut = cut + jnp.dot(stripe.astype(BF16), places[r], preferred_element_type=F32)
    patches[...] = jnp.concatenate([cut[0:128, 0:64], cut[128:256, 0:64]], axis=1).astype(BF16)
    patch_mean = jnp.sum(cut[:, 0:64], axis=0, keepdims=True) / PATCHES
    loads["patch_weight"].wait()
    loads["position"].wait()
    loads["gain"].wait()
    embed = patch_weight[...].astype(F32)
    embed_c = embed - jnp.mean(embed, axis=1, keepdims=True)
    basis[0:64, :] = (embed_c * gain[...]).astype(BF16)
    gram[0:64, :] = lax.dot_general(
        embed_c, embed_c, LAST, precision=HIGHEST, preferred_element_type=F32
    )
    place_mean = jnp.zeros((1, width), F32)
    for part in range(4):
        one = position[part * 64 : part * 64 + 64, :].astype(F32)
        place_mean = place_mean + jnp.sum(one, axis=0, keepdims=True)
        one = one - jnp.mean(one, axis=1, keepdims=True)
        basis[64 + part * 64 : 128 + part * 64, :] = (one * gain[...]).astype(BF16)
        gram[64 + part * 64 : 128 + part * 64, :] = lax.dot_general(
            one, embed_c, LAST, precision=HIGHEST, preferred_element_type=F32
        )
        square[part * 64 : part * 64 + 64, :] = jnp.sum(one * one, axis=1, keepdims=True)
    basis[320:384, :] = jnp.zeros((64, width), BF16)
    basis_t[...] = basis[...].T
    own_row = (
        jnp.dot(
            jnp.broadcast_to(patch_mean, (8, 64)),
            embed,
            precision=HIGHEST,
            preferred_element_type=F32,
        )
        + place_mean / PATCHES
    )

    head_t = jnp.concatenate([head_weight[...], jnp.zeros((4, width), F32)], axis=0)
    own_logit = lax.dot_general(
        own_row, head_t, LAST, precision=HIGHEST, preferred_element_type=F32
    )
    row = lax.broadcasted_iota(jnp.int32, (HEADS, 128), 0)
    lane = lax.broadcasted_iota(jnp.int32, (HEADS, 128), 1)
    mine = row == head
    own_logit = jnp.where(mine[:, 0:HEADS], own_logit, 0.0)

    loads["waves"].wait()
    pixels = image[0]
    first_cos = jnp.dot(waves[0], pixels, precision=HIGHEST, preferred_element_type=F32)
    first_sin = jnp.dot(waves[1], pixels, precision=HIGHEST, preferred_element_type=F32)
    spectrum = jnp.dot(first_cos, waves[2], precision=HIGHEST, preferred_element_type=F32)
    spectrum = spectrum + jnp.dot(
        first_sin, waves[3], precision=HIGHEST, preferred_element_type=F32
    )
    spectrum = spectrum / PIX

    pl.semaphore_wait(barrier, count)

    def member(m):
        return chip // 4 * 8 + m // 2 * 2 + core, vol // 2 * 2 + m % 2

    def flipped(k):
        low = (head + k) % 2
        mid = (head // 2 + k // 2) % 2
        return (head // 4 + k // 4) % 2 * 4 + mid * 2 + low

    def patch_copy(k, slot):
        to_dp, to_vol = member(flipped(k))
        return copy(
            patches,
            patch_buf.at[slot],
            patch_sems.at[0, k],
            patch_sems.at[1, slot],
            to_dp,
            to_vol,
        )

    def patch_relay(k):
        to_dp, to_vol = member(flipped(k))
        slot = flipped(4)
        return copy(
            patch_buf.at[slot],
            patch_buf.at[slot],
            patch_sems.at[0, 4 + k],
            patch_sems.at[1, slot],
            to_dp,
            to_vol,
        )

    def weight_copy(k, slot):
        to = (chip + k) % chips
        return copy(
            pieces.at[to % 4],
            weight.at[slot],
            weight_sems.at[0, k],
            weight_sems.at[1, slot],
            to * 2 + core,
            vol,
        )

    def weight_relay(at):
        s = at * 2 + core
        return copy(
            weight.at[s], weight.at[s], relay_sems.at[at], weight_sems.at[1, s], other, vol
        )

    def line_copy(k, slot):
        to = (vol + k) % vols
        return copy(picked.at[k], lines.at[slot], line_sems.at[0, k], line_sems.at[1, slot], dp, to)

    patch_copy(4, head).start()
    each(chips // 2, chips, lambda k: weight_copy(k, dp).start())
    each(1, 4, lambda k: patch_copy(k, head).start())
    each(1, chips // 2, lambda k: weight_copy(k, dp).start())
    weight_relay(chip).start()
    patch_buf[head] = patches[...]

    loads["index"].wait()
    loads["spots"].wait()
    loads["sel"].wait()
    loads["volume"].wait()

    def render(step_k, c):
        k = step_k + 1
        v = (vol + k) % vols
        turned = jnp.concatenate([index[v], jnp.zeros((4, 128), jnp.int32)], axis=0)
        turned = turned.astype(F32).T.astype(jnp.int32)
        spot_lane = lax.broadcasted_iota(jnp.int32, (128, 256), 1)
        spot_row = lax.broadcasted_iota(jnp.int32, (128, 256), 0)
        for hyp in range(K):
            line = turned[:, hyp : hyp + 1]
            level = (line >> 4) - vol * slab
            target = jnp.where((level >= 0) & (level < slab), line & 15, 1024)
            hot = jnp.where(spot_lane == (spot_row % 16) * 16 + target, 1.0, 0.0).astype(BF16)
            found = []
            for group in range(8):
                tiles = []
                for i in range(16):
                    spot = spots[v, hyp, group * 16 + i]
                    tiles.append(slab_buf[(spot >> 4) & (slab - 1)])
                tiles = jnp.concatenate(tiles, axis=0)
                found.append(
                    jnp.dot(
                        hot[group * 16 : group * 16 + 16], tiles, preferred_element_type=F32
                    )
                )
            found = jnp.concatenate(found, axis=0).astype(BF16)
            picked[k, hyp * PIX : (hyp + 1) * PIX, :] = jnp.dot(
                found, sel[...], preferred_element_type=F32
            ).astype(BF16)
        @pl.when(k < vols)
        def _():
            line_copy(k, vol).start()

        return c

    lax.fori_loop(0, vols, render, 0)
    lines[vol] = picked[vols]

    def weight_pass(k):
        at = (chip + chips - k) % chips
        weight_copy(k, at * 2 + core).wait_recv()
        weight_relay(at).start()


    first = lax.broadcasted_iota(jnp.int32, (PATCHES // 2, 128), 1) < 64
    high = gram[0:64].astype(BF16)
    gram_parts = jnp.concatenate([high.astype(F32), gram[0:64] - high.astype(F32)], axis=1)
    gram_parts = jnp.concatenate([gram_parts, jnp.zeros((64, 128), F32)], axis=0).astype(BF16)
    gram_places = jnp.concatenate([2.0 * gram[64:320], jnp.zeros((PATCHES, 64), F32)], axis=1)

    def norm(j):
        both = patch_buf[j].astype(F32)
        turned = pltpu.roll(both, 64, 1)
        both = jnp.concatenate(
            [jnp.where(first, both, turned), jnp.where(first, turned, both)], axis=0
        )
        one = both.astype(BF16)
        total = jnp.dot(one, gram_parts, preferred_element_type=F32) + gram_places
        total = jnp.sum(both * total, axis=1, keepdims=True)
        total = jnp.maximum(total + square[...], 0.0) / width
        scale = jnp.broadcast_to(lax.rsqrt(total + EPSILON), (PATCHES, 128))
        return one, one.T[0:64], scale

    def norms(ks):
        for k in ks:
            if k % 4 > 0:
                patch_copy(k, flipped(k)).wait_recv()
        found = [norm(flipped(k)) for k in ks]
        for k, (one, turned, scale) in zip(ks, found):
            j = flipped(k)
            tokens[j] = one
            tokens_t[:, pl.ds(pl.multiple_of(j * PATCHES, PATCHES), PATCHES)] = turned
            scales[j] = scale

    patch_copy(4, flipped(4)).wait_recv()
    each(1, 4, lambda k: patch_relay(k).start())
    norms((0, 4))
    each(1, chips // 2, weight_pass)
    norms((1, 2, 3))
    each(chips // 2, chips, weight_pass)
    norms((5, 6, 7))

    def weight_rest(k):
        s = (chip + chips - k) % chips * 2 + 1 - core
        weight_copy(0, s).wait_recv()

    each(0, chips, weight_rest)

    sides = weight[:, 0:rows, :].reshape(width, 128)
    value = weight[:, rows : rows + rows // 2, :]
    value = jnp.concatenate([value[:, :, 0:64], value[:, :, 64:128]], axis=1)
    half = jnp.where(lax.broadcasted_iota(jnp.int32, (1, 128), 1) < 64, HEAD_DIM ** (-0.5), 1.0)
    sides = jnp.dot(basis[0:320], sides, preferred_element_type=F32) * half
    value = jnp.dot(
        basis[0:320], value.reshape(width, HEAD_DIM), preferred_element_type=F32
    )
    both = jnp.concatenate([sides, value, jnp.zeros((320, 64), F32)], axis=1)
    total_buf[...] = both[64:320]
    turn = jnp.concatenate([both[0:64], jnp.zeros((64, 256), F32)], axis=0).astype(BF16)
    mixed = jnp.sum(weight[:, rows + rows // 2 :, :].astype(F32), axis=0)[0:8]
    mixed = mixed[:, 0:64] + mixed[:, 64:128]

    def forward(j):
        scale = scales[j]
        t = jnp.dot(tokens[j], turn, preferred_element_type=F32) + total_buf[...]
        t = (t * jnp.concatenate([scale, scale], axis=1)).astype(BF16)
        scores = lax.dot_general(t[:, 64:128], t[:, 0:64], LAST, preferred_element_type=F32)
        raised = jnp.exp(scores)
        chosen = (raised * (1.0 / jnp.sum(raised, axis=0, keepdims=True))).astype(BF16)
        col = jnp.sum(chosen.astype(F32), axis=1, keepdims=True)
        mean = jnp.sum(col * t[:, 128:256].astype(F32), axis=0, keepdims=True) / PATCHES
        return t, chosen, col * scale, mean

    def forwards(i):
        found = [forward(4 * i + u) for u in range(4)]
        for u in range(4):
            j = 4 * i + u
            triple[j], attention[j], column[j], mean_att[pl.ds(j, 1), :] = found[u]

    each(0, HEADS // 4, forwards)

    loads["contrast"].wait()
    each(1, vols, lambda k: line_copy(k, (vol + vols - k) % vols).wait_recv())
    slices = lines[0].astype(F32)
    for v in range(1, vols):
        slices = slices + lines[v].astype(F32)
    filt = contrast[0].astype(F32)
    misfits = jnp.zeros((HEADS, 128), F32)
    for k in range(K):
        misfit = filt * slices[k * PIX : (k + 1) * PIX] - spectrum
        value = jnp.sum(jnp.sum(misfit * misfit, axis=0, keepdims=True), axis=1, keepdims=True)
        misfits = jnp.where(lane == k, value / (PIX * PIX), misfits)
    errors_out[...] = misfits
    misfits = jnp.where(mine, pltpu.roll(misfits, 4, 1), 0.0)
    means = mean_att[:, 0:HEAD_DIM]
    logit = own_logit + lax.dot_general(
        means, mixed, LAST, precision=HIGHEST, preferred_element_type=F32
    )
    logit = jnp.where(
        lane < K, jnp.concatenate([logit, jnp.zeros((HEADS, 120), F32)], axis=1), misfits
    )
    small_send[...] = logit

    def small_copy(k, slot):
        to_dp, to_vol = member(flipped(k))
        return copy(
            small_send,
            small_recv.at[slot],
            small_sems.at[0, k],
            small_sems.at[1, slot],
            to_dp,
            to_vol,
        )

    each(1, HEADS, lambda k: small_copy(HEADS - k, head).start())
    small_recv[head] = small_send[...]
    each(1, HEADS, lambda k: small_copy(k, flipped(k)).wait_recv())
    summed = jnp.sum(small_recv[...], axis=0)
    misfits = jnp.where(lane < K, pltpu.roll(summed, 124, 1), 0.0)
    raised = jnp.where(lane < K, jnp.exp(summed), 0.0)
    chances = raised / jnp.sum(raised, axis=1, keepdims=True)
    expected = jnp.sum(chances * misfits, axis=1, keepdims=True)
    slope = chances * (misfits - expected)
    pulled = jnp.zeros((HEADS, HEAD_DIM), F32)
    for k in range(K):
        pulled = pulled + slope[:, k : k + 1] * mixed[k : k + 1, :]
    pulled_buf[...] = jnp.concatenate(
        [pulled / PATCHES, jnp.zeros((HEADS, 128 - HEAD_DIM), F32)], axis=1
    )
    slope_buf[...] = slope

    slope_t = slope.T[0:8]
    outer = jnp.zeros((HEADS, 128), F32)
    for j in range(HEADS):
        outer = outer + slope_t[:, j : j + 1] * mean_att[j : j + 1, :]
    own = jnp.sum(jnp.where(lane[:, 0:HEADS] == head, slope_t, 0.0), axis=1, keepdims=True)
    side_send[:, 0:width] = own * own_row
    side_send[:, width:] = outer
    side = copy(side_send, side_recv, core_sems.at[0], core_sems.at[1], other, vol)
    side.start()

    wide = lax.broadcasted_iota(jnp.int32, (PATCHES, 128), 1)

    def backward(j):
        t = triple[j]
        chosen = attention[j]
        wider = chosen.astype(F32)
        up = jnp.sum(
            t[:, 128:256].astype(F32) * pulled_buf[pl.ds(j, 1), :], axis=1, keepdims=True
        )
        center = jnp.sum(wider * up, axis=0, keepdims=True)
        inner = (wider * (up - center)).astype(BF16)
        sides = t[:, 0:128]
        key_slope = jnp.dot(inner, sides, preferred_element_type=F32)
        query_slope = lax.dot_general(inner, sides, FIRST, preferred_element_type=F32)
        scale = scales[j]
        slopes = jnp.where(wide < 64, key_slope, query_slope * HEAD_DIM ** (-0.5)) * scale
        spread = column[j] * slope_buf[pl.ds(j, 1), :]
        terms = jnp.concatenate([slopes, spread], axis=1)
        return terms

    total_buf[...] = jnp.zeros((PATCHES, 256), F32)

    def backwards(i):
        found = [backward(4 * i + u) for u in range(4)]
        total = total_buf[...]
        for u in range(4):
            at = pl.multiple_of((4 * i + u) * PATCHES, PATCHES)
            terms_buf[pl.ds(at, PATCHES), :] = found[u].astype(BF16)
            total = total + found[u]
        total_buf[...] = total

    each(0, HEADS // 4, backwards)

    factor_send[0:64, :] = jnp.dot(
        tokens_t[...], terms_buf[...], preferred_element_type=F32
    ).astype(BF16)
    factor_send[64:320, :] = total_buf[...].astype(BF16)
    factors = copy(factor_send, factor_recv, core_sems.at[2], core_sems.at[3], other, vol)
    factors.start()
    factors.wait_recv()
    side.wait_recv()
    factor_sum[0:320, :] = (
        factor_send[...].astype(F32) + factor_recv[...].astype(F32)
    ).astype(BF16)
    factor_sum[320:384, :] = jnp.zeros((64, 256), BF16)
    sides = side_send[...] + side_recv[...]
    pooled_t = sides[:, 0:width]
    outer = sides[:, width : width + HEAD_DIM]

    value_t = lax.dot_general(
        factor_sum[:, 128:256], basis[...], FIRST, preferred_element_type=F32
    )[0:8]
    fill = [jnp.zeros((HEADS, 64 - rows), F32)] if rows < 64 else []
    for d in range(dps):
        part = slice(d * rows, (d + 1) * rows)
        top = jnp.concatenate([value_t[:, part]] + fill + [outer], axis=1)
        low = jnp.concatenate([mixed, pooled_t[:, part]] + fill, axis=1)
        tile_send[d] = jnp.where(row < 4, top, pltpu.roll(low, 4, 0))

    def tile_copy(k, slot):
        e = (me + k) % count
        d = e // vols * 2 + core
        return copy(
            tile_send.at[d],
            tile_recv.at[slot],
            tile_sems.at[0, k],
            tile_sems.at[1, slot],
            d,
            e % vols,
        )

    def grad_copy(k, slot):
        e = (me + k) % count
        d = e // vols * 2 + core
        return copy(
            grad_send.at[d],
            grad_recv.at[slot],
            grad_sems.at[0, k],
            grad_sems.at[1, slot],
            d,
            e % vols,
        )

    each(count // 2, count, lambda k: tile_copy(k, me).start())
    each(1, count // 2, lambda k: tile_copy(k, me).start())
    grad_send[...] = (
        jnp.dot(basis_t[...], factor_sum[:, 0:128], preferred_element_type=F32)
        .astype(BF16)
        .reshape(dps, rows, 128)
    )
    each(count // 2, count, lambda k: grad_copy(k, me).start())
    each(1, count // 2, lambda k: grad_copy(k, me).start())
    grad_recv[me] = grad_send[dp]
    tile_recv[me] = tile_send[dp]

    each(1, count, lambda k: tile_copy(k, (me + count - k) % count).wait_recv())

    outers = []
    for h in range(HEADS):
        senders = senders_of(dps, vols, h)
        tile = tile_recv[senders[0]]
        for s in senders[1:]:
            tile = tile + tile_recv[s]
        outers.append(tile[:, 64:128])
    pooled_sum = pltpu.roll(jnp.sum(tile_recv[...], axis=0), 4, 0)
    branch = lax.dot_general(
        jnp.concatenate(outers, axis=1),
        project_out[...].astype(F32),
        LAST,
        precision=HIGHEST,
        preferred_element_type=F32,
    )
    fill = [jnp.zeros((HEADS, 64 - rows), F32)] if rows < 64 else []
    pooled_sum = pooled_sum + jnp.concatenate(
        [jnp.zeros((HEADS, 64), F32), branch] + fill, axis=1
    )
    head_send[...] = pooled_sum

    def head_copy(k, slot):
        to = (chip + k) % chips
        return copy(
            head_send,
            head_out.at[core, slot],
            head_sems.at[0, k],
            head_sems.at[1, slot],
            to * 2 + core,
            vol,
        )

    each(1, chips, lambda k: head_copy(k, chip).start())
    head_out[core, chip] = pooled_sum

    for h in range(HEADS):
        senders = senders_of(dps, vols, h)
        tile = tile_recv[senders[0]]
        mixed_h = jnp.where(row < 4, pltpu.roll(tile, 4, 0), 0.0)[:, 0:64]
        for s in senders[1:]:
            tile = tile + tile_recv[s]
        tile = jnp.where(row < 4, tile, 0.0)
        value_out[:, h * 64 : h * 64 + 64] = (
            lax.dot_general(
                tile[:, 0:rows], mixed_h, FIRST, precision=HIGHEST, preferred_element_type=F32
            )
            / PATCHES
        )
        value_out[:, 512 + h * 64 : 576 + h * 64] = jnp.dot(
            head_own, tile[:, 64:128], precision=HIGHEST, preferred_element_type=F32
        )

    each(1, chips, lambda k: head_copy(k, (chip + chips - k) % chips).wait_recv())
    heads = copy(
        head_out.at[core], head_out.at[core], core_sems.at[4], core_sems.at[5], other, vol
    )
    heads.start()

    each(1, count, lambda k: grad_copy(k, (me + count - k) % count).wait_recv())
    copy(
        head_out.at[1 - core], head_out.at[1 - core], core_sems.at[4], core_sems.at[5], other, vol
    ).wait_recv()

    each(1, 5, lambda k: patch_copy(k, head).wait_send())
    each(1, 4, lambda k: patch_relay(k).wait_send())
    each(1, chips, lambda k: weight_copy(k, dp).wait_send())
    each(0, chips, lambda at: weight_relay(at).wait_send())
    each(1, vols, lambda k: line_copy(k, vol).wait_send())
    each(1, HEADS, lambda k: small_copy(k, head).wait_send())
    side.wait_send()
    factors.wait_send()
    each(1, count, lambda k: tile_copy(k, me).wait_send())
    each(1, count, lambda k: grad_copy(k, me).wait_send())
    each(1, chips, lambda k: head_copy(k, chip).wait_send())
    heads.wait_send()


def senders_of(dps, vols, h):
    return [
        (z * 4 + h // 2) * vols + v * 2 + h % 2 for z in range(dps // 8) for v in range(vols // 2)
    ]


def finish(dps, vols, errors, grads, values, heads, errors_out, in_out, out_out, head_out):
    rows = values.shape[0]
    for h in range(HEADS):
        senders = senders_of(dps, vols, h)
        both = grads[senders[0]].astype(F32)
        for s in senders[1:]:
            both = both + grads[s].astype(F32)
        in_out[:, h * 64 : h * 64 + 64] = both[:, 64:128]
        in_out[:, 512 + h * 64 : 576 + h * 64] = both[:, 0:64]
    in_out[:, 1024:1536] = values[:, 0:512]
    out_out[...] = values[:, 512:1024]
    errors_out[...] = errors[0:1, 0:K]
    for d in range(dps):
        head_out[:, d * rows : (d + 1) * rows] = heads[d % 2, d // 2][0:K, 64 : 64 + rows]


def constants():
    freq = np.arange(PIX) - PIX // 2
    phase = (freq[:, None] * np.arange(PIX)[None, :] % PIX) * (2.0 * math.pi / PIX)
    cosine, sine = np.cos(phase), np.sin(phase)
    waves = np.stack([cosine, sine, (cosine + sine).T, (cosine - sine).T]).astype(np.float32)
    sel = np.zeros((2 * PIX, PIX), np.float32)
    sel[2 * np.arange(PIX), np.arange(PIX)] = 1.0
    places = np.zeros((PATCH, PIX, PIX), np.float32)
    for r in range(PATCH):
        places[r, np.arange(PIX), r * PATCH + np.arange(PIX) % PATCH] = 1.0
    return waves, sel, places


def local(
    dps,
    vols,
    images,
    contrast,
    volume,
    line_index,
    patch_weight,
    position,
    norm_gain,
    project_in,
    project_out,
    head_weight,
):
    width = norm_gain.shape[0]
    rows = project_in.shape[0]
    chips = dps // 2
    count = chips * vols
    waves, sel, places = constants()
    slab, side, _ = volume.shape
    vmem = pl.BlockSpec(memory_space=pltpu.VMEM)
    hbm = pl.BlockSpec(memory_space=pltpu.HBM)
    inputs = (
        images,
        contrast,
        patch_weight,
        position,
        norm_gain.reshape(1, width),
        project_in,
        project_out,
        head_weight.T,
        jnp.asarray(waves),
        jnp.asarray(sel, BF16),
        jnp.asarray(places, BF16),
    )
    errors, grads, values, heads = pl.pallas_call(
        functools.partial(step, dps, vols),
        out_shape=(
            jax.ShapeDtypeStruct((8, 128), F32),
            jax.ShapeDtypeStruct((count, rows, 128), BF16),
            jax.ShapeDtypeStruct((rows, 1024), F32),
            jax.ShapeDtypeStruct((2, chips, 8, 128), F32),
        ),
        in_specs=[hbm] * (2 + len(inputs)),
        out_specs=(vmem,) * 4,
        scratch_shapes=[
            pltpu.SMEM(line_index.shape, jnp.int32),
            pltpu.VMEM(line_index.shape, jnp.int32),
        ]
        + [pltpu.VMEM(one.shape, one.dtype) for one in inputs]
        + [
            pltpu.VMEM((slab * (side // 16), 16, side), BF16),
            pltpu.VMEM((vols + 1, K * PIX, PIX), BF16),
            pltpu.VMEM((PATCHES // 2, 128), BF16),
            pltpu.VMEM((4, rows + rows // 2 + 16, 128), BF16),
            pltpu.VMEM((128, 8), F32),
            pltpu.VMEM((vols, K * PIX, PIX), BF16),
            pltpu.VMEM((HEADS, PATCHES // 2, 128), BF16),
            pltpu.VMEM((dps, rows + rows // 2 + 16, 128), BF16),
            pltpu.VMEM((384, width), BF16),
            pltpu.VMEM((width, 384), BF16),
            pltpu.VMEM((320, 64), F32),
            pltpu.VMEM((PATCHES, 1), F32),
            pltpu.VMEM((HEADS, PATCHES, 128), BF16),
            pltpu.VMEM((64, HEADS * PATCHES), BF16),
            pltpu.VMEM((HEADS, PATCHES, 128), F32),
            pltpu.VMEM((HEADS, PATCHES, PATCHES), BF16),
            pltpu.VMEM((HEADS, PATCHES, 256), BF16),
            pltpu.VMEM((HEADS, PATCHES, 128), F32),
            pltpu.VMEM((HEADS, 128), F32),
            pltpu.VMEM((HEADS, 128), F32),
            pltpu.VMEM((HEADS, HEADS, 128), F32),
            pltpu.VMEM((HEADS, 128), F32),
            pltpu.VMEM((HEADS, 128), F32),
            pltpu.VMEM((HEADS * PATCHES, 256), BF16),
            pltpu.VMEM((PATCHES, 256), F32),
            pltpu.VMEM((320, 256), BF16),
            pltpu.VMEM((320, 256), BF16),
            pltpu.VMEM((384, 256), BF16),
            pltpu.VMEM((8, width + 128), F32),
            pltpu.VMEM((8, width + 128), F32),
            pltpu.VMEM((dps, rows, 128), BF16),
            pltpu.VMEM((dps, 8, 128), F32),
            pltpu.VMEM((count, 8, 128), F32),
            pltpu.VMEM((8, 128), F32),
            pltpu.SemaphoreType.DMA((14,)),
            pltpu.SemaphoreType.DMA((2, vols)),
            pltpu.SemaphoreType.DMA((2, HEADS)),
            pltpu.SemaphoreType.DMA((2, dps)),
            pltpu.SemaphoreType.DMA((chips,)),
            pltpu.SemaphoreType.DMA((2, HEADS)),
            pltpu.SemaphoreType.DMA((6,)),
            pltpu.SemaphoreType.DMA((2, count)),
            pltpu.SemaphoreType.DMA((2, count)),
            pltpu.SemaphoreType.DMA((2, chips)),
        ],
        compiler_params=pltpu.CompilerParams(
            collective_id=0, has_side_effects=True, vmem_limit_bytes=56 * 1024 * 1024
        ),
        name="pose_step",
    )(line_index, volume.reshape(slab * (side // 16), 16, side), *inputs)
    errors, in_grad, out_grad, head_grad = pl.pallas_call(
        functools.partial(finish, dps, vols),
        out_shape=(
            jax.ShapeDtypeStruct((1, K), F32),
            jax.ShapeDtypeStruct((rows, 3 * HEADS * HEAD_DIM), F32),
            jax.ShapeDtypeStruct((rows, HEADS * HEAD_DIM), F32),
            jax.ShapeDtypeStruct((K, width), F32),
        ),
        in_specs=[vmem] * 4,
        out_specs=(vmem,) * 4,
        name="finish",
    )(errors, grads, values, heads)
    return errors, in_grad, out_grad, head_grad.T


def solution(mesh):
    placed = (
        P(("dp", "vol"), None, None),
        P(("dp", "vol"), None, None),
        P("vol", None, None),
        P("dp", None, None),
        P(),
        P(),
        P(),
        P("dp", None),
        P("dp", None),
        P(),
    )
    return jax.shard_map(
        functools.partial(local, mesh.shape["dp"], mesh.shape["vol"]),
        mesh=mesh,
        in_specs=placed,
        out_specs=(P(("dp", "vol"), None), P("dp", None), P("dp", None), P()),
        check_vma=False,
    )
```

```python
import functools
import math

import jax
import jax.numpy as jnp
import numpy as np
from jax import lax
from jax.experimental import pallas as pl
from jax.experimental.pallas import tpu as pltpu
from jax.sharding import PartitionSpec as P

HEADS = 8
HEAD_DIM = 64
PIX = 128
PATCH = 8
PATCHES = 256
K = 4
EPSILON = 1e-05
F32 = jnp.float32
BF16 = jnp.bfloat16
HIGHEST = lax.Precision.HIGHEST
FIRST = (((0,), (0,)), ((), ()))
LAST = (((1,), (1,)), ((), ()))
MESH = pl.DeviceIdType.MESH


def step(
    dps,
    vols,
    index_hbm,
    volume,
    image_hbm,
    contrast_hbm,
    patch_weight_hbm,
    position_hbm,
    gain_hbm,
    project_in_hbm,
    project_out_hbm,
    head_hbm,
    waves_hbm,
    sel_hbm,
    places_hbm,
    errors_out,
    grad_recv,
    value_out,
    head_out,
    spots,
    index,
    image,
    contrast,
    patch_weight,
    position,
    gain,
    project_in,
    project_out,
    head_weight,
    waves,
    sel,
    places,
    slab_buf,
    picked,
    patches,
    pieces,
    head_wide,
    lines,
    patch_buf,
    weight,
    basis,
    basis_t,
    gram,
    square,
    tokens,
    tokens_t,
    scales,
    attention,
    triple,
    column,
    mean_att,
    small_send,
    small_recv,
    pulled_buf,
    terms_buf,
    total_buf,
    factor_send,
    factor_recv,
    factor_sum,
    side_send,
    side_recv,
    grad_send,
    tile_send,
    tile_recv,
    head_send,
    in_sems,
    line_sems,
    patch_sems,
    weight_sems,
    relay_sems,
    small_sems,
    core_sems,
    grad_sems,
    tile_sems,
    head_sems,
):
    dp = lax.axis_index("dp")
    vol = lax.axis_index("vol")
    core = dp % 2
    chip = dp // 2
    chips = dps // 2
    count = chips * vols
    me = chip * vols + vol
    pair = vol % 2
    head = (chip % 4) * 2 + pair
    rows = project_in.shape[0]
    width = gain.shape[1]
    slab = volume.shape[0]

    def copy(src, dst, send_sem, recv_sem, to_dp, to_vol):
        return pltpu.make_async_remote_copy(
            src_ref=src,
            dst_ref=dst,
            send_sem=send_sem,
            recv_sem=recv_sem,
            device_id=(to_dp, to_vol),
            device_id_type=MESH,
        )

    def each(first, last, body):
        def run(k, c):
            body(k)
            return c

        lax.fori_loop(first, last, run, 0)

    other = dp + 1 - 2 * core
    barrier = pltpu.get_barrier_semaphore()

    def greet(k):
        e = (me + k) % count
        pl.semaphore_signal(
            barrier, inc=1, device_id=(e // vols * 2 + core, e % vols), device_id_type=MESH
        )

    each(count // 2, count, greet)
    each(1, count // 2, greet)
    pl.semaphore_signal(barrier, inc=1, device_id=(other, vol), device_id_type=MESH)

    loads = {}
    for name, src, dst in (
        ("image", image_hbm, image),
        ("places", places_hbm, places),
        ("project_in", project_in_hbm, project_in),
        ("project_out", project_out_hbm, project_out),
        ("index", index_hbm, index),
        ("spots", index_hbm, spots),
        ("sel", sel_hbm, sel),
        ("waves", waves_hbm, waves),
        ("patch_weight", patch_weight_hbm, patch_weight),
        ("position", position_hbm, position),
        ("gain", gain_hbm, gain),
        ("head", head_hbm, head_weight),
        ("contrast", contrast_hbm, contrast),
        ("volume", volume, slab_buf),
    ):
        loads[name] = pltpu.make_async_copy(src, dst, in_sems.at[len(loads)])
        loads[name].start()

    loads["project_in"].wait()
    loads["project_out"].wait()
    loads["head"].wait()
    near = pl.ds(pl.multiple_of(dp * rows // 128 * 128, 128), 128)
    head_wide[...] = jnp.concatenate(
        [head_weight[:, near], jnp.zeros((4, 128), F32)], axis=0
    ).T
    head_own = head_wide[pl.ds(pl.multiple_of(dp * rows % 128, rows), rows), :]
    share = lax.dot_general(
        head_own,
        project_out[...].astype(F32),
        FIRST,
        precision=HIGHEST,
        preferred_element_type=F32,
    )
    for a in range(4):
        parts = [project_in[:, p * 512 + a * 128 : p * 512 + a * 128 + 128] for p in range(3)]
        parts.append(share[:, a * 128 : a * 128 + 128])
        query, key, value, mix = [
            jnp.where(pair == 0, one[:, 0:64], one[:, 64:128]) for one in parts
        ]
        high = mix.astype(BF16)
        mix = jnp.concatenate([high.astype(F32), mix - high.astype(F32)], axis=1)
        pieces[a, 0:rows, :] = jnp.concatenate([query, key], axis=1)
        pieces[a, rows : rows + rows // 2, :] = jnp.concatenate(
            [value[0 : rows // 2], value[rows // 2 : rows]], axis=1
        )
        pieces[a, rows + rows // 2 :, :] = jnp.concatenate(
            [mix, jnp.zeros((8, 128), F32)], axis=0
        ).astype(BF16)
    weight[dp] = pieces[chip % 4]
    loads["image"].wait()
    loads["places"].wait()
    cells = lax.broadcasted_iota(jnp.int32, (16, 16, 128), 1)
    spread_lane = lax.broadcasted_iota(jnp.int32, (16, 16, 128), 2)
    cut = jnp.zeros((PATCHES, 128), F32)
    for r in range(PATCH):
        stripe = image[0, pl.ds(r, 16, stride=PATCH), :]
        stripe = jnp.broadcast_to(stripe[:, None, :], (16, 16, 128))
        stripe = jnp.where(spread_lane // PATCH == cells, stripe, 0.0).reshape(PATCHES, 128)
        cut = cut + jnp.dot(stripe.astype(BF16), places[r], preferred_element_type=F32)
    patches[...] = jnp.concatenate([cut[0:128, 0:64], cut[128:256, 0:64]], axis=1).astype(BF16)
    patch_mean = jnp.sum(cut[:, 0:64], axis=0, keepdims=True) / PATCHES
    loads["patch_weight"].wait()
    loads["position"].wait()
    loads["gain"].wait()
    embed = patch_weight[...].astype(F32)
    embed_c = embed - jnp.mean(embed, axis=1, keepdims=True)
    basis[0:64, :] = (embed_c * gain[...]).astype(BF16)
    gram[0:64, :] = lax.dot_general(
        embed_c, embed_c, LAST, precision=HIGHEST, preferred_element_type=F32
    )
    place_mean = jnp.zeros((1, width), F32)
    for part in range(4):
        one = position[part * 64 : part * 64 + 64, :].astype(F32)
        place_mean = place_mean + jnp.sum(one, axis=0, keepdims=True)
        one = one - jnp.mean(one, axis=1, keepdims=True)
        basis[64 + part * 64 : 128 + part * 64, :] = (one * gain[...]).astype(BF16)
        gram[64 + part * 64 : 128 + part * 64, :] = lax.dot_general(
            one, embed_c, LAST, precision=HIGHEST, preferred_element_type=F32
        )
        square[part * 64 : part * 64 + 64, :] = jnp.sum(one * one, axis=1, keepdims=True)
    basis[320:384, :] = jnp.zeros((64, width), BF16)
    basis_t[...] = basis[...].T
    own_row = (
        jnp.dot(
            jnp.broadcast_to(patch_mean, (8, 64)),
            embed,
            precision=HIGHEST,
            preferred_element_type=F32,
        )
        + place_mean / PATCHES
    )

    head_t = jnp.concatenate([head_weight[...], jnp.zeros((4, width), F32)], axis=0)
    own_logit = lax.dot_general(
        own_row, head_t, LAST, precision=HIGHEST, preferred_element_type=F32
    )
    row = lax.broadcasted_iota(jnp.int32, (HEADS, 128), 0)
    lane = lax.broadcasted_iota(jnp.int32, (HEADS, 128), 1)
    mine = row == head
    own_logit = jnp.where(mine[:, 0:HEADS], own_logit, 0.0)

    loads["waves"].wait()
    pixels = image[0]
    first_cos = jnp.dot(waves[0], pixels, precision=HIGHEST, preferred_element_type=F32)
    first_sin = jnp.dot(waves[1], pixels, precision=HIGHEST, preferred_element_type=F32)
    spectrum = jnp.dot(first_cos, waves[2], precision=HIGHEST, preferred_element_type=F32)
    spectrum = spectrum + jnp.dot(
        first_sin, waves[3], precision=HIGHEST, preferred_element_type=F32
    )
    spectrum = spectrum / PIX

    pl.semaphore_wait(barrier, count)

    def member(m):
        return chip // 4 * 8 + m // 2 * 2 + core, vol // 2 * 2 + m % 2

    def flipped(k):
        low = (head + k) % 2
        mid = (head // 2 + k // 2) % 2
        return (head // 4 + k // 4) % 2 * 4 + mid * 2 + low

    def patch_copy(k, slot):
        to_dp, to_vol = member(flipped(k))
        return copy(
            patches,
            patch_buf.at[slot],
            patch_sems.at[0, k],
            patch_sems.at[1, slot],
            to_dp,
            to_vol,
        )

    def patch_relay(k):
        to_dp, to_vol = member(flipped(k))
        slot = flipped(4)
        return copy(
            patch_buf.at[slot],
            patch_buf.at[slot],
            patch_sems.at[0, 4 + k],
            patch_sems.at[1, slot],
            to_dp,
            to_vol,
        )

    def weight_copy(k, slot):
        to = (chip + k) % chips
        return copy(
            pieces.at[to % 4],
            weight.at[slot],
            weight_sems.at[0, k],
            weight_sems.at[1, slot],
            to * 2 + core,
            vol,
        )

    def weight_relay(at):
        s = at * 2 + core
        return copy(
            weight.at[s], weight.at[s], relay_sems.at[at], weight_sems.at[1, s], other, vol
        )

    def line_copy(k, slot):
        to = (vol + k) % vols
        return copy(picked.at[k], lines.at[slot], line_sems.at[0, k], line_sems.at[1, slot], dp, to)

    patch_copy(4, head).start()
    each(chips // 2, chips, lambda k: weight_copy(k, dp).start())
    each(1, 4, lambda k: patch_copy(k, head).start())
    each(1, chips // 2, lambda k: weight_copy(k, dp).start())
    weight_relay(chip).start()
    patch_buf[head] = patches[...]

    loads["index"].wait()
    loads["spots"].wait()
    loads["sel"].wait()
    loads["volume"].wait()

    def render(step_k, c):
        k = step_k + 1
        v = (vol + k) % vols
        turned = jnp.concatenate([index[v], jnp.zeros((4, 128), jnp.int32)], axis=0)
        turned = turned.astype(F32).T.astype(jnp.int32)
        spot_lane = lax.broadcasted_iota(jnp.int32, (128, 256), 1)
        spot_row = lax.broadcasted_iota(jnp.int32, (128, 256), 0)
        for hyp in range(K):
            line = turned[:, hyp : hyp + 1]
            level = (line >> 4) - vol * slab
            target = jnp.where((level >= 0) & (level < slab), line & 15, 1024)
            hot = jnp.where(spot_lane == (spot_row % 16) * 16 + target, 1.0, 0.0).astype(BF16)
            found = []
            for group in range(8):
                tiles = []
                for i in range(16):
                    spot = spots[v, hyp, group * 16 + i]
                    tiles.append(slab_buf[(spot >> 4) & (slab - 1)])
                tiles = jnp.concatenate(tiles, axis=0)
                found.append(
                    jnp.dot(
                        hot[group * 16 : group * 16 + 16], tiles, preferred_element_type=F32
                    )
                )
            found = jnp.concatenate(found, axis=0).astype(BF16)
            picked[k, hyp * PIX : (hyp + 1) * PIX, :] = jnp.dot(
                found, sel[...], preferred_element_type=F32
            ).astype(BF16)
        @pl.when(k < vols)
        def _():
            line_copy(k, vol).start()

        return c

    lax.fori_loop(0, vols, render, 0)
    lines[vol] = picked[vols]

    def weight_pass(k):
        at = (chip + chips - k) % chips
        weight_copy(k, at * 2 + core).wait_recv()
        weight_relay(at).start()


    first = lax.broadcasted_iota(jnp.int32, (PATCHES // 2, 128), 1) < 64
    high = gram[0:64].astype(BF16)
    gram_parts = jnp.concatenate([high.astype(F32), gram[0:64] - high.astype(F32)], axis=1)
    gram_parts = jnp.concatenate([gram_parts, jnp.zeros((64, 128), F32)], axis=0).astype(BF16)
    gram_places = jnp.concatenate([2.0 * gram[64:320], jnp.zeros((PATCHES, 64), F32)], axis=1)

    def norm(j):
        both = patch_buf[j].astype(F32)
        turned = pltpu.roll(both, 64, 1)
        both = jnp.concatenate(
            [jnp.where(first, both, turned), jnp.where(first, turned, both)], axis=0
        )
        one = both.astype(BF16)
        total = jnp.dot(one, gram_parts, preferred_element_type=F32) + gram_places
        total = jnp.sum(both * total, axis=1, keepdims=True)
        total = jnp.maximum(total + square[...], 0.0) / width
        scale = jnp.broadcast_to(lax.rsqrt(total + EPSILON), (PATCHES, 128))
        return one, one.T[0:64], scale

    def norms(ks):
        for k in ks:
            if k % 4 > 0:
                patch_copy(k, flipped(k)).wait_recv()
        found = [norm(flipped(k)) for k in ks]
        for k, (one, turned, scale) in zip(ks, found):
            j = flipped(k)
            tokens[j] = one
            tokens_t[:, pl.ds(pl.multiple_of(j * PATCHES, PATCHES), PATCHES)] = turned
            scales[j] = scale

    patch_copy(4, flipped(4)).wait_recv()
    each(1, 4, lambda k: patch_relay(k).start())
    norms((0, 4))
    each(1, chips // 2, weight_pass)
    norms((1, 2, 3))
    each(chips // 2, chips, weight_pass)
    norms((5, 6, 7))

    def weight_rest(k):
        s = (chip + chips - k) % chips * 2 + 1 - core
        weight_copy(0, s).wait_recv()

    each(0, chips, weight_rest)

    sides = weight[:, 0:rows, :].reshape(width, 128)
    value = weight[:, rows : rows + rows // 2, :]
    value = jnp.concatenate([value[:, :, 0:64], value[:, :, 64:128]], axis=1)
    half = jnp.where(lax.broadcasted_iota(jnp.int32, (1, 128), 1) < 64, HEAD_DIM ** (-0.5), 1.0)
    sides = jnp.dot(basis[0:320], sides, preferred_element_type=F32) * half
    value = jnp.dot(
        basis[0:320], value.reshape(width, HEAD_DIM), preferred_element_type=F32
    )
    both = jnp.concatenate([sides, value, jnp.zeros((320, 64), F32)], axis=1)
    total_buf[...] = both[64:320]
    turn = jnp.concatenate([both[0:64], jnp.zeros((64, 256), F32)], axis=0).astype(BF16)
    mixed = jnp.sum(weight[:, rows + rows // 2 :, :].astype(F32), axis=0)[0:8]
    mixed = mixed[:, 0:64] + mixed[:, 64:128]

    def forward(j):
        scale = scales[j]
        t = jnp.dot(tokens[j], turn, preferred_element_type=F32) + total_buf[...]
        t = (t * jnp.concatenate([scale, scale], axis=1)).astype(BF16)
        scores = lax.dot_general(t[:, 64:128], t[:, 0:64], LAST, preferred_element_type=F32)
        raised = jnp.exp(scores)
        chosen = (raised * (1.0 / jnp.sum(raised, axis=0, keepdims=True))).astype(BF16)
        col = jnp.sum(chosen.astype(F32), axis=1, keepdims=True)
        mean = jnp.sum(col * t[:, 128:256].astype(F32), axis=0, keepdims=True) / PATCHES
        return t, chosen, col * scale, mean

    def forwards(i):
        found = [forward(8 * i + u) for u in range(8)]
        for u in range(8):
            j = 8 * i + u
            triple[j], attention[j], column[j], mean_att[pl.ds(j, 1), :] = found[u]

    each(0, HEADS // 8, forwards)

    loads["contrast"].wait()
    each(1, vols, lambda k: line_copy(k, (vol + vols - k) % vols).wait_recv())
    slices = lines[0].astype(F32)
    for v in range(1, vols):
        slices = slices + lines[v].astype(F32)
    filt = contrast[0].astype(F32)
    misfits = jnp.zeros((HEADS, 128), F32)
    for k in range(K):
        misfit = filt * slices[k * PIX : (k + 1) * PIX] - spectrum
        value = jnp.sum(jnp.sum(misfit * misfit, axis=0, keepdims=True), axis=1, keepdims=True)
        misfits = jnp.where(lane == k, value / (PIX * PIX), misfits)
    errors_out[...] = misfits
    misfits = jnp.where(mine, pltpu.roll(misfits, 4, 1), 0.0)
    means = mean_att[:, 0:HEAD_DIM]
    logit = own_logit + lax.dot_general(
        means, mixed, LAST, precision=HIGHEST, preferred_element_type=F32
    )
    logit = jnp.where(
        lane < K, jnp.concatenate([logit, jnp.zeros((HEADS, 120), F32)], axis=1), misfits
    )
    small_send[...] = logit

    def small_copy(k, slot):
        to_dp, to_vol = member(flipped(k))
        return copy(
            small_send,
            small_recv.at[slot],
            small_sems.at[0, k],
            small_sems.at[1, slot],
            to_dp,
            to_vol,
        )

    each(1, HEADS, lambda k: small_copy(HEADS - k, head).start())
    small_recv[head] = small_send[...]
    place_lane = lax.broadcasted_iota(jnp.int32, (PATCHES, 128), 1)
    weigh = jnp.zeros((PATCHES, 128), F32)
    for j in range(HEADS):
        weigh = jnp.where(place_lane == j, column[j], weigh)
    weigh = weigh.T[0:HEADS]
    low = weigh.astype(BF16)
    seen = jnp.zeros((HEADS, 128), F32)
    for j in range(HEADS):
        seen = jnp.where(
            row == j, jnp.dot(low, tokens[j], preferred_element_type=F32), seen
        )
    seen = jnp.concatenate([seen[:, 0:64], weigh, jnp.zeros((HEADS, 64), F32)], axis=1)
    weighed = jnp.dot(seen.astype(BF16), basis[...], preferred_element_type=F32)
    each(1, HEADS, lambda k: small_copy(k, flipped(k)).wait_recv())
    summed = jnp.sum(small_recv[...], axis=0)
    misfits = jnp.where(lane < K, pltpu.roll(summed, 124, 1), 0.0)
    raised = jnp.where(lane < K, jnp.exp(summed), 0.0)
    chances = raised / jnp.sum(raised, axis=1, keepdims=True)
    expected = jnp.sum(chances * misfits, axis=1, keepdims=True)
    slope = chances * (misfits - expected)
    pulled = jnp.zeros((HEADS, HEAD_DIM), F32)
    for k in range(K):
        pulled = pulled + slope[:, k : k + 1] * mixed[k : k + 1, :]
    pulled_buf[...] = jnp.concatenate(
        [pulled / PATCHES, jnp.zeros((HEADS, 128 - HEAD_DIM), F32)], axis=1
    )

    slope_t = slope.T[0:8]
    outer = jnp.zeros((HEADS, 128), F32)
    value_t = jnp.zeros((HEADS, width), F32)
    for j in range(HEADS):
        outer = outer + slope_t[:, j : j + 1] * mean_att[j : j + 1, :]
        value_t = value_t + slope_t[:, j : j + 1] * weighed[j : j + 1, :]
    own = jnp.sum(jnp.where(lane[:, 0:HEADS] == head, slope_t, 0.0), axis=1, keepdims=True)
    side_send[0:8, 0:width] = own * own_row
    side_send[0:8, width:] = outer
    side_send[8:16, 0:width] = value_t
    side_send[8:16, width:] = jnp.zeros((8, 128), F32)
    side = copy(side_send, side_recv, core_sems.at[0], core_sems.at[1], other, vol)
    side.start()

    wide = lax.broadcasted_iota(jnp.int32, (PATCHES, 128), 1)

    def backward(j):
        t = triple[j]
        chosen = attention[j]
        wider = chosen.astype(F32)
        up = jnp.sum(
            t[:, 128:256].astype(F32) * pulled_buf[pl.ds(j, 1), :], axis=1, keepdims=True
        )
        center = jnp.sum(wider * up, axis=0, keepdims=True)
        inner = (wider * (up - center)).astype(BF16)
        sides = t[:, 0:128]
        key_slope = jnp.dot(inner, sides, preferred_element_type=F32)
        query_slope = lax.dot_general(inner, sides, FIRST, preferred_element_type=F32)
        scale = scales[j]
        return jnp.where(wide < 64, key_slope, query_slope * HEAD_DIM ** (-0.5)) * scale

    total_buf[...] = jnp.zeros((PATCHES, 256), F32)

    def backwards(i):
        found = [backward(4 * i + u) for u in range(4)]
        total = total_buf[:, 0:128]
        for u in range(4):
            at = pl.multiple_of((4 * i + u) * PATCHES, PATCHES)
            terms_buf[pl.ds(at, PATCHES), :] = found[u].astype(BF16)
            total = total + found[u]
        total_buf[:, 0:128] = total

    each(0, HEADS // 8, backwards)
    side.wait_recv()
    sides = side_send[...] + side_recv[...]
    pooled_t = sides[0:8, 0:width]
    value_t = sides[8:16, 0:width]
    outer = sides[0:8, width : width + HEAD_DIM]

    fill = [jnp.zeros((HEADS, 64 - rows), F32)] if rows < 64 else []
    for d in range(dps):
        part = slice(d * rows, (d + 1) * rows)
        top = jnp.concatenate([value_t[:, part]] + fill + [outer], axis=1)
        low = jnp.concatenate([mixed, pooled_t[:, part]] + fill, axis=1)
        tile_send[d] = jnp.where(row < 4, top, pltpu.roll(low, 4, 0))

    def tile_copy(k, slot):
        e = (me + k) % count
        d = e // vols * 2 + core
        return copy(
            tile_send.at[d],
            tile_recv.at[slot],
            tile_sems.at[0, k],
            tile_sems.at[1, slot],
            d,
            e % vols,
        )

    each(count // 2, count, lambda k: tile_copy(k, me).start())
    each(1, count // 2, lambda k: tile_copy(k, me).start())
    each(HEADS // 8, HEADS // 4, backwards)

    factor_send[0:64, :] = jnp.dot(
        tokens_t[...], terms_buf[...], preferred_element_type=F32
    ).astype(BF16)
    factor_send[64:320, :] = total_buf[:, 0:128].astype(BF16)
    factors = copy(factor_send, factor_recv, core_sems.at[2], core_sems.at[3], other, vol)
    factors.start()
    factors.wait_recv()
    factor_sum[0:320, :] = (
        factor_send[...].astype(F32) + factor_recv[...].astype(F32)
    ).astype(BF16)
    factor_sum[320:384, :] = jnp.zeros((64, 128), BF16)
    def grad_copy(k, slot):
        e = (me + k) % count
        d = e // vols * 2 + core
        return copy(
            grad_send.at[d],
            grad_recv.at[slot],
            grad_sems.at[0, k],
            grad_sems.at[1, slot],
            d,
            e % vols,
        )

    grad_send[...] = (
        jnp.dot(basis_t[...], factor_sum[...], preferred_element_type=F32)
        .astype(BF16)
        .reshape(dps, rows, 128)
    )
    each(count // 2, count, lambda k: grad_copy(k, me).start())
    each(1, count // 2, lambda k: grad_copy(k, me).start())
    grad_recv[me] = grad_send[dp]
    tile_recv[me] = tile_send[dp]

    each(1, count, lambda k: tile_copy(k, (me + count - k) % count).wait_recv())

    outers = []
    for h in range(HEADS):
        senders = senders_of(dps, vols, h)
        tile = tile_recv[senders[0]]
        for s in senders[1:]:
            tile = tile + tile_recv[s]
        outers.append(tile[:, 64:128])
    pooled_sum = pltpu.roll(jnp.sum(tile_recv[...], axis=0), 4, 0)
    branch = lax.dot_general(
        jnp.concatenate(outers, axis=1),
        project_out[...].astype(F32),
        LAST,
        precision=HIGHEST,
        preferred_element_type=F32,
    )
    fill = [jnp.zeros((HEADS, 64 - rows), F32)] if rows < 64 else []
    pooled_sum = pooled_sum + jnp.concatenate(
        [jnp.zeros((HEADS, 64), F32), branch] + fill, axis=1
    )
    head_send[...] = pooled_sum

    def head_copy(k, slot):
        to = (chip + k) % chips
        return copy(
            head_send,
            head_out.at[core, slot],
            head_sems.at[0, k],
            head_sems.at[1, slot],
            to * 2 + core,
            vol,
        )

    each(1, chips, lambda k: head_copy(k, chip).start())
    head_out[core, chip] = pooled_sum

    for h in range(HEADS):
        senders = senders_of(dps, vols, h)
        tile = tile_recv[senders[0]]
        mixed_h = jnp.where(row < 4, pltpu.roll(tile, 4, 0), 0.0)[:, 0:64]
        for s in senders[1:]:
            tile = tile + tile_recv[s]
        tile = jnp.where(row < 4, tile, 0.0)
        value_out[:, h * 64 : h * 64 + 64] = (
            lax.dot_general(
                tile[:, 0:rows], mixed_h, FIRST, precision=HIGHEST, preferred_element_type=F32
            )
            / PATCHES
        )
        value_out[:, 512 + h * 64 : 576 + h * 64] = jnp.dot(
            head_own, tile[:, 64:128], precision=HIGHEST, preferred_element_type=F32
        )

    each(1, chips, lambda k: head_copy(k, (chip + chips - k) % chips).wait_recv())
    heads = copy(
        head_out.at[core], head_out.at[core], core_sems.at[4], core_sems.at[5], other, vol
    )
    heads.start()

    each(1, count, lambda k: grad_copy(k, (me + count - k) % count).wait_recv())
    copy(
        head_out.at[1 - core], head_out.at[1 - core], core_sems.at[4], core_sems.at[5], other, vol
    ).wait_recv()

    each(1, 5, lambda k: patch_copy(k, head).wait_send())
    each(1, 4, lambda k: patch_relay(k).wait_send())
    each(1, chips, lambda k: weight_copy(k, dp).wait_send())
    each(0, chips, lambda at: weight_relay(at).wait_send())
    each(1, vols, lambda k: line_copy(k, vol).wait_send())
    each(1, HEADS, lambda k: small_copy(k, head).wait_send())
    side.wait_send()
    factors.wait_send()
    each(1, count, lambda k: tile_copy(k, me).wait_send())
    each(1, count, lambda k: grad_copy(k, me).wait_send())
    each(1, chips, lambda k: head_copy(k, chip).wait_send())
    heads.wait_send()


def senders_of(dps, vols, h):
    return [
        (z * 4 + h // 2) * vols + v * 2 + h % 2 for z in range(dps // 8) for v in range(vols // 2)
    ]


def finish(dps, vols, errors, grads, values, heads, errors_out, in_out, out_out, head_out):
    rows = values.shape[0]
    for h in range(HEADS):
        senders = senders_of(dps, vols, h)
        both = grads[senders[0]].astype(F32)
        for s in senders[1:]:
            both = both + grads[s].astype(F32)
        in_out[:, h * 64 : h * 64 + 64] = both[:, 64:128]
        in_out[:, 512 + h * 64 : 576 + h * 64] = both[:, 0:64]
    in_out[:, 1024:1536] = values[:, 0:512]
    out_out[...] = values[:, 512:1024]
    errors_out[...] = errors[0:1, 0:K]
    for d in range(dps):
        head_out[:, d * rows : (d + 1) * rows] = heads[d % 2, d // 2][0:K, 64 : 64 + rows]


def constants():
    freq = np.arange(PIX) - PIX // 2
    phase = (freq[:, None] * np.arange(PIX)[None, :] % PIX) * (2.0 * math.pi / PIX)
    cosine, sine = np.cos(phase), np.sin(phase)
    waves = np.stack([cosine, sine, (cosine + sine).T, (cosine - sine).T]).astype(np.float32)
    sel = np.zeros((2 * PIX, PIX), np.float32)
    sel[2 * np.arange(PIX), np.arange(PIX)] = 1.0
    places = np.zeros((PATCH, PIX, PIX), np.float32)
    for r in range(PATCH):
        places[r, np.arange(PIX), r * PATCH + np.arange(PIX) % PATCH] = 1.0
    return waves, sel, places


def local(
    dps,
    vols,
    images,
    contrast,
    volume,
    line_index,
    patch_weight,
    position,
    norm_gain,
    project_in,
    project_out,
    head_weight,
):
    width = norm_gain.shape[0]
    rows = project_in.shape[0]
    chips = dps // 2
    count = chips * vols
    waves, sel, places = constants()
    slab, side, _ = volume.shape
    vmem = pl.BlockSpec(memory_space=pltpu.VMEM)
    hbm = pl.BlockSpec(memory_space=pltpu.HBM)
    inputs = (
        images,
        contrast,
        patch_weight,
        position,
        norm_gain.reshape(1, width),
        project_in,
        project_out,
        head_weight.T,
        jnp.asarray(waves),
        jnp.asarray(sel, BF16),
        jnp.asarray(places, BF16),
    )
    errors, grads, values, heads = pl.pallas_call(
        functools.partial(step, dps, vols),
        out_shape=(
            jax.ShapeDtypeStruct((8, 128), F32),
            jax.ShapeDtypeStruct((count, rows, 128), BF16),
            jax.ShapeDtypeStruct((rows, 1024), F32),
            jax.ShapeDtypeStruct((2, chips, 8, 128), F32),
        ),
        in_specs=[hbm] * (2 + len(inputs)),
        out_specs=(vmem,) * 4,
        scratch_shapes=[
            pltpu.SMEM(line_index.shape, jnp.int32),
            pltpu.VMEM(line_index.shape, jnp.int32),
        ]
        + [pltpu.VMEM(one.shape, one.dtype) for one in inputs]
        + [
            pltpu.VMEM((slab * (side // 16), 16, side), BF16),
            pltpu.VMEM((vols + 1, K * PIX, PIX), BF16),
            pltpu.VMEM((PATCHES // 2, 128), BF16),
            pltpu.VMEM((4, rows + rows // 2 + 16, 128), BF16),
            pltpu.VMEM((128, 8), F32),
            pltpu.VMEM((vols, K * PIX, PIX), BF16),
            pltpu.VMEM((HEADS, PATCHES // 2, 128), BF16),
            pltpu.VMEM((dps, rows + rows // 2 + 16, 128), BF16),
            pltpu.VMEM((384, width), BF16),
            pltpu.VMEM((width, 384), BF16),
            pltpu.VMEM((320, 64), F32),
            pltpu.VMEM((PATCHES, 1), F32),
            pltpu.VMEM((HEADS, PATCHES, 128), BF16),
            pltpu.VMEM((64, HEADS * PATCHES), BF16),
            pltpu.VMEM((HEADS, PATCHES, 128), F32),
            pltpu.VMEM((HEADS, PATCHES, PATCHES), BF16),
            pltpu.VMEM((HEADS, PATCHES, 256), BF16),
            pltpu.VMEM((HEADS, PATCHES, 128), F32),
            pltpu.VMEM((HEADS, 128), F32),
            pltpu.VMEM((HEADS, 128), F32),
            pltpu.VMEM((HEADS, HEADS, 128), F32),
            pltpu.VMEM((HEADS, 128), F32),
            pltpu.VMEM((HEADS * PATCHES, 128), BF16),
            pltpu.VMEM((PATCHES, 256), F32),
            pltpu.VMEM((320, 128), BF16),
            pltpu.VMEM((320, 128), BF16),
            pltpu.VMEM((384, 128), BF16),
            pltpu.VMEM((16, width + 128), F32),
            pltpu.VMEM((16, width + 128), F32),
            pltpu.VMEM((dps, rows, 128), BF16),
            pltpu.VMEM((dps, 8, 128), F32),
            pltpu.VMEM((count, 8, 128), F32),
            pltpu.VMEM((8, 128), F32),
            pltpu.SemaphoreType.DMA((14,)),
            pltpu.SemaphoreType.DMA((2, vols)),
            pltpu.SemaphoreType.DMA((2, HEADS)),
            pltpu.SemaphoreType.DMA((2, dps)),
            pltpu.SemaphoreType.DMA((chips,)),
            pltpu.SemaphoreType.DMA((2, HEADS)),
            pltpu.SemaphoreType.DMA((6,)),
            pltpu.SemaphoreType.DMA((2, count)),
            pltpu.SemaphoreType.DMA((2, count)),
            pltpu.SemaphoreType.DMA((2, chips)),
        ],
        compiler_params=pltpu.CompilerParams(
            collective_id=0, has_side_effects=True, vmem_limit_bytes=56 * 1024 * 1024
        ),
        name="pose_step",
    )(line_index, volume.reshape(slab * (side // 16), 16, side), *inputs)
    errors, in_grad, out_grad, head_grad = pl.pallas_call(
        functools.partial(finish, dps, vols),
        out_shape=(
            jax.ShapeDtypeStruct((1, K), F32),
            jax.ShapeDtypeStruct((rows, 3 * HEADS * HEAD_DIM), F32),
            jax.ShapeDtypeStruct((rows, HEADS * HEAD_DIM), F32),
            jax.ShapeDtypeStruct((K, width), F32),
        ),
        in_specs=[vmem] * 4,
        out_specs=(vmem,) * 4,
        name="finish",
    )(errors, grads, values, heads)
    return errors, in_grad, out_grad, head_grad.T


def solution(mesh):
    placed = (
        P(("dp", "vol"), None, None),
        P(("dp", "vol"), None, None),
        P("vol", None, None),
        P("dp", None, None),
        P(),
        P(),
        P(),
        P("dp", None),
        P("dp", None),
        P(),
    )
    return jax.shard_map(
        functools.partial(local, mesh.shape["dp"], mesh.shape["vol"]),
        mesh=mesh,
        in_specs=placed,
        out_specs=(P(("dp", "vol"), None), P("dp", None), P("dp", None), P()),
        check_vma=False,
    )
```

```python
import functools
import math

import jax
import jax.numpy as jnp
import numpy as np
from jax import lax
from jax.experimental import pallas as pl
from jax.experimental.pallas import tpu as pltpu
from jax.sharding import PartitionSpec as P

HEADS = 8
HEAD_DIM = 64
PIX = 128
PATCH = 8
PATCHES = 256
K = 4
EPSILON = 1e-05
F32 = jnp.float32
BF16 = jnp.bfloat16
HIGHEST = lax.Precision.HIGHEST
FIRST = (((0,), (0,)), ((), ()))
LAST = (((1,), (1,)), ((), ()))
MESH = pl.DeviceIdType.MESH


def step(
    dps,
    vols,
    index_hbm,
    volume,
    image_hbm,
    contrast_hbm,
    patch_weight_hbm,
    position_hbm,
    gain_hbm,
    project_in_hbm,
    project_out_hbm,
    head_hbm,
    waves_hbm,
    sel_hbm,
    places_hbm,
    errors_out,
    grad_recv,
    value_out,
    head_out,
    spots,
    index,
    image,
    contrast,
    patch_weight,
    position,
    gain,
    project_in,
    project_out,
    head_weight,
    waves,
    sel,
    places,
    slab_buf,
    picked,
    patches,
    pieces,
    head_wide,
    lines,
    patch_buf,
    weight,
    basis,
    basis_t,
    gram,
    square,
    tokens,
    tokens_t,
    scales,
    attention,
    triple,
    column,
    mean_att,
    small_send,
    small_recv,
    pulled_buf,
    terms_buf,
    total_buf,
    factor_send,
    factor_recv,
    factor_sum,
    side_send,
    side_recv,
    grad_send,
    tile_send,
    tile_recv,
    head_send,
    in_sems,
    line_sems,
    patch_sems,
    weight_sems,
    relay_sems,
    small_sems,
    core_sems,
    grad_sems,
    tile_sems,
    head_sems,
):
    dp = lax.axis_index("dp")
    vol = lax.axis_index("vol")
    core = dp % 2
    chip = dp // 2
    chips = dps // 2
    count = chips * vols
    me = chip * vols + vol
    pair = vol % 2
    head = (chip % 4) * 2 + pair
    rows = project_in.shape[0]
    width = gain.shape[1]
    slab = volume.shape[0]

    def copy(src, dst, send_sem, recv_sem, to_dp, to_vol):
        return pltpu.make_async_remote_copy(
            src_ref=src,
            dst_ref=dst,
            send_sem=send_sem,
            recv_sem=recv_sem,
            device_id=(to_dp, to_vol),
            device_id_type=MESH,
        )

    def each(first, last, body):
        def run(k, c):
            body(k)
            return c

        lax.fori_loop(first, last, run, 0)

    other = dp + 1 - 2 * core
    barrier = pltpu.get_barrier_semaphore()

    def greet(k):
        e = (me + k) % count
        pl.semaphore_signal(
            barrier, inc=1, device_id=(e // vols * 2 + core, e % vols), device_id_type=MESH
        )

    each(count // 2, count, greet)
    each(1, count // 2, greet)
    pl.semaphore_signal(barrier, inc=1, device_id=(other, vol), device_id_type=MESH)

    loads = {}
    for name, src, dst in (
        ("image", image_hbm, image),
        ("places", places_hbm, places),
        ("project_in", project_in_hbm, project_in),
        ("project_out", project_out_hbm, project_out),
        ("index", index_hbm, index),
        ("spots", index_hbm, spots),
        ("sel", sel_hbm, sel),
        ("waves", waves_hbm, waves),
        ("patch_weight", patch_weight_hbm, patch_weight),
        ("position", position_hbm, position),
        ("gain", gain_hbm, gain),
        ("head", head_hbm, head_weight),
        ("contrast", contrast_hbm, contrast),
        ("volume", volume, slab_buf),
    ):
        loads[name] = pltpu.make_async_copy(src, dst, in_sems.at[len(loads)])
        loads[name].start()

    loads["project_in"].wait()
    loads["project_out"].wait()
    loads["head"].wait()
    near = pl.ds(pl.multiple_of(dp * rows // 128 * 128, 128), 128)
    head_wide[...] = jnp.concatenate(
        [head_weight[:, near], jnp.zeros((4, 128), F32)], axis=0
    ).T
    head_own = head_wide[pl.ds(pl.multiple_of(dp * rows % 128, rows), rows), :]
    share = lax.dot_general(
        head_own,
        project_out[...].astype(F32),
        FIRST,
        precision=HIGHEST,
        preferred_element_type=F32,
    )
    for a in range(4):
        parts = [project_in[:, p * 512 + a * 128 : p * 512 + a * 128 + 128] for p in range(3)]
        parts.append(share[:, a * 128 : a * 128 + 128])
        query, key, value, mix = [
            jnp.where(pair == 0, one[:, 0:64], one[:, 64:128]) for one in parts
        ]
        high = mix.astype(BF16)
        mix = jnp.concatenate([high.astype(F32), mix - high.astype(F32)], axis=1)
        pieces[a, 0:rows, :] = jnp.concatenate([query, key], axis=1)
        pieces[a, rows : rows + rows // 2, :] = jnp.concatenate(
            [value[0 : rows // 2], value[rows // 2 : rows]], axis=1
        )
        pieces[a, rows + rows // 2 :, :] = jnp.concatenate(
            [mix, jnp.zeros((8, 128), F32)], axis=0
        ).astype(BF16)
    weight[dp] = pieces[chip % 4]
    loads["image"].wait()
    loads["places"].wait()
    cells = lax.broadcasted_iota(jnp.int32, (16, 16, 128), 1)
    spread_lane = lax.broadcasted_iota(jnp.int32, (16, 16, 128), 2)
    cut = jnp.zeros((PATCHES, 128), F32)
    for r in range(PATCH):
        stripe = image[0, pl.ds(r, 16, stride=PATCH), :]
        stripe = jnp.broadcast_to(stripe[:, None, :], (16, 16, 128))
        stripe = jnp.where(spread_lane // PATCH == cells, stripe, 0.0).reshape(PATCHES, 128)
        cut = cut + jnp.dot(stripe.astype(BF16), places[r], preferred_element_type=F32)
    patches[...] = jnp.concatenate([cut[0:128, 0:64], cut[128:256, 0:64]], axis=1).astype(BF16)
    patch_mean = jnp.sum(cut[:, 0:64], axis=0, keepdims=True) / PATCHES
    loads["patch_weight"].wait()
    loads["position"].wait()
    loads["gain"].wait()
    embed = patch_weight[...].astype(F32)
    embed_c = embed - jnp.mean(embed, axis=1, keepdims=True)
    basis[0:64, :] = (embed_c * gain[...]).astype(BF16)
    gram[0:64, :] = lax.dot_general(
        embed_c, embed_c, LAST, precision=HIGHEST, preferred_element_type=F32
    )
    place_mean = jnp.zeros((1, width), F32)
    for part in range(4):
        one = position[part * 64 : part * 64 + 64, :].astype(F32)
        place_mean = place_mean + jnp.sum(one, axis=0, keepdims=True)
        one = one - jnp.mean(one, axis=1, keepdims=True)
        basis[64 + part * 64 : 128 + part * 64, :] = (one * gain[...]).astype(BF16)
        gram[64 + part * 64 : 128 + part * 64, :] = lax.dot_general(
            one, embed_c, LAST, precision=HIGHEST, preferred_element_type=F32
        )
        square[part * 64 : part * 64 + 64, :] = jnp.sum(one * one, axis=1, keepdims=True)
    basis[320:384, :] = jnp.zeros((64, width), BF16)
    basis_t[...] = basis[...].T
    own_row = (
        jnp.dot(
            jnp.broadcast_to(patch_mean, (8, 64)),
            embed,
            precision=HIGHEST,
            preferred_element_type=F32,
        )
        + place_mean / PATCHES
    )

    head_t = jnp.concatenate([head_weight[...], jnp.zeros((4, width), F32)], axis=0)
    own_logit = lax.dot_general(
        own_row, head_t, LAST, precision=HIGHEST, preferred_element_type=F32
    )
    row = lax.broadcasted_iota(jnp.int32, (HEADS, 128), 0)
    lane = lax.broadcasted_iota(jnp.int32, (HEADS, 128), 1)
    mine = row == head
    own_logit = jnp.where(mine[:, 0:HEADS], own_logit, 0.0)

    loads["waves"].wait()
    pixels = image[0]
    first_cos = jnp.dot(waves[0], pixels, precision=HIGHEST, preferred_element_type=F32)
    first_sin = jnp.dot(waves[1], pixels, precision=HIGHEST, preferred_element_type=F32)
    spectrum = jnp.dot(first_cos, waves[2], precision=HIGHEST, preferred_element_type=F32)
    spectrum = spectrum + jnp.dot(
        first_sin, waves[3], precision=HIGHEST, preferred_element_type=F32
    )
    spectrum = spectrum / PIX

    pl.semaphore_wait(barrier, count)

    def member(m):
        return chip // 4 * 8 + m // 2 * 2 + core, vol // 2 * 2 + m % 2

    def flipped(k):
        low = (head + k) % 2
        mid = (head // 2 + k // 2) % 2
        return (head // 4 + k // 4) % 2 * 4 + mid * 2 + low

    def patch_copy(k, slot):
        to_dp, to_vol = member(flipped(k))
        return copy(
            patches,
            patch_buf.at[slot],
            patch_sems.at[0, k],
            patch_sems.at[1, slot],
            to_dp,
            to_vol,
        )

    def patch_relay(k):
        to_dp, to_vol = member(flipped(k))
        slot = flipped(4)
        return copy(
            patch_buf.at[slot],
            patch_buf.at[slot],
            patch_sems.at[0, 4 + k],
            patch_sems.at[1, slot],
            to_dp,
            to_vol,
        )

    def weight_copy(k, slot):
        to = (chip + k) % chips
        return copy(
            pieces.at[to % 4],
            weight.at[slot],
            weight_sems.at[0, k],
            weight_sems.at[1, slot],
            to * 2 + core,
            vol,
        )

    def weight_relay(at):
        s = at * 2 + core
        return copy(
            weight.at[s], weight.at[s], relay_sems.at[at], weight_sems.at[1, s], other, vol
        )

    def line_copy(k, slot):
        to = (vol + k) % vols
        return copy(picked.at[k], lines.at[slot], line_sems.at[0, k], line_sems.at[1, slot], dp, to)

    patch_copy(4, head).start()
    each(chips // 2, chips, lambda k: weight_copy(k, dp).start())
    each(1, 4, lambda k: patch_copy(k, head).start())
    each(1, chips // 2, lambda k: weight_copy(k, dp).start())
    weight_relay(chip).start()
    patch_buf[head] = patches[...]

    loads["index"].wait()
    loads["spots"].wait()
    loads["sel"].wait()
    loads["volume"].wait()

    def render(step_k, c):
        k = step_k + 1
        v = (vol + k) % vols
        turned = jnp.concatenate([index[v], jnp.zeros((4, 128), jnp.int32)], axis=0)
        turned = turned.astype(F32).T.astype(jnp.int32)
        spot_lane = lax.broadcasted_iota(jnp.int32, (128, 256), 1)
        spot_row = lax.broadcasted_iota(jnp.int32, (128, 256), 0)
        for hyp in range(K):
            line = turned[:, hyp : hyp + 1]
            level = (line >> 4) - vol * slab
            target = jnp.where((level >= 0) & (level < slab), line & 15, 1024)
            hot = jnp.where(spot_lane == (spot_row % 16) * 16 + target, 1.0, 0.0).astype(BF16)
            found = []
            for group in range(8):
                tiles = []
                for i in range(16):
                    spot = spots[v, hyp, group * 16 + i]
                    tiles.append(slab_buf[(spot >> 4) & (slab - 1)])
                tiles = jnp.concatenate(tiles, axis=0)
                found.append(
                    jnp.dot(
                        hot[group * 16 : group * 16 + 16], tiles, preferred_element_type=F32
                    )
                )
            found = jnp.concatenate(found, axis=0).astype(BF16)
            picked[k, hyp * PIX : (hyp + 1) * PIX, :] = jnp.dot(
                found, sel[...], preferred_element_type=F32
            ).astype(BF16)
        @pl.when(k < vols)
        def _():
            line_copy(k, vol).start()

        return c

    lax.fori_loop(0, vols, render, 0)
    lines[vol] = picked[vols]

    def weight_pass(k):
        at = (chip + chips - k) % chips
        weight_copy(k, at * 2 + core).wait_recv()
        weight_relay(at).start()


    first = lax.broadcasted_iota(jnp.int32, (PATCHES // 2, 128), 1) < 64
    high = gram[0:64].astype(BF16)
    gram_parts = jnp.concatenate([high.astype(F32), gram[0:64] - high.astype(F32)], axis=1)
    gram_parts = jnp.concatenate([gram_parts, jnp.zeros((64, 128), F32)], axis=0).astype(BF16)
    gram_places = jnp.concatenate([2.0 * gram[64:320], jnp.zeros((PATCHES, 64), F32)], axis=1)

    def norm(j):
        both = patch_buf[j].astype(F32)
        turned = pltpu.roll(both, 64, 1)
        both = jnp.concatenate(
            [jnp.where(first, both, turned), jnp.where(first, turned, both)], axis=0
        )
        one = both.astype(BF16)
        total = jnp.dot(one, gram_parts, preferred_element_type=F32) + gram_places
        total = jnp.sum(both * total, axis=1, keepdims=True)
        total = jnp.maximum(total + square[...], 0.0) / width
        scale = jnp.broadcast_to(lax.rsqrt(total + EPSILON), (PATCHES, 128))
        return one, one.T[0:64], scale

    def norms(ks):
        for k in ks:
            if k % 4 > 0:
                patch_copy(k, flipped(k)).wait_recv()
        found = [norm(flipped(k)) for k in ks]
        for k, (one, turned, scale) in zip(ks, found):
            j = flipped(k)
            tokens[j] = one
            tokens_t[:, pl.ds(pl.multiple_of(j * PATCHES, PATCHES), PATCHES)] = turned
            scales[j] = scale

    patch_copy(4, flipped(4)).wait_recv()
    each(1, 4, lambda k: patch_relay(k).start())
    norms((0, 4))
    each(1, chips // 2, weight_pass)
    norms((1, 2, 3))
    each(chips // 2, chips, weight_pass)
    norms((5, 6, 7))

    def weight_rest(k):
        s = (chip + chips - k) % chips * 2 + 1 - core
        weight_copy(0, s).wait_recv()

    each(0, chips, weight_rest)

    sides = weight[:, 0:rows, :].reshape(width, 128)
    value = weight[:, rows : rows + rows // 2, :]
    value = jnp.concatenate([value[:, :, 0:64], value[:, :, 64:128]], axis=1)
    half = jnp.where(lax.broadcasted_iota(jnp.int32, (1, 128), 1) < 64, HEAD_DIM ** (-0.5), 1.0)
    sides = jnp.dot(basis[0:320], sides, preferred_element_type=F32) * half
    value = jnp.dot(
        basis[0:320], value.reshape(width, HEAD_DIM), preferred_element_type=F32
    )
    both = jnp.concatenate([sides, value, jnp.zeros((320, 64), F32)], axis=1)
    total_buf[...] = both[64:320]
    turn = jnp.concatenate([both[0:64], jnp.zeros((64, 256), F32)], axis=0).astype(BF16)
    mixed = jnp.sum(weight[:, rows + rows // 2 :, :].astype(F32), axis=0)[0:8]
    mixed = mixed[:, 0:64] + mixed[:, 64:128]

    def forward(j):
        scale = scales[j]
        t = jnp.dot(tokens[j], turn, preferred_element_type=F32) + total_buf[...]
        t = (t * jnp.concatenate([scale, scale], axis=1)).astype(BF16)
        scores = lax.dot_general(t[:, 64:128], t[:, 0:64], LAST, preferred_element_type=F32)
        raised = jnp.exp(scores)
        chosen = (raised * (1.0 / jnp.sum(raised, axis=0, keepdims=True))).astype(BF16)
        col = jnp.sum(chosen.astype(F32), axis=1, keepdims=True)
        mean = jnp.sum(col * t[:, 128:256].astype(F32), axis=0, keepdims=True) / PATCHES
        return t, chosen, col * scale, mean

    def forwards(i):
        found = [forward(8 * i + u) for u in range(8)]
        for u in range(8):
            j = 8 * i + u
            triple[j], attention[j], column[j], mean_att[pl.ds(j, 1), :] = found[u]

    each(0, HEADS // 8, forwards)

    loads["contrast"].wait()
    each(1, vols, lambda k: line_copy(k, (vol + vols - k) % vols).wait_recv())
    slices = lines[0].astype(F32)
    for v in range(1, vols):
        slices = slices + lines[v].astype(F32)
    filt = contrast[0].astype(F32)
    misfits = jnp.zeros((HEADS, 128), F32)
    for k in range(K):
        misfit = filt * slices[k * PIX : (k + 1) * PIX] - spectrum
        value = jnp.sum(jnp.sum(misfit * misfit, axis=0, keepdims=True), axis=1, keepdims=True)
        misfits = jnp.where(lane == k, value / (PIX * PIX), misfits)
    errors_out[...] = misfits
    misfits = jnp.where(mine, pltpu.roll(misfits, 4, 1), 0.0)
    means = mean_att[:, 0:HEAD_DIM]
    logit = own_logit + lax.dot_general(
        means, mixed, LAST, precision=HIGHEST, preferred_element_type=F32
    )
    logit = jnp.where(
        lane < K, jnp.concatenate([logit, jnp.zeros((HEADS, 120), F32)], axis=1), misfits
    )
    small_send[...] = logit

    def small_copy(k, slot):
        to_dp, to_vol = member(flipped(k))
        return copy(
            small_send,
            small_recv.at[slot],
            small_sems.at[0, k],
            small_sems.at[1, slot],
            to_dp,
            to_vol,
        )

    each(1, HEADS, lambda k: small_copy(HEADS - k, head).start())
    small_recv[head] = small_send[...]
    place_lane = lax.broadcasted_iota(jnp.int32, (PATCHES, 128), 1)
    weigh = jnp.zeros((PATCHES, 128), F32)
    for j in range(HEADS):
        weigh = jnp.where(place_lane == j, column[j], weigh)
    weigh = weigh.T[0:HEADS]
    low = weigh.astype(BF16)
    seen = jnp.zeros((HEADS, 128), F32)
    for j in range(HEADS):
        seen = jnp.where(
            row == j, jnp.dot(low, tokens[j], preferred_element_type=F32), seen
        )
    seen = jnp.concatenate([seen[:, 0:64], weigh, jnp.zeros((HEADS, 64), F32)], axis=1)
    weighed = jnp.dot(seen.astype(BF16), basis[...], preferred_element_type=F32)
    each(1, HEADS, lambda k: small_copy(k, flipped(k)).wait_recv())
    summed = jnp.sum(small_recv[...], axis=0)
    misfits = jnp.where(lane < K, pltpu.roll(summed, 124, 1), 0.0)
    raised = jnp.where(lane < K, jnp.exp(summed), 0.0)
    chances = raised / jnp.sum(raised, axis=1, keepdims=True)
    expected = jnp.sum(chances * misfits, axis=1, keepdims=True)
    slope = chances * (misfits - expected)
    pulled = jnp.zeros((HEADS, HEAD_DIM), F32)
    for k in range(K):
        pulled = pulled + slope[:, k : k + 1] * mixed[k : k + 1, :]
    pulled_buf[...] = jnp.concatenate(
        [pulled / PATCHES, jnp.zeros((HEADS, 128 - HEAD_DIM), F32)], axis=1
    )

    slope_t = slope.T[0:8]
    outer = jnp.zeros((HEADS, 128), F32)
    value_t = jnp.zeros((HEADS, width), F32)
    for j in range(HEADS):
        outer = outer + slope_t[:, j : j + 1] * mean_att[j : j + 1, :]
        value_t = value_t + slope_t[:, j : j + 1] * weighed[j : j + 1, :]
    own = jnp.sum(jnp.where(lane[:, 0:HEADS] == head, slope_t, 0.0), axis=1, keepdims=True)
    side_send[0:8, 0:width] = own * own_row
    side_send[0:8, width:] = outer
    side_send[8:16, 0:width] = value_t
    side_send[8:16, width:] = jnp.zeros((8, 128), F32)
    side = copy(side_send, side_recv, core_sems.at[0], core_sems.at[1], other, vol)
    side.start()

    wide = lax.broadcasted_iota(jnp.int32, (PATCHES, 128), 1)

    def backward(j):
        t = triple[j]
        chosen = attention[j]
        wider = chosen.astype(F32)
        up = jnp.sum(
            t[:, 128:256].astype(F32) * pulled_buf[pl.ds(j, 1), :], axis=1, keepdims=True
        )
        center = jnp.sum(wider * up, axis=0, keepdims=True)
        inner = (wider * (up - center)).astype(BF16)
        sides = t[:, 0:128]
        key_slope = jnp.dot(inner, sides, preferred_element_type=F32)
        query_slope = lax.dot_general(inner, sides, FIRST, preferred_element_type=F32)
        scale = scales[j]
        return jnp.where(wide < 64, key_slope, query_slope * HEAD_DIM ** (-0.5)) * scale

    total_buf[...] = jnp.zeros((PATCHES, 256), F32)

    def backwards(i):
        found = [backward(4 * i + u) for u in range(4)]
        total = total_buf[:, 0:128]
        for u in range(4):
            at = pl.multiple_of((4 * i + u) * PATCHES, PATCHES)
            terms_buf[pl.ds(at, PATCHES), :] = found[u].astype(BF16)
            total = total + found[u]
        total_buf[:, 0:128] = total

    each(0, HEADS // 8, backwards)
    side.wait_recv()
    sides = side_send[...] + side_recv[...]
    pooled_t = sides[0:8, 0:width]
    value_t = sides[8:16, 0:width]
    outer = sides[0:8, width : width + HEAD_DIM]

    fill = [jnp.zeros((HEADS, 64 - rows), F32)] if rows < 64 else []
    for d in range(dps):
        part = slice(d * rows, (d + 1) * rows)
        top = jnp.concatenate([value_t[:, part]] + fill + [outer], axis=1)
        low = jnp.concatenate([mixed, pooled_t[:, part]] + fill, axis=1)
        tile_send[d] = jnp.where(row < 4, top, pltpu.roll(low, 4, 0))

    def tile_copy(k, slot):
        e = (me + k) % count
        d = e // vols * 2 + core
        return copy(
            tile_send.at[d],
            tile_recv.at[slot],
            tile_sems.at[0, k],
            tile_sems.at[1, slot],
            d,
            e % vols,
        )

    each(count // 2, count, lambda k: tile_copy(k, me).start())
    each(1, count // 2, lambda k: tile_copy(k, me).start())
    each(HEADS // 8, HEADS // 4, backwards)

    factor_send[0:64, :] = jnp.dot(
        tokens_t[...], terms_buf[...], preferred_element_type=F32
    ).astype(BF16)
    factor_send[64:320, :] = total_buf[:, 0:128].astype(BF16)
    factors = copy(factor_send, factor_recv, core_sems.at[2], core_sems.at[3], other, vol)
    factors.start()
    factors.wait_recv()
    factor_sum[0:320, :] = (
        factor_send[...].astype(F32) + factor_recv[...].astype(F32)
    ).astype(BF16)
    factor_sum[320:384, :] = jnp.zeros((64, 128), BF16)
    def grad_copy(k, slot):
        e = (me + k) % count
        d = e // vols * 2 + core
        return copy(
            grad_send.at[e // vols],
            grad_recv.at[slot],
            grad_sems.at[0, k],
            grad_sems.at[1, slot],
            d,
            e % vols,
        )

    found = [
        basis_t[pl.ds(pl.multiple_of((2 * i + core) * rows, rows), rows), :] for i in range(chips)
    ]
    grad_send[...] = (
        jnp.dot(jnp.concatenate(found, axis=0), factor_sum[...], preferred_element_type=F32)
        .astype(BF16)
        .reshape(chips, rows, 128)
    )
    each(count // 2, count, lambda k: grad_copy(k, me).start())
    each(1, count // 2, lambda k: grad_copy(k, me).start())
    grad_recv[me] = grad_send[chip]
    each(1, 5, lambda k: patch_copy(k, head).wait_send())
    each(1, 4, lambda k: patch_relay(k).wait_send())
    each(1, chips, lambda k: weight_copy(k, dp).wait_send())
    each(0, chips, lambda at: weight_relay(at).wait_send())
    each(1, vols, lambda k: line_copy(k, vol).wait_send())
    each(1, HEADS, lambda k: small_copy(k, head).wait_send())
    side.wait_send()
    factors.wait_send()
    each(1, count, lambda k: tile_copy(k, me).wait_send())
    tile_recv[me] = tile_send[dp]

    each(1, count, lambda k: tile_copy(k, (me + count - k) % count).wait_recv())

    outers = []
    for h in range(HEADS):
        senders = senders_of(dps, vols, h)
        tile = tile_recv[senders[0]]
        for s in senders[1:]:
            tile = tile + tile_recv[s]
        outers.append(tile[:, 64:128])
    pooled_sum = pltpu.roll(jnp.sum(tile_recv[...], axis=0), 4, 0)
    branch = lax.dot_general(
        jnp.concatenate(outers, axis=1),
        project_out[...].astype(F32),
        LAST,
        precision=HIGHEST,
        preferred_element_type=F32,
    )
    fill = [jnp.zeros((HEADS, 64 - rows), F32)] if rows < 64 else []
    pooled_sum = pooled_sum + jnp.concatenate(
        [jnp.zeros((HEADS, 64), F32), branch] + fill, axis=1
    )
    head_send[...] = pooled_sum

    def head_copy(k, slot):
        to = (chip + k) % chips
        return copy(
            head_send,
            head_out.at[core, slot],
            head_sems.at[0, k],
            head_sems.at[1, slot],
            to * 2 + core,
            vol,
        )

    each(1, chips, lambda k: head_copy(k, chip).start())
    head_out[core, chip] = pooled_sum

    for h in range(HEADS):
        senders = senders_of(dps, vols, h)
        tile = tile_recv[senders[0]]
        mixed_h = jnp.where(row < 4, pltpu.roll(tile, 4, 0), 0.0)[:, 0:64]
        for s in senders[1:]:
            tile = tile + tile_recv[s]
        tile = jnp.where(row < 4, tile, 0.0)
        value_out[:, h * 64 : h * 64 + 64] = (
            lax.dot_general(
                tile[:, 0:rows], mixed_h, FIRST, precision=HIGHEST, preferred_element_type=F32
            )
            / PATCHES
        )
        value_out[:, 512 + h * 64 : 576 + h * 64] = jnp.dot(
            head_own, tile[:, 64:128], precision=HIGHEST, preferred_element_type=F32
        )

    each(1, chips, lambda k: head_copy(k, (chip + chips - k) % chips).wait_recv())
    heads = copy(
        head_out.at[core], head_out.at[core], core_sems.at[4], core_sems.at[5], other, vol
    )
    heads.start()

    each(1, count, lambda k: grad_copy(k, me).wait_send())
    each(1, chips, lambda k: head_copy(k, chip).wait_send())
    heads.wait_send()
    each(1, count, lambda k: grad_copy(k, (me + count - k) % count).wait_recv())
    copy(
        head_out.at[1 - core], head_out.at[1 - core], core_sems.at[4], core_sems.at[5], other, vol
    ).wait_recv()


def senders_of(dps, vols, h):
    return [
        (z * 4 + h // 2) * vols + v * 2 + h % 2 for z in range(dps // 8) for v in range(vols // 2)
    ]


def finish(dps, vols, errors, grads, values, heads, errors_out, in_out, out_out, head_out):
    rows = values.shape[0]
    for h in range(HEADS):
        senders = senders_of(dps, vols, h)
        both = grads[senders[0]].astype(F32)
        for s in senders[1:]:
            both = both + grads[s].astype(F32)
        in_out[:, h * 64 : h * 64 + 64] = both[:, 64:128]
        in_out[:, 512 + h * 64 : 576 + h * 64] = both[:, 0:64]
    in_out[:, 1024:1536] = values[:, 0:512]
    out_out[...] = values[:, 512:1024]
    errors_out[...] = errors[0:1, 0:K]
    for d in range(dps):
        head_out[:, d * rows : (d + 1) * rows] = heads[d % 2, d // 2][0:K, 64 : 64 + rows]


def constants():
    freq = np.arange(PIX) - PIX // 2
    phase = (freq[:, None] * np.arange(PIX)[None, :] % PIX) * (2.0 * math.pi / PIX)
    cosine, sine = np.cos(phase), np.sin(phase)
    waves = np.stack([cosine, sine, (cosine + sine).T, (cosine - sine).T]).astype(np.float32)
    sel = np.zeros((2 * PIX, PIX), np.float32)
    sel[2 * np.arange(PIX), np.arange(PIX)] = 1.0
    places = np.zeros((PATCH, PIX, PIX), np.float32)
    for r in range(PATCH):
        places[r, np.arange(PIX), r * PATCH + np.arange(PIX) % PATCH] = 1.0
    return waves, sel, places


def local(
    dps,
    vols,
    images,
    contrast,
    volume,
    line_index,
    patch_weight,
    position,
    norm_gain,
    project_in,
    project_out,
    head_weight,
):
    width = norm_gain.shape[0]
    rows = project_in.shape[0]
    chips = dps // 2
    count = chips * vols
    waves, sel, places = constants()
    slab, side, _ = volume.shape
    vmem = pl.BlockSpec(memory_space=pltpu.VMEM)
    hbm = pl.BlockSpec(memory_space=pltpu.HBM)
    inputs = (
        images,
        contrast,
        patch_weight,
        position,
        norm_gain.reshape(1, width),
        project_in,
        project_out,
        head_weight.T,
        jnp.asarray(waves),
        jnp.asarray(sel, BF16),
        jnp.asarray(places, BF16),
    )
    errors, grads, values, heads = pl.pallas_call(
        functools.partial(step, dps, vols),
        out_shape=(
            jax.ShapeDtypeStruct((8, 128), F32),
            jax.ShapeDtypeStruct((count, rows, 128), BF16),
            jax.ShapeDtypeStruct((rows, 1024), F32),
            jax.ShapeDtypeStruct((2, chips, 8, 128), F32),
        ),
        in_specs=[hbm] * (2 + len(inputs)),
        out_specs=(vmem,) * 4,
        scratch_shapes=[
            pltpu.SMEM(line_index.shape, jnp.int32),
            pltpu.VMEM(line_index.shape, jnp.int32),
        ]
        + [pltpu.VMEM(one.shape, one.dtype) for one in inputs]
        + [
            pltpu.VMEM((slab * (side // 16), 16, side), BF16),
            pltpu.VMEM((vols + 1, K * PIX, PIX), BF16),
            pltpu.VMEM((PATCHES // 2, 128), BF16),
            pltpu.VMEM((4, rows + rows // 2 + 16, 128), BF16),
            pltpu.VMEM((128, 8), F32),
            pltpu.VMEM((vols, K * PIX, PIX), BF16),
            pltpu.VMEM((HEADS, PATCHES // 2, 128), BF16),
            pltpu.VMEM((dps, rows + rows // 2 + 16, 128), BF16),
            pltpu.VMEM((384, width), BF16),
            pltpu.VMEM((width, 384), BF16),
            pltpu.VMEM((320, 64), F32),
            pltpu.VMEM((PATCHES, 1), F32),
            pltpu.VMEM((HEADS, PATCHES, 128), BF16),
            pltpu.VMEM((64, HEADS * PATCHES), BF16),
            pltpu.VMEM((HEADS, PATCHES, 128), F32),
            pltpu.VMEM((HEADS, PATCHES, PATCHES), BF16),
            pltpu.VMEM((HEADS, PATCHES, 256), BF16),
            pltpu.VMEM((HEADS, PATCHES, 128), F32),
            pltpu.VMEM((HEADS, 128), F32),
            pltpu.VMEM((HEADS, 128), F32),
            pltpu.VMEM((HEADS, HEADS, 128), F32),
            pltpu.VMEM((HEADS, 128), F32),
            pltpu.VMEM((HEADS * PATCHES, 128), BF16),
            pltpu.VMEM((PATCHES, 256), F32),
            pltpu.VMEM((320, 128), BF16),
            pltpu.VMEM((320, 128), BF16),
            pltpu.VMEM((384, 128), BF16),
            pltpu.VMEM((16, width + 128), F32),
            pltpu.VMEM((16, width + 128), F32),
            pltpu.VMEM((chips, rows, 128), BF16),
            pltpu.VMEM((dps, 8, 128), F32),
            pltpu.VMEM((count, 8, 128), F32),
            pltpu.VMEM((8, 128), F32),
            pltpu.SemaphoreType.DMA((14,)),
            pltpu.SemaphoreType.DMA((2, vols)),
            pltpu.SemaphoreType.DMA((2, HEADS)),
            pltpu.SemaphoreType.DMA((2, dps)),
            pltpu.SemaphoreType.DMA((chips,)),
            pltpu.SemaphoreType.DMA((2, HEADS)),
            pltpu.SemaphoreType.DMA((6,)),
            pltpu.SemaphoreType.DMA((2, count)),
            pltpu.SemaphoreType.DMA((2, count)),
            pltpu.SemaphoreType.DMA((2, chips)),
        ],
        compiler_params=pltpu.CompilerParams(
            collective_id=0, has_side_effects=True, vmem_limit_bytes=56 * 1024 * 1024
        ),
        name="pose_step",
    )(line_index, volume.reshape(slab * (side // 16), 16, side), *inputs)
    errors, in_grad, out_grad, head_grad = pl.pallas_call(
        functools.partial(finish, dps, vols),
        out_shape=(
            jax.ShapeDtypeStruct((1, K), F32),
            jax.ShapeDtypeStruct((rows, 3 * HEADS * HEAD_DIM), F32),
            jax.ShapeDtypeStruct((rows, HEADS * HEAD_DIM), F32),
            jax.ShapeDtypeStruct((K, width), F32),
        ),
        in_specs=[vmem] * 4,
        out_specs=(vmem,) * 4,
        name="finish",
    )(errors, grads, values, heads)
    return errors, in_grad, out_grad, head_grad.T


def solution(mesh):
    placed = (
        P(("dp", "vol"), None, None),
        P(("dp", "vol"), None, None),
        P("vol", None, None),
        P("dp", None, None),
        P(),
        P(),
        P(),
        P("dp", None),
        P("dp", None),
        P(),
    )
    return jax.shard_map(
        functools.partial(local, mesh.shape["dp"], mesh.shape["vol"]),
        mesh=mesh,
        in_specs=placed,
        out_specs=(P(("dp", "vol"), None), P("dp", None), P("dp", None), P()),
        check_vma=False,
    )
```

```python
import functools
import math

import jax
import jax.numpy as jnp
import numpy as np
from jax import lax
from jax.experimental import pallas as pl
from jax.experimental.pallas import tpu as pltpu
from jax.sharding import PartitionSpec as P

HEADS = 8
HEAD_DIM = 64
PIX = 128
PATCH = 8
PATCHES = 256
K = 4
EPSILON = 1e-05
F32 = jnp.float32
BF16 = jnp.bfloat16
HIGHEST = lax.Precision.HIGHEST
FIRST = (((0,), (0,)), ((), ()))
LAST = (((1,), (1,)), ((), ()))
MESH = pl.DeviceIdType.MESH


def step(
    dps,
    vols,
    index_hbm,
    volume,
    image_hbm,
    contrast_hbm,
    patch_weight_hbm,
    position_hbm,
    gain_hbm,
    project_in_hbm,
    project_out_hbm,
    head_hbm,
    waves_hbm,
    sel_hbm,
    places_hbm,
    errors_out,
    grad_recv,
    value_out,
    head_out,
    spots,
    index,
    image,
    contrast,
    patch_weight,
    position,
    gain,
    project_in,
    project_out,
    head_weight,
    waves,
    sel,
    places,
    slab_buf,
    picked,
    patches,
    pieces,
    head_wide,
    lines,
    patch_buf,
    weight,
    basis,
    basis_t,
    gram,
    square,
    tokens,
    tokens_t,
    scales,
    attention,
    triple,
    column,
    mean_att,
    small_send,
    small_recv,
    pulled_buf,
    terms_buf,
    total_buf,
    factor_send,
    factor_recv,
    factor_sum,
    side_send,
    side_recv,
    grad_send,
    tile_send,
    tile_recv,
    head_send,
    in_sems,
    line_sems,
    patch_sems,
    weight_sems,
    relay_sems,
    small_sems,
    core_sems,
    grad_sems,
    tile_sems,
    head_sems,
):
    dp = lax.axis_index("dp")
    vol = lax.axis_index("vol")
    core = dp % 2
    chip = dp // 2
    chips = dps // 2
    count = chips * vols
    me = chip * vols + vol
    pair = vol % 2
    head = (chip % 4) * 2 + pair
    rows = project_in.shape[0]
    width = gain.shape[1]
    slab = volume.shape[0]

    def copy(src, dst, send_sem, recv_sem, to_dp, to_vol):
        return pltpu.make_async_remote_copy(
            src_ref=src,
            dst_ref=dst,
            send_sem=send_sem,
            recv_sem=recv_sem,
            device_id=(to_dp, to_vol),
            device_id_type=MESH,
        )

    def each(first, last, body):
        def run(k, c):
            body(k)
            return c

        lax.fori_loop(first, last, run, 0)

    other = dp + 1 - 2 * core
    barrier = pltpu.get_barrier_semaphore()

    def greet(k):
        e = (me + k) % count
        pl.semaphore_signal(
            barrier, inc=1, device_id=(e // vols * 2 + core, e % vols), device_id_type=MESH
        )

    each(count // 2, count, greet)
    each(1, count // 2, greet)
    pl.semaphore_signal(barrier, inc=1, device_id=(other, vol), device_id_type=MESH)

    loads = {}
    for name, src, dst in (
        ("image", image_hbm, image),
        ("places", places_hbm, places),
        ("project_in", project_in_hbm, project_in),
        ("project_out", project_out_hbm, project_out),
        ("index", index_hbm, index),
        ("spots", index_hbm, spots),
        ("sel", sel_hbm, sel),
        ("waves", waves_hbm, waves),
        ("patch_weight", patch_weight_hbm, patch_weight),
        ("position", position_hbm, position),
        ("gain", gain_hbm, gain),
        ("head", head_hbm, head_weight),
        ("contrast", contrast_hbm, contrast),
        ("volume", volume, slab_buf),
    ):
        loads[name] = pltpu.make_async_copy(src, dst, in_sems.at[len(loads)])
        loads[name].start()

    loads["project_in"].wait()
    loads["project_out"].wait()
    loads["head"].wait()
    near = pl.ds(pl.multiple_of(dp * rows // 128 * 128, 128), 128)
    head_wide[...] = jnp.concatenate(
        [head_weight[:, near], jnp.zeros((4, 128), F32)], axis=0
    ).T
    head_own = head_wide[pl.ds(pl.multiple_of(dp * rows % 128, rows), rows), :]
    share = lax.dot_general(
        head_own,
        project_out[...].astype(F32),
        FIRST,
        precision=HIGHEST,
        preferred_element_type=F32,
    )
    for a in range(4):
        parts = [project_in[:, p * 512 + a * 128 : p * 512 + a * 128 + 128] for p in range(3)]
        parts.append(share[:, a * 128 : a * 128 + 128])
        query, key, value, mix = [
            jnp.where(pair == 0, one[:, 0:64], one[:, 64:128]) for one in parts
        ]
        high = mix.astype(BF16)
        mix = jnp.concatenate([high.astype(F32), mix - high.astype(F32)], axis=1)
        pieces[a, 0:rows, :] = jnp.concatenate([query, key], axis=1)
        pieces[a, rows : rows + rows // 2, :] = jnp.concatenate(
            [value[0 : rows // 2], value[rows // 2 : rows]], axis=1
        )
        pieces[a, rows + rows // 2 :, :] = jnp.concatenate(
            [mix, jnp.zeros((8, 128), F32)], axis=0
        ).astype(BF16)
    weight[dp] = pieces[chip % 4]
    loads["image"].wait()
    loads["places"].wait()
    cells = lax.broadcasted_iota(jnp.int32, (16, 16, 128), 1)
    spread_lane = lax.broadcasted_iota(jnp.int32, (16, 16, 128), 2)
    cut = jnp.zeros((PATCHES, 128), F32)
    for r in range(PATCH):
        stripe = image[0, pl.ds(r, 16, stride=PATCH), :]
        stripe = jnp.broadcast_to(stripe[:, None, :], (16, 16, 128))
        stripe = jnp.where(spread_lane // PATCH == cells, stripe, 0.0).reshape(PATCHES, 128)
        cut = cut + jnp.dot(stripe.astype(BF16), places[r], preferred_element_type=F32)
    patches[...] = jnp.concatenate([cut[0:128, 0:64], cut[128:256, 0:64]], axis=1).astype(BF16)
    patch_mean = jnp.sum(cut[:, 0:64], axis=0, keepdims=True) / PATCHES
    loads["patch_weight"].wait()
    loads["position"].wait()
    loads["gain"].wait()
    embed = patch_weight[...].astype(F32)
    embed_c = embed - jnp.mean(embed, axis=1, keepdims=True)
    basis[0:64, :] = (embed_c * gain[...]).astype(BF16)
    gram[0:64, :] = lax.dot_general(
        embed_c, embed_c, LAST, precision=HIGHEST, preferred_element_type=F32
    )
    place_mean = jnp.zeros((1, width), F32)
    for part in range(4):
        one = position[part * 64 : part * 64 + 64, :].astype(F32)
        place_mean = place_mean + jnp.sum(one, axis=0, keepdims=True)
        one = one - jnp.mean(one, axis=1, keepdims=True)
        basis[64 + part * 64 : 128 + part * 64, :] = (one * gain[...]).astype(BF16)
        gram[64 + part * 64 : 128 + part * 64, :] = lax.dot_general(
            one, embed_c, LAST, precision=HIGHEST, preferred_element_type=F32
        )
        square[part * 64 : part * 64 + 64, :] = jnp.sum(one * one, axis=1, keepdims=True)
    basis[320:384, :] = jnp.zeros((64, width), BF16)
    basis_t[...] = basis[...].T
    own_row = (
        jnp.dot(
            jnp.broadcast_to(patch_mean, (8, 64)),
            embed,
            precision=HIGHEST,
            preferred_element_type=F32,
        )
        + place_mean / PATCHES
    )

    head_t = jnp.concatenate([head_weight[...], jnp.zeros((4, width), F32)], axis=0)
    own_logit = lax.dot_general(
        own_row, head_t, LAST, precision=HIGHEST, preferred_element_type=F32
    )
    row = lax.broadcasted_iota(jnp.int32, (HEADS, 128), 0)
    lane = lax.broadcasted_iota(jnp.int32, (HEADS, 128), 1)
    mine = row == head
    own_logit = jnp.where(mine[:, 0:HEADS], own_logit, 0.0)

    loads["waves"].wait()
    pixels = image[0]
    first_cos = jnp.dot(waves[0], pixels, precision=HIGHEST, preferred_element_type=F32)
    first_sin = jnp.dot(waves[1], pixels, precision=HIGHEST, preferred_element_type=F32)
    spectrum = jnp.dot(first_cos, waves[2], precision=HIGHEST, preferred_element_type=F32)
    spectrum = spectrum + jnp.dot(
        first_sin, waves[3], precision=HIGHEST, preferred_element_type=F32
    )
    spectrum = spectrum / PIX

    pl.semaphore_wait(barrier, count)

    def member(m):
        return chip // 4 * 8 + m // 2 * 2 + core, vol // 2 * 2 + m % 2

    def flipped(k):
        low = (head + k) % 2
        mid = (head // 2 + k // 2) % 2
        return (head // 4 + k // 4) % 2 * 4 + mid * 2 + low

    def patch_copy(k, slot):
        to_dp, to_vol = member(flipped(k))
        return copy(
            patches,
            patch_buf.at[slot],
            patch_sems.at[0, k],
            patch_sems.at[1, slot],
            to_dp,
            to_vol,
        )

    def patch_relay(k):
        to_dp, to_vol = member(flipped(k))
        slot = flipped(4)
        return copy(
            patch_buf.at[slot],
            patch_buf.at[slot],
            patch_sems.at[0, 4 + k],
            patch_sems.at[1, slot],
            to_dp,
            to_vol,
        )

    def weight_copy(k, slot):
        to = (chip + k) % chips
        return copy(
            pieces.at[to % 4],
            weight.at[slot],
            weight_sems.at[0, k],
            weight_sems.at[1, slot],
            to * 2 + core,
            vol,
        )

    def weight_relay(at):
        s = at * 2 + core
        return copy(
            weight.at[s], weight.at[s], relay_sems.at[at], weight_sems.at[1, s], other, vol
        )

    def line_copy(k, slot):
        to = (vol + k) % vols
        return copy(picked.at[k], lines.at[slot], line_sems.at[0, k], line_sems.at[1, slot], dp, to)

    each(chips // 2, chips, lambda k: weight_copy(k, dp).start())
    patch_copy(4, head).start()
    each(1, 4, lambda k: patch_copy(k, head).start())
    each(1, chips // 2, lambda k: weight_copy(k, dp).start())
    weight_relay(chip).start()
    patch_buf[head] = patches[...]

    loads["index"].wait()
    loads["spots"].wait()
    loads["sel"].wait()
    loads["volume"].wait()

    def render(step_k, c):
        k = step_k + 1
        v = (vol + k) % vols
        turned = jnp.concatenate([index[v], jnp.zeros((4, 128), jnp.int32)], axis=0)
        turned = turned.astype(F32).T.astype(jnp.int32)
        spot_lane = lax.broadcasted_iota(jnp.int32, (128, 256), 1)
        spot_row = lax.broadcasted_iota(jnp.int32, (128, 256), 0)
        for hyp in range(K):
            line = turned[:, hyp : hyp + 1]
            level = (line >> 4) - vol * slab
            target = jnp.where((level >= 0) & (level < slab), line & 15, 1024)
            hot = jnp.where(spot_lane == (spot_row % 16) * 16 + target, 1.0, 0.0).astype(BF16)
            found = []
            for group in range(8):
                tiles = []
                for i in range(16):
                    spot = spots[v, hyp, group * 16 + i]
                    tiles.append(slab_buf[(spot >> 4) & (slab - 1)])
                tiles = jnp.concatenate(tiles, axis=0)
                found.append(
                    jnp.dot(
                        hot[group * 16 : group * 16 + 16], tiles, preferred_element_type=F32
                    )
                )
            found = jnp.concatenate(found, axis=0).astype(BF16)
            picked[k, hyp * PIX : (hyp + 1) * PIX, :] = jnp.dot(
                found, sel[...], preferred_element_type=F32
            ).astype(BF16)
        @pl.when(k < vols)
        def _():
            line_copy(k, vol).start()

        return c

    lax.fori_loop(0, vols, render, 0)
    lines[vol] = picked[vols]

    def weight_pass(k):
        at = (chip + chips - k) % chips
        weight_copy(k, at * 2 + core).wait_recv()
        weight_relay(at).start()


    first = lax.broadcasted_iota(jnp.int32, (PATCHES // 2, 128), 1) < 64
    high = gram[0:64].astype(BF16)
    gram_parts = jnp.concatenate([high.astype(F32), gram[0:64] - high.astype(F32)], axis=1)
    gram_parts = jnp.concatenate([gram_parts, jnp.zeros((64, 128), F32)], axis=0).astype(BF16)
    gram_places = jnp.concatenate([2.0 * gram[64:320], jnp.zeros((PATCHES, 64), F32)], axis=1)

    def norm(j):
        both = patch_buf[j].astype(F32)
        turned = pltpu.roll(both, 64, 1)
        both = jnp.concatenate(
            [jnp.where(first, both, turned), jnp.where(first, turned, both)], axis=0
        )
        one = both.astype(BF16)
        total = jnp.dot(one, gram_parts, preferred_element_type=F32) + gram_places
        total = jnp.sum(both * total, axis=1, keepdims=True)
        total = jnp.maximum(total + square[...], 0.0) / width
        scale = jnp.broadcast_to(lax.rsqrt(total + EPSILON), (PATCHES, 128))
        return one, one.T[0:64], scale

    def norms(ks):
        for k in ks:
            if k % 4 > 0:
                patch_copy(k, flipped(k)).wait_recv()
        found = [norm(flipped(k)) for k in ks]
        for k, (one, turned, scale) in zip(ks, found):
            j = flipped(k)
            tokens[j] = one
            tokens_t[:, pl.ds(pl.multiple_of(j * PATCHES, PATCHES), PATCHES)] = turned
            scales[j] = scale

    patch_copy(4, flipped(4)).wait_recv()
    each(1, 4, lambda k: patch_relay(k).start())
    norms((0, 4))
    each(1, chips // 2, weight_pass)
    norms((1, 2, 3))
    each(chips // 2, chips, weight_pass)
    norms((5, 6, 7))

    def weight_rest(k):
        s = (chip + chips - k) % chips * 2 + 1 - core
        weight_copy(0, s).wait_recv()

    each(0, chips, weight_rest)

    sides = weight[:, 0:rows, :].reshape(width, 128)
    value = weight[:, rows : rows + rows // 2, :]
    value = jnp.concatenate([value[:, :, 0:64], value[:, :, 64:128]], axis=1)
    half = jnp.where(lax.broadcasted_iota(jnp.int32, (1, 128), 1) < 64, HEAD_DIM ** (-0.5), 1.0)
    sides = jnp.dot(basis[0:320], sides, preferred_element_type=F32) * half
    value = jnp.dot(
        basis[0:320], value.reshape(width, HEAD_DIM), preferred_element_type=F32
    )
    both = jnp.concatenate([sides, value, jnp.zeros((320, 64), F32)], axis=1)
    total_buf[...] = both[64:320]
    turn = jnp.concatenate([both[0:64], jnp.zeros((64, 256), F32)], axis=0).astype(BF16)
    mixed = jnp.sum(weight[:, rows + rows // 2 :, :].astype(F32), axis=0)[0:8]
    mixed = mixed[:, 0:64] + mixed[:, 64:128]

    def forward(j):
        scale = scales[j]
        t = jnp.dot(tokens[j], turn, preferred_element_type=F32) + total_buf[...]
        t = (t * jnp.concatenate([scale, scale], axis=1)).astype(BF16)
        scores = lax.dot_general(t[:, 64:128], t[:, 0:64], LAST, preferred_element_type=F32)
        raised = jnp.exp(scores)
        chosen = (raised * (1.0 / jnp.sum(raised, axis=0, keepdims=True))).astype(BF16)
        col = jnp.sum(chosen.astype(F32), axis=1, keepdims=True)
        mean = jnp.sum(col * t[:, 128:256].astype(F32), axis=0, keepdims=True) / PATCHES
        return t, chosen, col * scale, mean

    def forwards(i):
        found = [forward(8 * i + u) for u in range(8)]
        for u in range(8):
            j = 8 * i + u
            triple[j], attention[j], column[j], mean_att[pl.ds(j, 1), :] = found[u]

    each(0, HEADS // 8, forwards)

    loads["contrast"].wait()
    each(1, vols, lambda k: line_copy(k, (vol + vols - k) % vols).wait_recv())
    slices = lines[0].astype(F32)
    for v in range(1, vols):
        slices = slices + lines[v].astype(F32)
    filt = contrast[0].astype(F32)
    misfits = jnp.zeros((HEADS, 128), F32)
    for k in range(K):
        misfit = filt * slices[k * PIX : (k + 1) * PIX] - spectrum
        value = jnp.sum(jnp.sum(misfit * misfit, axis=0, keepdims=True), axis=1, keepdims=True)
        misfits = jnp.where(lane == k, value / (PIX * PIX), misfits)
    errors_out[...] = misfits
    misfits = jnp.where(mine, pltpu.roll(misfits, 4, 1), 0.0)
    means = mean_att[:, 0:HEAD_DIM]
    logit = own_logit + lax.dot_general(
        means, mixed, LAST, precision=HIGHEST, preferred_element_type=F32
    )
    logit = jnp.where(
        lane < K, jnp.concatenate([logit, jnp.zeros((HEADS, 120), F32)], axis=1), misfits
    )
    small_send[...] = logit

    def small_copy(k, slot):
        to_dp, to_vol = member(flipped(k))
        return copy(
            small_send,
            small_recv.at[slot],
            small_sems.at[0, k],
            small_sems.at[1, slot],
            to_dp,
            to_vol,
        )

    each(1, HEADS, lambda k: small_copy(HEADS - k, head).start())
    small_recv[head] = small_send[...]
    place_lane = lax.broadcasted_iota(jnp.int32, (PATCHES, 128), 1)
    weigh = jnp.zeros((PATCHES, 128), F32)
    for j in range(HEADS):
        weigh = jnp.where(place_lane == j, column[j], weigh)
    weigh = weigh.T[0:HEADS]
    low = weigh.astype(BF16)
    seen = jnp.zeros((HEADS, 128), F32)
    for j in range(HEADS):
        seen = jnp.where(
            row == j, jnp.dot(low, tokens[j], preferred_element_type=F32), seen
        )
    seen = jnp.concatenate([seen[:, 0:64], weigh, jnp.zeros((HEADS, 64), F32)], axis=1)
    weighed = jnp.dot(seen.astype(BF16), basis[...], preferred_element_type=F32)
    each(1, HEADS, lambda k: small_copy(k, flipped(k)).wait_recv())
    summed = jnp.sum(small_recv[...], axis=0)
    misfits = jnp.where(lane < K, pltpu.roll(summed, 124, 1), 0.0)
    raised = jnp.where(lane < K, jnp.exp(summed), 0.0)
    chances = raised / jnp.sum(raised, axis=1, keepdims=True)
    expected = jnp.sum(chances * misfits, axis=1, keepdims=True)
    slope = chances * (misfits - expected)
    pulled = jnp.zeros((HEADS, HEAD_DIM), F32)
    for k in range(K):
        pulled = pulled + slope[:, k : k + 1] * mixed[k : k + 1, :]
    pulled_buf[...] = jnp.concatenate(
        [pulled / PATCHES, jnp.zeros((HEADS, 128 - HEAD_DIM), F32)], axis=1
    )

    slope_t = slope.T[0:8]
    outer = jnp.zeros((HEADS, 128), F32)
    value_t = jnp.zeros((HEADS, width), F32)
    for j in range(HEADS):
        outer = outer + slope_t[:, j : j + 1] * mean_att[j : j + 1, :]
        value_t = value_t + slope_t[:, j : j + 1] * weighed[j : j + 1, :]
    own = jnp.sum(jnp.where(lane[:, 0:HEADS] == head, slope_t, 0.0), axis=1, keepdims=True)
    side_send[0:8, 0:width] = own * own_row
    side_send[0:8, width:] = outer
    side_send[8:16, 0:width] = value_t
    side_send[8:16, width:] = jnp.zeros((8, 128), F32)
    side = copy(side_send, side_recv, core_sems.at[0], core_sems.at[1], other, vol)
    side.start()

    wide = lax.broadcasted_iota(jnp.int32, (PATCHES, 128), 1)

    def backward(j):
        t = triple[j]
        chosen = attention[j]
        wider = chosen.astype(F32)
        up = jnp.sum(
            t[:, 128:256].astype(F32) * pulled_buf[pl.ds(j, 1), :], axis=1, keepdims=True
        )
        center = jnp.sum(wider * up, axis=0, keepdims=True)
        inner = (wider * (up - center)).astype(BF16)
        sides = t[:, 0:128]
        key_slope = jnp.dot(inner, sides, preferred_element_type=F32)
        query_slope = lax.dot_general(inner, sides, FIRST, preferred_element_type=F32)
        scale = scales[j]
        return jnp.where(wide < 64, key_slope, query_slope * HEAD_DIM ** (-0.5)) * scale

    total_buf[...] = jnp.zeros((PATCHES, 256), F32)

    def backwards(i):
        found = [backward(4 * i + u) for u in range(4)]
        total = total_buf[:, 0:128]
        for u in range(4):
            at = pl.multiple_of((4 * i + u) * PATCHES, PATCHES)
            terms_buf[pl.ds(at, PATCHES), :] = found[u].astype(BF16)
            total = total + found[u]
        total_buf[:, 0:128] = total

    each(0, HEADS // 8, backwards)
    side.wait_recv()
    sides = side_send[...] + side_recv[...]
    pooled_t = sides[0:8, 0:width]
    value_t = sides[8:16, 0:width]
    outer = sides[0:8, width : width + HEAD_DIM]

    fill = [jnp.zeros((HEADS, 64 - rows), F32)] if rows < 64 else []
    for d in range(dps):
        part = slice(d * rows, (d + 1) * rows)
        top = jnp.concatenate([value_t[:, part]] + fill + [outer], axis=1)
        low = jnp.concatenate([mixed, pooled_t[:, part]] + fill, axis=1)
        tile_send[d] = jnp.where(row < 4, top, pltpu.roll(low, 4, 0))

    def tile_copy(k, slot):
        e = (me + k) % count
        d = e // vols * 2 + core
        return copy(
            tile_send.at[d],
            tile_recv.at[slot],
            tile_sems.at[0, k],
            tile_sems.at[1, slot],
            d,
            e % vols,
        )

    each(count // 2, count, lambda k: tile_copy(k, me).start())
    each(1, count // 2, lambda k: tile_copy(k, me).start())
    each(HEADS // 8, HEADS // 4, backwards)

    factor_send[0:64, :] = jnp.dot(
        tokens_t[...], terms_buf[...], preferred_element_type=F32
    ).astype(BF16)
    factor_send[64:320, :] = total_buf[:, 0:128].astype(BF16)
    factors = copy(factor_send, factor_recv, core_sems.at[2], core_sems.at[3], other, vol)
    factors.start()
    factors.wait_recv()
    factor_sum[0:320, :] = (
        factor_send[...].astype(F32) + factor_recv[...].astype(F32)
    ).astype(BF16)
    factor_sum[320:384, :] = jnp.zeros((64, 128), BF16)
    def grad_copy(k, slot):
        e = (me + k) % count
        d = e // vols * 2 + core
        return copy(
            grad_send.at[e // vols],
            grad_recv.at[slot],
            grad_sems.at[0, k],
            grad_sems.at[1, slot],
            d,
            e % vols,
        )

    found = [
        basis_t[pl.ds(pl.multiple_of((2 * i + core) * rows, rows), rows), :] for i in range(chips)
    ]
    grad_send[...] = (
        jnp.dot(jnp.concatenate(found, axis=0), factor_sum[...], preferred_element_type=F32)
        .astype(BF16)
        .reshape(chips, rows, 128)
    )
    each(count // 2, count, lambda k: grad_copy(k, me).start())
    each(1, count // 2, lambda k: grad_copy(k, me).start())
    grad_recv[me] = grad_send[chip]
    each(1, 5, lambda k: patch_copy(k, head).wait_send())
    each(1, 4, lambda k: patch_relay(k).wait_send())
    each(1, chips, lambda k: weight_copy(k, dp).wait_send())
    each(0, chips, lambda at: weight_relay(at).wait_send())
    each(1, vols, lambda k: line_copy(k, vol).wait_send())
    each(1, HEADS, lambda k: small_copy(k, head).wait_send())
    side.wait_send()
    factors.wait_send()
    each(1, count, lambda k: tile_copy(k, me).wait_send())
    tile_recv[me] = tile_send[dp]

    each(1, count, lambda k: tile_copy(k, (me + count - k) % count).wait_recv())

    outers = []
    for h in range(HEADS):
        senders = senders_of(dps, vols, h)
        tile = tile_recv[senders[0]]
        for s in senders[1:]:
            tile = tile + tile_recv[s]
        outers.append(tile[:, 64:128])
    pooled_sum = pltpu.roll(jnp.sum(tile_recv[...], axis=0), 4, 0)
    branch = lax.dot_general(
        jnp.concatenate(outers, axis=1),
        project_out[...].astype(F32),
        LAST,
        precision=HIGHEST,
        preferred_element_type=F32,
    )
    fill = [jnp.zeros((HEADS, 64 - rows), F32)] if rows < 64 else []
    pooled_sum = pooled_sum + jnp.concatenate(
        [jnp.zeros((HEADS, 64), F32), branch] + fill, axis=1
    )
    head_send[...] = pooled_sum

    def head_copy(k, slot):
        to = (chip + k) % chips
        return copy(
            head_send,
            head_out.at[core, slot],
            head_sems.at[0, k],
            head_sems.at[1, slot],
            to * 2 + core,
            vol,
        )

    each(1, chips, lambda k: head_copy(k, chip).start())
    head_out[core, chip] = pooled_sum

    for h in range(HEADS):
        senders = senders_of(dps, vols, h)
        tile = tile_recv[senders[0]]
        mixed_h = jnp.where(row < 4, pltpu.roll(tile, 4, 0), 0.0)[:, 0:64]
        for s in senders[1:]:
            tile = tile + tile_recv[s]
        tile = jnp.where(row < 4, tile, 0.0)
        value_out[:, h * 64 : h * 64 + 64] = (
            lax.dot_general(
                tile[:, 0:rows], mixed_h, FIRST, precision=HIGHEST, preferred_element_type=F32
            )
            / PATCHES
        )
        value_out[:, 512 + h * 64 : 576 + h * 64] = jnp.dot(
            head_own, tile[:, 64:128], precision=HIGHEST, preferred_element_type=F32
        )

    each(1, chips, lambda k: head_copy(k, (chip + chips - k) % chips).wait_recv())
    heads = copy(
        head_out.at[core], head_out.at[core], core_sems.at[4], core_sems.at[5], other, vol
    )
    heads.start()

    each(1, count, lambda k: grad_copy(k, me).wait_send())
    each(1, chips, lambda k: head_copy(k, chip).wait_send())
    heads.wait_send()
    each(1, count, lambda k: grad_copy(k, (me + count - k) % count).wait_recv())
    copy(
        head_out.at[1 - core], head_out.at[1 - core], core_sems.at[4], core_sems.at[5], other, vol
    ).wait_recv()


def senders_of(dps, vols, h):
    return [
        (z * 4 + h // 2) * vols + v * 2 + h % 2 for z in range(dps // 8) for v in range(vols // 2)
    ]


def finish(dps, vols, errors, grads, values, heads, errors_out, in_out, out_out, head_out):
    rows = values.shape[0]
    for h in range(HEADS):
        senders = senders_of(dps, vols, h)
        both = grads[senders[0]].astype(F32)
        for s in senders[1:]:
            both = both + grads[s].astype(F32)
        in_out[:, h * 64 : h * 64 + 64] = both[:, 64:128]
        in_out[:, 512 + h * 64 : 576 + h * 64] = both[:, 0:64]
    in_out[:, 1024:1536] = values[:, 0:512]
    out_out[...] = values[:, 512:1024]
    errors_out[...] = errors[0:1, 0:K]
    for d in range(dps):
        head_out[:, d * rows : (d + 1) * rows] = heads[d % 2, d // 2][0:K, 64 : 64 + rows]


def constants():
    freq = np.arange(PIX) - PIX // 2
    phase = (freq[:, None] * np.arange(PIX)[None, :] % PIX) * (2.0 * math.pi / PIX)
    cosine, sine = np.cos(phase), np.sin(phase)
    waves = np.stack([cosine, sine, (cosine + sine).T, (cosine - sine).T]).astype(np.float32)
    sel = np.zeros((2 * PIX, PIX), np.float32)
    sel[2 * np.arange(PIX), np.arange(PIX)] = 1.0
    places = np.zeros((PATCH, PIX, PIX), np.float32)
    for r in range(PATCH):
        places[r, np.arange(PIX), r * PATCH + np.arange(PIX) % PATCH] = 1.0
    return waves, sel, places


def local(
    dps,
    vols,
    images,
    contrast,
    volume,
    line_index,
    patch_weight,
    position,
    norm_gain,
    project_in,
    project_out,
    head_weight,
):
    width = norm_gain.shape[0]
    rows = project_in.shape[0]
    chips = dps // 2
    count = chips * vols
    waves, sel, places = constants()
    slab, side, _ = volume.shape
    vmem = pl.BlockSpec(memory_space=pltpu.VMEM)
    hbm = pl.BlockSpec(memory_space=pltpu.HBM)
    inputs = (
        images,
        contrast,
        patch_weight,
        position,
        norm_gain.reshape(1, width),
        project_in,
        project_out,
        head_weight.T,
        jnp.asarray(waves),
        jnp.asarray(sel, BF16),
        jnp.asarray(places, BF16),
    )
    errors, grads, values, heads = pl.pallas_call(
        functools.partial(step, dps, vols),
        out_shape=(
            jax.ShapeDtypeStruct((8, 128), F32),
            jax.ShapeDtypeStruct((count, rows, 128), BF16),
            jax.ShapeDtypeStruct((rows, 1024), F32),
            jax.ShapeDtypeStruct((2, chips, 8, 128), F32),
        ),
        in_specs=[hbm] * (2 + len(inputs)),
        out_specs=(vmem,) * 4,
        scratch_shapes=[
            pltpu.SMEM(line_index.shape, jnp.int32),
            pltpu.VMEM(line_index.shape, jnp.int32),
        ]
        + [pltpu.VMEM(one.shape, one.dtype) for one in inputs]
        + [
            pltpu.VMEM((slab * (side // 16), 16, side), BF16),
            pltpu.VMEM((vols + 1, K * PIX, PIX), BF16),
            pltpu.VMEM((PATCHES // 2, 128), BF16),
            pltpu.VMEM((4, rows + rows // 2 + 16, 128), BF16),
            pltpu.VMEM((128, 8), F32),
            pltpu.VMEM((vols, K * PIX, PIX), BF16),
            pltpu.VMEM((HEADS, PATCHES // 2, 128), BF16),
            pltpu.VMEM((dps, rows + rows // 2 + 16, 128), BF16),
            pltpu.VMEM((384, width), BF16),
            pltpu.VMEM((width, 384), BF16),
            pltpu.VMEM((320, 64), F32),
            pltpu.VMEM((PATCHES, 1), F32),
            pltpu.VMEM((HEADS, PATCHES, 128), BF16),
            pltpu.VMEM((64, HEADS * PATCHES), BF16),
            pltpu.VMEM((HEADS, PATCHES, 128), F32),
            pltpu.VMEM((HEADS, PATCHES, PATCHES), BF16),
            pltpu.VMEM((HEADS, PATCHES, 256), BF16),
            pltpu.VMEM((HEADS, PATCHES, 128), F32),
            pltpu.VMEM((HEADS, 128), F32),
            pltpu.VMEM((HEADS, 128), F32),
            pltpu.VMEM((HEADS, HEADS, 128), F32),
            pltpu.VMEM((HEADS, 128), F32),
            pltpu.VMEM((HEADS * PATCHES, 128), BF16),
            pltpu.VMEM((PATCHES, 256), F32),
            pltpu.VMEM((320, 128), BF16),
            pltpu.VMEM((320, 128), BF16),
            pltpu.VMEM((384, 128), BF16),
            pltpu.VMEM((16, width + 128), F32),
            pltpu.VMEM((16, width + 128), F32),
            pltpu.VMEM((chips, rows, 128), BF16),
            pltpu.VMEM((dps, 8, 128), F32),
            pltpu.VMEM((count, 8, 128), F32),
            pltpu.VMEM((8, 128), F32),
            pltpu.SemaphoreType.DMA((14,)),
            pltpu.SemaphoreType.DMA((2, vols)),
            pltpu.SemaphoreType.DMA((2, HEADS)),
            pltpu.SemaphoreType.DMA((2, dps)),
            pltpu.SemaphoreType.DMA((chips,)),
            pltpu.SemaphoreType.DMA((2, HEADS)),
            pltpu.SemaphoreType.DMA((6,)),
            pltpu.SemaphoreType.DMA((2, count)),
            pltpu.SemaphoreType.DMA((2, count)),
            pltpu.SemaphoreType.DMA((2, chips)),
        ],
        compiler_params=pltpu.CompilerParams(
            collective_id=0, has_side_effects=True, vmem_limit_bytes=56 * 1024 * 1024
        ),
        name="pose_step",
    )(line_index, volume.reshape(slab * (side // 16), 16, side), *inputs)
    errors, in_grad, out_grad, head_grad = pl.pallas_call(
        functools.partial(finish, dps, vols),
        out_shape=(
            jax.ShapeDtypeStruct((1, K), F32),
            jax.ShapeDtypeStruct((rows, 3 * HEADS * HEAD_DIM), F32),
            jax.ShapeDtypeStruct((rows, HEADS * HEAD_DIM), F32),
            jax.ShapeDtypeStruct((K, width), F32),
        ),
        in_specs=[vmem] * 4,
        out_specs=(vmem,) * 4,
        name="finish",
    )(errors, grads, values, heads)
    return errors, in_grad, out_grad, head_grad.T


def solution(mesh):
    placed = (
        P(("dp", "vol"), None, None),
        P(("dp", "vol"), None, None),
        P("vol", None, None),
        P("dp", None, None),
        P(),
        P(),
        P(),
        P("dp", None),
        P("dp", None),
        P(),
    )
    return jax.shard_map(
        functools.partial(local, mesh.shape["dp"], mesh.shape["vol"]),
        mesh=mesh,
        in_specs=placed,
        out_specs=(P(("dp", "vol"), None), P("dp", None), P("dp", None), P()),
        check_vma=False,
    )
```

```python
import functools
import math

import jax
import jax.numpy as jnp
import numpy as np
from jax import lax
from jax.experimental import pallas as pl
from jax.experimental.pallas import tpu as pltpu
from jax.sharding import PartitionSpec as P

HEADS = 8
HEAD_DIM = 64
PIX = 128
PATCH = 8
PATCHES = 256
K = 4
EPSILON = 1e-05
F32 = jnp.float32
BF16 = jnp.bfloat16
HIGHEST = lax.Precision.HIGHEST
FIRST = (((0,), (0,)), ((), ()))
LAST = (((1,), (1,)), ((), ()))
MESH = pl.DeviceIdType.MESH


def step(
    dps,
    vols,
    index_hbm,
    volume,
    image_hbm,
    contrast_hbm,
    patch_weight_hbm,
    position_hbm,
    gain_hbm,
    project_in_hbm,
    project_out_hbm,
    head_hbm,
    waves_hbm,
    sel_hbm,
    places_hbm,
    errors_out,
    grad_recv,
    value_out,
    head_out,
    spots,
    index,
    image,
    contrast,
    patch_weight,
    position,
    gain,
    project_in,
    project_out,
    head_weight,
    waves,
    sel,
    places,
    slab_buf,
    picked,
    patches,
    pieces,
    head_wide,
    lines,
    patch_buf,
    weight,
    basis,
    basis_t,
    gram,
    square,
    tokens,
    tokens_t,
    scales,
    attention,
    triple,
    column,
    mean_att,
    small_send,
    small_recv,
    pulled_buf,
    terms_buf,
    total_buf,
    factor_send,
    factor_recv,
    factor_sum,
    side_send,
    side_recv,
    grad_send,
    tile_send,
    tile_recv,
    head_send,
    in_sems,
    line_sems,
    patch_sems,
    weight_sems,
    relay_sems,
    small_sems,
    core_sems,
    grad_sems,
    tile_sems,
    head_sems,
):
    dp = lax.axis_index("dp")
    vol = lax.axis_index("vol")
    core = dp % 2
    chip = dp // 2
    chips = dps // 2
    count = chips * vols
    me = chip * vols + vol
    pair = vol % 2
    head = (chip % 4) * 2 + pair
    rows = project_in.shape[0]
    width = gain.shape[1]
    slab = volume.shape[0]

    def copy(src, dst, send_sem, recv_sem, to_dp, to_vol):
        return pltpu.make_async_remote_copy(
            src_ref=src,
            dst_ref=dst,
            send_sem=send_sem,
            recv_sem=recv_sem,
            device_id=(to_dp, to_vol),
            device_id_type=MESH,
        )

    def each(first, last, body):
        def run(k, c):
            body(k)
            return c

        lax.fori_loop(first, last, run, 0)

    other = dp + 1 - 2 * core
    barrier = pltpu.get_barrier_semaphore()

    def greet(k):
        e = (me + k) % count
        pl.semaphore_signal(
            barrier, inc=1, device_id=(e // vols * 2 + core, e % vols), device_id_type=MESH
        )

    each(count // 2, count, greet)
    each(1, count // 2, greet)
    pl.semaphore_signal(barrier, inc=1, device_id=(other, vol), device_id_type=MESH)

    loads = {}
    for name, src, dst in (
        ("image", image_hbm, image),
        ("places", places_hbm, places),
        ("project_in", project_in_hbm, project_in),
        ("project_out", project_out_hbm, project_out),
        ("index", index_hbm, index),
        ("spots", index_hbm, spots),
        ("sel", sel_hbm, sel),
        ("waves", waves_hbm, waves),
        ("patch_weight", patch_weight_hbm, patch_weight),
        ("position", position_hbm, position),
        ("gain", gain_hbm, gain),
        ("head", head_hbm, head_weight),
        ("contrast", contrast_hbm, contrast),
        ("volume", volume, slab_buf),
    ):
        loads[name] = pltpu.make_async_copy(src, dst, in_sems.at[len(loads)])
        loads[name].start()

    loads["project_in"].wait()
    loads["project_out"].wait()
    loads["head"].wait()
    near = pl.ds(pl.multiple_of(dp * rows // 128 * 128, 128), 128)
    head_wide[...] = jnp.concatenate(
        [head_weight[:, near], jnp.zeros((4, 128), F32)], axis=0
    ).T
    head_own = head_wide[pl.ds(pl.multiple_of(dp * rows % 128, rows), rows), :]
    share = lax.dot_general(
        head_own,
        project_out[...].astype(F32),
        FIRST,
        precision=HIGHEST,
        preferred_element_type=F32,
    )
    for a in range(4):
        parts = [project_in[:, p * 512 + a * 128 : p * 512 + a * 128 + 128] for p in range(3)]
        parts.append(share[:, a * 128 : a * 128 + 128])
        query, key, value, mix = [
            jnp.where(pair == 0, one[:, 0:64], one[:, 64:128]) for one in parts
        ]
        high = mix.astype(BF16)
        mix = jnp.concatenate([high.astype(F32), mix - high.astype(F32)], axis=1)
        pieces[a, 0:rows, :] = jnp.concatenate([query, key], axis=1)
        pieces[a, rows : rows + rows // 2, :] = jnp.concatenate(
            [value[0 : rows // 2], value[rows // 2 : rows]], axis=1
        )
        pieces[a, rows + rows // 2 :, :] = jnp.concatenate(
            [mix, jnp.zeros((8, 128), F32)], axis=0
        ).astype(BF16)
    weight[dp] = pieces[chip % 4]
    loads["image"].wait()
    loads["places"].wait()
    cells = lax.broadcasted_iota(jnp.int32, (16, 16, 128), 1)
    spread_lane = lax.broadcasted_iota(jnp.int32, (16, 16, 128), 2)
    cut = jnp.zeros((PATCHES, 128), F32)
    for r in range(PATCH):
        stripe = image[0, pl.ds(r, 16, stride=PATCH), :]
        stripe = jnp.broadcast_to(stripe[:, None, :], (16, 16, 128))
        stripe = jnp.where(spread_lane // PATCH == cells, stripe, 0.0).reshape(PATCHES, 128)
        cut = cut + jnp.dot(stripe.astype(BF16), places[r], preferred_element_type=F32)
    patches[...] = jnp.concatenate([cut[0:128, 0:64], cut[128:256, 0:64]], axis=1).astype(BF16)
    patch_mean = jnp.sum(cut[:, 0:64], axis=0, keepdims=True) / PATCHES
    loads["patch_weight"].wait()
    loads["position"].wait()
    loads["gain"].wait()
    embed = patch_weight[...].astype(F32)
    embed_c = embed - jnp.mean(embed, axis=1, keepdims=True)
    basis[0:64, :] = (embed_c * gain[...]).astype(BF16)
    gram[0:64, :] = lax.dot_general(
        embed_c, embed_c, LAST, precision=HIGHEST, preferred_element_type=F32
    )
    place_mean = jnp.zeros((1, width), F32)
    for part in range(4):
        one = position[part * 64 : part * 64 + 64, :].astype(F32)
        place_mean = place_mean + jnp.sum(one, axis=0, keepdims=True)
        one = one - jnp.mean(one, axis=1, keepdims=True)
        basis[64 + part * 64 : 128 + part * 64, :] = (one * gain[...]).astype(BF16)
        gram[64 + part * 64 : 128 + part * 64, :] = lax.dot_general(
            one, embed_c, LAST, precision=HIGHEST, preferred_element_type=F32
        )
        square[part * 64 : part * 64 + 64, :] = jnp.sum(one * one, axis=1, keepdims=True)
    basis[320:384, :] = jnp.zeros((64, width), BF16)
    basis_t[...] = basis[...].T
    own_row = (
        jnp.dot(
            jnp.broadcast_to(patch_mean, (8, 64)),
            embed,
            precision=HIGHEST,
            preferred_element_type=F32,
        )
        + place_mean / PATCHES
    )

    head_t = jnp.concatenate([head_weight[...], jnp.zeros((4, width), F32)], axis=0)
    own_logit = lax.dot_general(
        own_row, head_t, LAST, precision=HIGHEST, preferred_element_type=F32
    )
    row = lax.broadcasted_iota(jnp.int32, (HEADS, 128), 0)
    lane = lax.broadcasted_iota(jnp.int32, (HEADS, 128), 1)
    mine = row == head
    own_logit = jnp.where(mine[:, 0:HEADS], own_logit, 0.0)

    loads["waves"].wait()
    pixels = image[0]
    first_cos = jnp.dot(waves[0], pixels, precision=HIGHEST, preferred_element_type=F32)
    first_sin = jnp.dot(waves[1], pixels, precision=HIGHEST, preferred_element_type=F32)
    spectrum = jnp.dot(first_cos, waves[2], precision=HIGHEST, preferred_element_type=F32)
    spectrum = spectrum + jnp.dot(
        first_sin, waves[3], precision=HIGHEST, preferred_element_type=F32
    )
    spectrum = spectrum / PIX

    pl.semaphore_wait(barrier, count)

    def member(m):
        return chip // 4 * 8 + m // 2 * 2 + core, vol // 2 * 2 + m % 2

    def flipped(k):
        low = (head + k) % 2
        mid = (head // 2 + k // 2) % 2
        return (head // 4 + k // 4) % 2 * 4 + mid * 2 + low

    def patch_copy(k, slot):
        to_dp, to_vol = member(flipped(k))
        return copy(
            patches,
            patch_buf.at[slot],
            patch_sems.at[0, k],
            patch_sems.at[1, slot],
            to_dp,
            to_vol,
        )

    def patch_relay(k):
        to_dp, to_vol = member(flipped(k))
        slot = flipped(4)
        return copy(
            patch_buf.at[slot],
            patch_buf.at[slot],
            patch_sems.at[0, 4 + k],
            patch_sems.at[1, slot],
            to_dp,
            to_vol,
        )

    def weight_copy(k, slot):
        to = (chip + k) % chips
        return copy(
            pieces.at[to % 4],
            weight.at[slot],
            weight_sems.at[0, k],
            weight_sems.at[1, slot],
            to * 2 + core,
            vol,
        )

    def weight_relay(at):
        s = at * 2 + core
        return copy(
            weight.at[s], weight.at[s], relay_sems.at[at], weight_sems.at[1, s], other, vol
        )

    def line_copy(k, slot):
        to = (vol + k) % vols
        return copy(picked.at[k], lines.at[slot], line_sems.at[0, k], line_sems.at[1, slot], dp, to)

    each(chips // 2, chips, lambda k: weight_copy(k, dp).start())
    patch_copy(4, head).start()
    each(1, 4, lambda k: patch_copy(k, head).start())
    each(1, chips // 2, lambda k: weight_copy(k, dp).start())
    weight_relay(chip).start()
    patch_buf[head] = patches[...]

    loads["index"].wait()
    loads["spots"].wait()
    loads["sel"].wait()
    loads["volume"].wait()

    def render(step_k, c):
        k = step_k + 1
        v = (vol + k) % vols
        turned = jnp.concatenate([index[v], jnp.zeros((4, 128), jnp.int32)], axis=0)
        turned = turned.astype(F32).T.astype(jnp.int32)
        spot_lane = lax.broadcasted_iota(jnp.int32, (128, 256), 1)
        spot_row = lax.broadcasted_iota(jnp.int32, (128, 256), 0)
        for hyp in range(K):
            line = turned[:, hyp : hyp + 1]
            level = (line >> 4) - vol * slab
            target = jnp.where((level >= 0) & (level < slab), line & 15, 1024)
            hot = jnp.where(spot_lane == (spot_row % 16) * 16 + target, 1.0, 0.0).astype(BF16)
            found = []
            for group in range(8):
                tiles = []
                for i in range(16):
                    spot = spots[v, hyp, group * 16 + i]
                    tiles.append(slab_buf[(spot >> 4) & (slab - 1)])
                tiles = jnp.concatenate(tiles, axis=0)
                found.append(
                    jnp.dot(
                        hot[group * 16 : group * 16 + 16], tiles, preferred_element_type=F32
                    )
                )
            found = jnp.concatenate(found, axis=0).astype(BF16)
            picked[k, hyp * PIX : (hyp + 1) * PIX, :] = jnp.dot(
                found, sel[...], preferred_element_type=F32
            ).astype(BF16)
        @pl.when(k < vols)
        def _():
            line_copy(k, vol).start()

        return c

    lax.fori_loop(0, vols, render, 0)
    lines[vol] = picked[vols]

    def weight_pass(k):
        at = (chip + chips - k) % chips
        weight_copy(k, at * 2 + core).wait_recv()
        weight_relay(at).start()


    first = lax.broadcasted_iota(jnp.int32, (PATCHES // 2, 128), 1) < 64
    high = gram[0:64].astype(BF16)
    gram_parts = jnp.concatenate([high.astype(F32), gram[0:64] - high.astype(F32)], axis=1)
    gram_parts = jnp.concatenate([gram_parts, jnp.zeros((64, 128), F32)], axis=0).astype(BF16)
    gram_places = jnp.concatenate([2.0 * gram[64:320], jnp.zeros((PATCHES, 64), F32)], axis=1)

    def norm(j):
        both = patch_buf[j].astype(F32)
        turned = pltpu.roll(both, 64, 1)
        both = jnp.concatenate(
            [jnp.where(first, both, turned), jnp.where(first, turned, both)], axis=0
        )
        one = both.astype(BF16)
        total = jnp.dot(one, gram_parts, preferred_element_type=F32) + gram_places
        total = jnp.sum(both * total, axis=1, keepdims=True)
        total = jnp.maximum(total + square[...], 0.0) / width
        scale = jnp.broadcast_to(lax.rsqrt(total + EPSILON), (PATCHES, 128))
        return one, one.T[0:64], scale

    def norms(ks):
        for k in ks:
            if k % 4 > 0:
                patch_copy(k, flipped(k)).wait_recv()
        found = [norm(flipped(k)) for k in ks]
        for k, (one, turned, scale) in zip(ks, found):
            j = flipped(k)
            tokens[j] = one
            tokens_t[:, pl.ds(pl.multiple_of(j * PATCHES, PATCHES), PATCHES)] = turned
            scales[j] = scale

    patch_copy(4, flipped(4)).wait_recv()
    each(1, 4, lambda k: patch_relay(k).start())
    norms((0, 4))
    each(1, chips // 2, weight_pass)
    norms((1, 2, 3))
    each(chips // 2, chips, weight_pass)
    norms((5, 6, 7))

    loads["contrast"].wait()
    each(1, vols, lambda k: line_copy(k, (vol + vols - k) % vols).wait_recv())
    slices = lines[0].astype(F32)
    for v in range(1, vols):
        slices = slices + lines[v].astype(F32)
    filt = contrast[0].astype(F32)
    misfits = jnp.zeros((HEADS, 128), F32)
    for k in range(K):
        misfit = filt * slices[k * PIX : (k + 1) * PIX] - spectrum
        value = jnp.sum(jnp.sum(misfit * misfit, axis=0, keepdims=True), axis=1, keepdims=True)
        misfits = jnp.where(lane == k, value / (PIX * PIX), misfits)
    errors_out[...] = misfits
    misfits = jnp.where(mine, pltpu.roll(misfits, 4, 1), 0.0)
    def weight_rest(k):
        s = (chip + chips - k) % chips * 2 + 1 - core
        weight_copy(0, s).wait_recv()

    each(0, chips, weight_rest)

    sides = weight[:, 0:rows, :].reshape(width, 128)
    value = weight[:, rows : rows + rows // 2, :]
    value = jnp.concatenate([value[:, :, 0:64], value[:, :, 64:128]], axis=1)
    half = jnp.where(lax.broadcasted_iota(jnp.int32, (1, 128), 1) < 64, HEAD_DIM ** (-0.5), 1.0)
    sides = jnp.dot(basis[0:320], sides, preferred_element_type=F32) * half
    value = jnp.dot(
        basis[0:320], value.reshape(width, HEAD_DIM), preferred_element_type=F32
    )
    both = jnp.concatenate([sides, value, jnp.zeros((320, 64), F32)], axis=1)
    total_buf[...] = both[64:320]
    turn = jnp.concatenate([both[0:64], jnp.zeros((64, 256), F32)], axis=0).astype(BF16)
    mixed = jnp.sum(weight[:, rows + rows // 2 :, :].astype(F32), axis=0)[0:8]
    mixed = mixed[:, 0:64] + mixed[:, 64:128]

    def forward(j):
        scale = scales[j]
        t = jnp.dot(tokens[j], turn, preferred_element_type=F32) + total_buf[...]
        t = (t * jnp.concatenate([scale, scale], axis=1)).astype(BF16)
        scores = lax.dot_general(t[:, 64:128], t[:, 0:64], LAST, preferred_element_type=F32)
        raised = jnp.exp(scores)
        chosen = (raised * (1.0 / jnp.sum(raised, axis=0, keepdims=True))).astype(BF16)
        col = jnp.sum(chosen.astype(F32), axis=1, keepdims=True)
        mean = jnp.sum(col * t[:, 128:256].astype(F32), axis=0, keepdims=True) / PATCHES
        return t, chosen, col * scale, mean

    def forwards(i):
        found = [forward(8 * i + u) for u in range(8)]
        for u in range(8):
            j = 8 * i + u
            triple[j], attention[j], column[j], mean_att[pl.ds(j, 1), :] = found[u]

    each(0, HEADS // 8, forwards)

    means = mean_att[:, 0:HEAD_DIM]
    logit = own_logit + lax.dot_general(
        means, mixed, LAST, precision=HIGHEST, preferred_element_type=F32
    )
    logit = jnp.where(
        lane < K, jnp.concatenate([logit, jnp.zeros((HEADS, 120), F32)], axis=1), misfits
    )
    small_send[...] = logit

    def small_copy(k, slot):
        to_dp, to_vol = member(flipped(k))
        return copy(
            small_send,
            small_recv.at[slot],
            small_sems.at[0, k],
            small_sems.at[1, slot],
            to_dp,
            to_vol,
        )

    each(1, HEADS, lambda k: small_copy(HEADS - k, head).start())
    small_recv[head] = small_send[...]
    place_lane = lax.broadcasted_iota(jnp.int32, (PATCHES, 128), 1)
    weigh = jnp.zeros((PATCHES, 128), F32)
    for j in range(HEADS):
        weigh = jnp.where(place_lane == j, column[j], weigh)
    weigh = weigh.T[0:HEADS]
    low = weigh.astype(BF16)
    seen = jnp.zeros((HEADS, 128), F32)
    for j in range(HEADS):
        seen = jnp.where(
            row == j, jnp.dot(low, tokens[j], preferred_element_type=F32), seen
        )
    seen = jnp.concatenate([seen[:, 0:64], weigh, jnp.zeros((HEADS, 64), F32)], axis=1)
    weighed = jnp.dot(seen.astype(BF16), basis[...], preferred_element_type=F32)
    each(1, HEADS, lambda k: small_copy(k, flipped(k)).wait_recv())
    summed = jnp.sum(small_recv[...], axis=0)
    misfits = jnp.where(lane < K, pltpu.roll(summed, 124, 1), 0.0)
    raised = jnp.where(lane < K, jnp.exp(summed), 0.0)
    chances = raised / jnp.sum(raised, axis=1, keepdims=True)
    expected = jnp.sum(chances * misfits, axis=1, keepdims=True)
    slope = chances * (misfits - expected)
    pulled = jnp.zeros((HEADS, HEAD_DIM), F32)
    for k in range(K):
        pulled = pulled + slope[:, k : k + 1] * mixed[k : k + 1, :]
    pulled_buf[...] = jnp.concatenate(
        [pulled / PATCHES, jnp.zeros((HEADS, 128 - HEAD_DIM), F32)], axis=1
    )

    slope_t = slope.T[0:8]
    outer = jnp.zeros((HEADS, 128), F32)
    value_t = jnp.zeros((HEADS, width), F32)
    for j in range(HEADS):
        outer = outer + slope_t[:, j : j + 1] * mean_att[j : j + 1, :]
        value_t = value_t + slope_t[:, j : j + 1] * weighed[j : j + 1, :]
    own = jnp.sum(jnp.where(lane[:, 0:HEADS] == head, slope_t, 0.0), axis=1, keepdims=True)
    side_send[0:8, 0:width] = own * own_row
    side_send[0:8, width:] = outer
    side_send[8:16, 0:width] = value_t
    side_send[8:16, width:] = jnp.zeros((8, 128), F32)
    side = copy(side_send, side_recv, core_sems.at[0], core_sems.at[1], other, vol)
    side.start()

    wide = lax.broadcasted_iota(jnp.int32, (PATCHES, 128), 1)

    def backward(j):
        t = triple[j]
        chosen = attention[j]
        wider = chosen.astype(F32)
        up = jnp.sum(
            t[:, 128:256].astype(F32) * pulled_buf[pl.ds(j, 1), :], axis=1, keepdims=True
        )
        center = jnp.sum(wider * up, axis=0, keepdims=True)
        inner = (wider * (up - center)).astype(BF16)
        sides = t[:, 0:128]
        key_slope = jnp.dot(inner, sides, preferred_element_type=F32)
        query_slope = lax.dot_general(inner, sides, FIRST, preferred_element_type=F32)
        scale = scales[j]
        return jnp.where(wide < 64, key_slope, query_slope * HEAD_DIM ** (-0.5)) * scale

    total_buf[...] = jnp.zeros((PATCHES, 256), F32)

    def backwards(i):
        found = [backward(4 * i + u) for u in range(4)]
        total = total_buf[:, 0:128]
        for u in range(4):
            at = pl.multiple_of((4 * i + u) * PATCHES, PATCHES)
            terms_buf[pl.ds(at, PATCHES), :] = found[u].astype(BF16)
            total = total + found[u]
        total_buf[:, 0:128] = total

    each(0, HEADS // 8, backwards)
    side.wait_recv()
    sides = side_send[...] + side_recv[...]
    pooled_t = sides[0:8, 0:width]
    value_t = sides[8:16, 0:width]
    outer = sides[0:8, width : width + HEAD_DIM]

    fill = [jnp.zeros((HEADS, 64 - rows), F32)] if rows < 64 else []
    for d in range(dps):
        part = slice(d * rows, (d + 1) * rows)
        top = jnp.concatenate([value_t[:, part]] + fill + [outer], axis=1)
        low = jnp.concatenate([mixed, pooled_t[:, part]] + fill, axis=1)
        tile_send[d] = jnp.where(row < 4, top, pltpu.roll(low, 4, 0))

    def tile_copy(k, slot):
        e = (me + k) % count
        d = e // vols * 2 + core
        return copy(
            tile_send.at[d],
            tile_recv.at[slot],
            tile_sems.at[0, k],
            tile_sems.at[1, slot],
            d,
            e % vols,
        )

    each(count // 2, count, lambda k: tile_copy(k, me).start())
    each(1, count // 2, lambda k: tile_copy(k, me).start())
    each(HEADS // 8, HEADS // 4, backwards)

    factor_send[0:64, :] = jnp.dot(
        tokens_t[...], terms_buf[...], preferred_element_type=F32
    ).astype(BF16)
    factor_send[64:320, :] = total_buf[:, 0:128].astype(BF16)
    factors = copy(factor_send, factor_recv, core_sems.at[2], core_sems.at[3], other, vol)
    factors.start()
    factors.wait_recv()
    factor_sum[0:320, :] = (
        factor_send[...].astype(F32) + factor_recv[...].astype(F32)
    ).astype(BF16)
    factor_sum[320:384, :] = jnp.zeros((64, 128), BF16)
    def grad_copy(k, slot):
        e = (me + k) % count
        d = e // vols * 2 + core
        return copy(
            grad_send.at[e // vols],
            grad_recv.at[slot],
            grad_sems.at[0, k],
            grad_sems.at[1, slot],
            d,
            e % vols,
        )

    found = [
        basis_t[pl.ds(pl.multiple_of((2 * i + core) * rows, rows), rows), :] for i in range(chips)
    ]
    grad_send[...] = (
        jnp.dot(jnp.concatenate(found, axis=0), factor_sum[...], preferred_element_type=F32)
        .astype(BF16)
        .reshape(chips, rows, 128)
    )
    each(count // 2, count, lambda k: grad_copy(k, me).start())
    each(1, count // 2, lambda k: grad_copy(k, me).start())
    grad_recv[me] = grad_send[chip]
    each(1, 5, lambda k: patch_copy(k, head).wait_send())
    each(1, 4, lambda k: patch_relay(k).wait_send())
    each(1, chips, lambda k: weight_copy(k, dp).wait_send())
    each(0, chips, lambda at: weight_relay(at).wait_send())
    each(1, vols, lambda k: line_copy(k, vol).wait_send())
    each(1, HEADS, lambda k: small_copy(k, head).wait_send())
    side.wait_send()
    factors.wait_send()
    each(1, count, lambda k: tile_copy(k, me).wait_send())
    tile_recv[me] = tile_send[dp]

    each(1, count, lambda k: tile_copy(k, (me + count - k) % count).wait_recv())

    outers = []
    for h in range(HEADS):
        senders = senders_of(dps, vols, h)
        tile = tile_recv[senders[0]]
        for s in senders[1:]:
            tile = tile + tile_recv[s]
        outers.append(tile[:, 64:128])
    pooled_sum = pltpu.roll(jnp.sum(tile_recv[...], axis=0), 4, 0)
    branch = lax.dot_general(
        jnp.concatenate(outers, axis=1),
        project_out[...].astype(F32),
        LAST,
        precision=HIGHEST,
        preferred_element_type=F32,
    )
    fill = [jnp.zeros((HEADS, 64 - rows), F32)] if rows < 64 else []
    pooled_sum = pooled_sum + jnp.concatenate(
        [jnp.zeros((HEADS, 64), F32), branch] + fill, axis=1
    )
    head_send[...] = pooled_sum

    def head_copy(k, slot):
        to = (chip + k) % chips
        return copy(
            head_send,
            head_out.at[core, slot],
            head_sems.at[0, k],
            head_sems.at[1, slot],
            to * 2 + core,
            vol,
        )

    each(1, chips, lambda k: head_copy(k, chip).start())
    head_out[core, chip] = pooled_sum

    for h in range(HEADS):
        senders = senders_of(dps, vols, h)
        tile = tile_recv[senders[0]]
        mixed_h = jnp.where(row < 4, pltpu.roll(tile, 4, 0), 0.0)[:, 0:64]
        for s in senders[1:]:
            tile = tile + tile_recv[s]
        tile = jnp.where(row < 4, tile, 0.0)
        value_out[:, h * 64 : h * 64 + 64] = (
            lax.dot_general(
                tile[:, 0:rows], mixed_h, FIRST, precision=HIGHEST, preferred_element_type=F32
            )
            / PATCHES
        )
        value_out[:, 512 + h * 64 : 576 + h * 64] = jnp.dot(
            head_own, tile[:, 64:128], precision=HIGHEST, preferred_element_type=F32
        )

    each(1, chips, lambda k: head_copy(k, (chip + chips - k) % chips).wait_recv())
    heads = copy(
        head_out.at[core], head_out.at[core], core_sems.at[4], core_sems.at[5], other, vol
    )
    heads.start()

    each(1, count, lambda k: grad_copy(k, me).wait_send())
    each(1, chips, lambda k: head_copy(k, chip).wait_send())
    heads.wait_send()
    each(1, count, lambda k: grad_copy(k, (me + count - k) % count).wait_recv())
    copy(
        head_out.at[1 - core], head_out.at[1 - core], core_sems.at[4], core_sems.at[5], other, vol
    ).wait_recv()


def senders_of(dps, vols, h):
    return [
        (z * 4 + h // 2) * vols + v * 2 + h % 2 for z in range(dps // 8) for v in range(vols // 2)
    ]


def finish(dps, vols, errors, grads, values, heads, errors_out, in_out, out_out, head_out):
    rows = values.shape[0]
    for h in range(HEADS):
        senders = senders_of(dps, vols, h)
        both = grads[senders[0]].astype(F32)
        for s in senders[1:]:
            both = both + grads[s].astype(F32)
        in_out[:, h * 64 : h * 64 + 64] = both[:, 64:128]
        in_out[:, 512 + h * 64 : 576 + h * 64] = both[:, 0:64]
    in_out[:, 1024:1536] = values[:, 0:512]
    out_out[...] = values[:, 512:1024]
    errors_out[...] = errors[0:1, 0:K]
    for d in range(dps):
        head_out[:, d * rows : (d + 1) * rows] = heads[d % 2, d // 2][0:K, 64 : 64 + rows]


def constants():
    freq = np.arange(PIX) - PIX // 2
    phase = (freq[:, None] * np.arange(PIX)[None, :] % PIX) * (2.0 * math.pi / PIX)
    cosine, sine = np.cos(phase), np.sin(phase)
    waves = np.stack([cosine, sine, (cosine + sine).T, (cosine - sine).T]).astype(np.float32)
    sel = np.zeros((2 * PIX, PIX), np.float32)
    sel[2 * np.arange(PIX), np.arange(PIX)] = 1.0
    places = np.zeros((PATCH, PIX, PIX), np.float32)
    for r in range(PATCH):
        places[r, np.arange(PIX), r * PATCH + np.arange(PIX) % PATCH] = 1.0
    return waves, sel, places


def local(
    dps,
    vols,
    images,
    contrast,
    volume,
    line_index,
    patch_weight,
    position,
    norm_gain,
    project_in,
    project_out,
    head_weight,
):
    width = norm_gain.shape[0]
    rows = project_in.shape[0]
    chips = dps // 2
    count = chips * vols
    waves, sel, places = constants()
    slab, side, _ = volume.shape
    vmem = pl.BlockSpec(memory_space=pltpu.VMEM)
    hbm = pl.BlockSpec(memory_space=pltpu.HBM)
    inputs = (
        images,
        contrast,
        patch_weight,
        position,
        norm_gain.reshape(1, width),
        project_in,
        project_out,
        head_weight.T,
        jnp.asarray(waves),
        jnp.asarray(sel, BF16),
        jnp.asarray(places, BF16),
    )
    errors, grads, values, heads = pl.pallas_call(
        functools.partial(step, dps, vols),
        out_shape=(
            jax.ShapeDtypeStruct((8, 128), F32),
            jax.ShapeDtypeStruct((count, rows, 128), BF16),
            jax.ShapeDtypeStruct((rows, 1024), F32),
            jax.ShapeDtypeStruct((2, chips, 8, 128), F32),
        ),
        in_specs=[hbm] * (2 + len(inputs)),
        out_specs=(vmem,) * 4,
        scratch_shapes=[
            pltpu.SMEM(line_index.shape, jnp.int32),
            pltpu.VMEM(line_index.shape, jnp.int32),
        ]
        + [pltpu.VMEM(one.shape, one.dtype) for one in inputs]
        + [
            pltpu.VMEM((slab * (side // 16), 16, side), BF16),
            pltpu.VMEM((vols + 1, K * PIX, PIX), BF16),
            pltpu.VMEM((PATCHES // 2, 128), BF16),
            pltpu.VMEM((4, rows + rows // 2 + 16, 128), BF16),
            pltpu.VMEM((128, 8), F32),
            pltpu.VMEM((vols, K * PIX, PIX), BF16),
            pltpu.VMEM((HEADS, PATCHES // 2, 128), BF16),
            pltpu.VMEM((dps, rows + rows // 2 + 16, 128), BF16),
            pltpu.VMEM((384, width), BF16),
            pltpu.VMEM((width, 384), BF16),
            pltpu.VMEM((320, 64), F32),
            pltpu.VMEM((PATCHES, 1), F32),
            pltpu.VMEM((HEADS, PATCHES, 128), BF16),
            pltpu.VMEM((64, HEADS * PATCHES), BF16),
            pltpu.VMEM((HEADS, PATCHES, 128), F32),
            pltpu.VMEM((HEADS, PATCHES, PATCHES), BF16),
            pltpu.VMEM((HEADS, PATCHES, 256), BF16),
            pltpu.VMEM((HEADS, PATCHES, 128), F32),
            pltpu.VMEM((HEADS, 128), F32),
            pltpu.VMEM((HEADS, 128), F32),
            pltpu.VMEM((HEADS, HEADS, 128), F32),
            pltpu.VMEM((HEADS, 128), F32),
            pltpu.VMEM((HEADS * PATCHES, 128), BF16),
            pltpu.VMEM((PATCHES, 256), F32),
            pltpu.VMEM((320, 128), BF16),
            pltpu.VMEM((320, 128), BF16),
            pltpu.VMEM((384, 128), BF16),
            pltpu.VMEM((16, width + 128), F32),
            pltpu.VMEM((16, width + 128), F32),
            pltpu.VMEM((chips, rows, 128), BF16),
            pltpu.VMEM((dps, 8, 128), F32),
            pltpu.VMEM((count, 8, 128), F32),
            pltpu.VMEM((8, 128), F32),
            pltpu.SemaphoreType.DMA((14,)),
            pltpu.SemaphoreType.DMA((2, vols)),
            pltpu.SemaphoreType.DMA((2, HEADS)),
            pltpu.SemaphoreType.DMA((2, dps)),
            pltpu.SemaphoreType.DMA((chips,)),
            pltpu.SemaphoreType.DMA((2, HEADS)),
            pltpu.SemaphoreType.DMA((6,)),
            pltpu.SemaphoreType.DMA((2, count)),
            pltpu.SemaphoreType.DMA((2, count)),
            pltpu.SemaphoreType.DMA((2, chips)),
        ],
        compiler_params=pltpu.CompilerParams(
            collective_id=0, has_side_effects=True, vmem_limit_bytes=56 * 1024 * 1024
        ),
        name="pose_step",
    )(line_index, volume.reshape(slab * (side // 16), 16, side), *inputs)
    errors, in_grad, out_grad, head_grad = pl.pallas_call(
        functools.partial(finish, dps, vols),
        out_shape=(
            jax.ShapeDtypeStruct((1, K), F32),
            jax.ShapeDtypeStruct((rows, 3 * HEADS * HEAD_DIM), F32),
            jax.ShapeDtypeStruct((rows, HEADS * HEAD_DIM), F32),
            jax.ShapeDtypeStruct((K, width), F32),
        ),
        in_specs=[vmem] * 4,
        out_specs=(vmem,) * 4,
        name="finish",
    )(errors, grads, values, heads)
    return errors, in_grad, out_grad, head_grad.T


def solution(mesh):
    placed = (
        P(("dp", "vol"), None, None),
        P(("dp", "vol"), None, None),
        P("vol", None, None),
        P("dp", None, None),
        P(),
        P(),
        P(),
        P("dp", None),
        P("dp", None),
        P(),
    )
    return jax.shard_map(
        functools.partial(local, mesh.shape["dp"], mesh.shape["vol"]),
        mesh=mesh,
        in_specs=placed,
        out_specs=(P(("dp", "vol"), None), P("dp", None), P("dp", None), P()),
        check_vma=False,
    )
```
